256 devices in a mesh: pipe: 8 (over x_hi, y), dp: 32 (over z, x_lo, core).
Axes of the slice: x: 4 (x_hi: 2, x_lo: 2; x = x_hi * 2 + x_lo), y: 4, z: 8, core: 2. Of those that a mesh axis runs over, the one named last changes fastest.
Arguments:
- video: bfloat16 [4, 32, 3, 16, 8, 128], P(None, 'dp'), may hold values from -6 to 6
- cotangent: bfloat16 [4, 32, 3, 16, 8, 128], P(None, 'dp'), may hold values from -6 to 6
- weights: bfloat16 [8, 3456, 128], P('pipe'), may hold values from -0.109375 to 0.109375
- gains: float32 [8, 128], P('pipe'), may hold values from 0.1 to 1.9
Outputs:
- segment_out: bfloat16 [8, 4, 32, 3, 16, 8, 128], P('pipe', None, 'dp')
- in_grad: bfloat16 [8, 4, 32, 3, 16, 8, 128], P('pipe', None, 'dp')
- weight_grad: float32 [8, 442368], P('pipe', 'dp')
The draws below stay inside these ranges and needn't reach their ends.
All inputs are finite; a program needn't handle non-finite values.
Results may differ from the reference program's by a relative error of at most 0.025.
Values may be sent and summed in bfloat16 or wider, within the bound.
A program may use at most 64 MiB of HBM per device.

```python
import math
import jax
import jax.numpy as jnp
from jax import lax

C = 128
GROUPS = 32
MB = 4
FRAMES = 3
ROWS = 16
COLS = 8
SEGMENTS = 8
CLIPS = 32


def level_of(own_key, dims, shards, least, high):
    factor_of = 1.0
    for axis_at, parts in shards:
        steps = jax.random.uniform(jax.random.fold_in(jax.random.fold_in(own_key, 6), axis_at), (parts,), jnp.float32, least / len(shards), high / len(shards))
        factor_of = factor_of * jnp.repeat(jnp.exp(steps), dims[axis_at] // parts).reshape((-1,) + (1,) * (len(dims) - 1 - axis_at))
    return factor_of


def scatter_about(own_key, shape, scale, reach, cuts=(), dtype=jnp.bfloat16):
    level = level_of(own_key, shape, cuts, -0.22, 0.18) if cuts else 1.0
    array = jax.random.normal(own_key, shape, jnp.float32) * scale * level
    return jnp.minimum(jnp.maximum(array, -reach), reach).astype(dtype)


def setup_inputs(seed: int = 0) -> dict:
    seeds = jax.random.split(jax.random.key(seed), 5)
    return {
        "video": scatter_about(seeds[0], (MB, CLIPS, FRAMES, ROWS, COLS, C), 1.0, 6.0, ((1, 32),)),
        "cotangent": scatter_about(seeds[1], (MB, CLIPS, FRAMES, ROWS, COLS, C), 1.0, 6.0, ((1, 32),)),
        "weights": scatter_about(seeds[2], (SEGMENTS, 27 * C, C), (27 * C) ** -0.5, 0.109375, ((0, 8),)),
        "gains": jnp.clip(1.0 + 0.18 * jax.random.normal(seeds[3], (SEGMENTS, C), jnp.float32), 0.1, 1.9),
    }


def norm_act(values, gain):
    batch, frames, rows, cols, chans = values.shape
    grouped = values.reshape(batch, frames, rows, cols, GROUPS, chans // GROUPS)
    mean = lax.optimization_barrier(jnp.mean(grouped, axis=(1, 2, 3, 5), keepdims=True))
    centred = grouped - mean
    var = lax.optimization_barrier(jnp.mean(centred * centred, axis=(1, 2, 3, 5), keepdims=True))
    normed = (centred * lax.rsqrt(var + 1e-06)).reshape(values.shape) * gain
    return jax.nn.silu(normed)

def patches(act):
    frames, rows, cols = (act.shape[1], act.shape[2], act.shape[3])
    leading = act[:, :1]
    padded = jnp.concatenate([leading, leading, act], axis=1)
    padded = jnp.pad(padded, ((0, 0), (0, 0), (1, 1), (1, 1), (0, 0)))
    pieces = [padded[:, frame_off:frame_off + frames, row_off:row_off + rows, col_off:col_off + cols, :] for frame_off in range(3) for row_off in range(3) for col_off in range(3)]
    return jnp.concatenate(pieces, axis=-1).reshape(-1, 27 * act.shape[-1])

def forward(inputs, weight, gain):
    values = inputs.astype(jnp.float32)
    act = norm_act(values, gain).astype(jnp.bfloat16)
    cols_mat = patches(act)
    branch = jnp.dot(cols_mat, weight, preferred_element_type=jnp.float32).reshape(inputs.shape)
    return ((values + branch).astype(jnp.bfloat16), cols_mat)

def backward(inputs, grad, weight, gain, cols_mat):
    values = inputs.astype(jnp.float32)
    flat_grad = grad.reshape(-1, grad.shape[-1])
    term = lax.dot_general(cols_mat, flat_grad, (((0,), (0,)), ((), ())), preferred_element_type=jnp.float32)
    grad_cols = lax.dot_general(flat_grad, weight, (((1,), (1,)), ((), ())), preferred_element_type=jnp.float32)
    _, pull_cols = jax.vjp(patches, jnp.zeros(inputs.shape, jnp.float32))
    grad_act = pull_cols(grad_cols)[0]
    _, pull_norm = jax.vjp(lambda field: norm_act(field, gain), values)
    grad_in = grad.astype(jnp.float32) + pull_norm(grad_act)[0]
    return (grad_in.astype(jnp.bfloat16), term)

def reference(video, cotangent, weights, gains):
    inputs_all = []
    outputs_all = []
    current = video
    for segment in range(SEGMENTS):
        inputs_all.append(current)
        current = jnp.stack([forward(current[micro], weights[segment], gains[segment])[0] for micro in range(MB)])
        outputs_all.append(current)
    grad = cotangent
    in_grads = [None] * SEGMENTS
    weight_grads = [None] * SEGMENTS
    scale = 1.0 / math.sqrt(MB * CLIPS * FRAMES * ROWS * COLS)
    for segment in reversed(range(SEGMENTS)):
        total = jnp.zeros((27 * C, C), jnp.float32)
        pieces = []
        for micro in range(MB):
            unit_in = inputs_all[segment][micro]
            cols_mat = forward(unit_in, weights[segment], gains[segment])[1]
            grad_in, term = backward(unit_in, grad[micro], weights[segment], gains[segment], cols_mat)
            total = total + term
            pieces.append(grad_in)
        grad = jnp.stack(pieces)
        in_grads[segment] = grad
        weight_grads[segment] = (total * scale).reshape(-1)
    return (jnp.stack(outputs_all), jnp.stack(in_grads), jnp.stack(weight_grads))
```

```python
import functools
import math

import jax
import jax.numpy as jnp
from jax import lax
from jax.experimental import pallas as pl
from jax.experimental.pallas import tpu as pltpu
from jax.sharding import PartitionSpec as P

GROUPS = 32
UNITS = 4
FRAMES, ROWS, COLS, C = 3, 16, 8, 128
PLANE = ROWS * COLS
PIX = FRAMES * PLANE
TAPS = 9
SLAB = TAPS * C
WROWS = 3 * SLAB
QUARTER = WROWS // 4
MESH = pl.DeviceIdType.MESH
F32, BF16 = jnp.float32, jnp.bfloat16


def group_sum(part):
    lane = lax.broadcasted_iota(jnp.int32, part.shape, 1)
    pair = part + jnp.where(lane % 2 == 0, pltpu.roll(part, C - 1, 1), pltpu.roll(part, 1, 1))
    quad = pair + jnp.where(lane % 4 < 2, pltpu.roll(pair, C - 2, 1), pltpu.roll(pair, 2, 1))
    return jnp.sum(quad, axis=0, keepdims=True)


def fill_shifts(field, dest, flip):
    col = lax.broadcasted_iota(jnp.int32, field.shape, 1)
    for col_off in range(3):
        step = (1 - col_off) if flip else (col_off - 1)
        if step == 0:
            moved = field
        elif step == 1:
            moved = jnp.where(col < COLS - 1, pltpu.roll(field, COLS - 1, 1), 0.0)
        else:
            moved = jnp.where(col > 0, pltpu.roll(field, 1, 1), 0.0)
        planes = moved.reshape(FRAMES, ROWS, COLS, C)
        blank = jnp.zeros((FRAMES, 1, COLS, C), F32)
        for row_off in range(3):
            step = (1 - row_off) if flip else (row_off - 1)
            if step == 0:
                rows = planes
            elif step == 1:
                rows = jnp.concatenate([planes[:, 1:], blank], axis=1)
            else:
                rows = jnp.concatenate([blank, planes[:, : ROWS - 1]], axis=1)
            at = (row_off * 3 + col_off) * C
            dest[:, at : at + C] = rows.reshape(PIX, C).astype(BF16)


def dot(lhs, rhs):
    return jnp.dot(lhs, rhs, preferred_element_type=F32)


def kernel(
    depth,
    scale,
    video,
    cot,
    w,
    gains,
    seg_out,
    grad_out,
    wg_out,
    wb,
    gbuf,
    xs,
    gs,
    acts,
    xhat_s,
    slope_s,
    rstd_s,
    shifts,
    actb,
    grdb,
    total,
    buf1,
    got1,
    buf2,
    got2,
    buf3,
    got3,
    load_sem,
    w_send,
    w_recv,
    gain_send,
    gain_recv,
    hop_send,
    hop_recv,
    out_send,
    seg_recv,
    act_recv,
    grd_recv,
    ing_recv,
    rs_send,
    rs_recv,
    z_send,
    z_recv,
):
    pipe = lax.axis_index("pipe")
    dp = lax.axis_index("dp")
    half = lax.div(pipe, UNITS)
    y = lax.rem(pipe, UNITS)
    core = lax.rem(dp, 2)
    x_lo = lax.rem(lax.div(dp, 2), 2)
    z = lax.div(dp, 4)
    base = half * UNITS
    yr = lax.rem(y + 1, UNITS)
    yo = lax.rem(y + 2, UNITS)
    yl = lax.rem(y + 3, UNITS)
    other_core = dp + 1 - 2 * core
    other_x = dp + 2 - 4 * x_lo
    other_half = pipe + UNITS - 2 * base

    def dev(pipe_at, dp_at):
        return (pipe_at, dp_at)

    def z_peer(step):
        return lax.rem(z + step, depth) * 4 + lax.rem(dp, 4)

    def remote(src, dst, send, recv, target):
        return pltpu.make_async_remote_copy(
            src_ref=src, dst_ref=dst, send_sem=send, recv_sem=recv, device_id=target, device_id_type=MESH
        )

    load_w = pltpu.make_async_copy(w, wb.at[y], load_sem.at[0])
    load_w.start()
    load_gain = pltpu.make_async_copy(gains, gbuf.at[y], load_sem.at[1])
    load_gain.start()

    @pl.when(half == 0)
    def _():
        pltpu.make_async_copy(video.at[y], xs.at[0], load_sem.at[2]).start()

    @pl.when(half == 1)
    def _():
        pltpu.make_async_copy(cot.at[y], gs.at[UNITS], load_sem.at[2]).start()

    barrier = pltpu.get_barrier_semaphore()
    peers = [dev(base + at, dp) for at in (yr, yo, yl)]
    peers += [dev(other_half, dp), dev(pipe, other_core), dev(pipe, other_x)]
    peers += [dev(pipe, z_peer(step)) for step in range(1, depth)]
    for peer in peers:
        pl.semaphore_signal(barrier, inc=1, device_id=peer, device_id_type=MESH)
    pl.semaphore_wait(barrier, len(peers))

    def gain_copy(at, slot):
        return remote(gains, gbuf.at[y], gain_send.at[slot], gain_recv.at[y], dev(base + at, dp))

    for slot, at in enumerate((yr, yo, yl)):
        gain_copy(at, slot).start()

    qa = core * 2
    qb = core * 2 + 1
    right, left, twin = dev(base + yr, dp), dev(base + yl, dp), dev(pipe, other_core)

    def rows_of(quarter):
        return pl.ds(pl.multiple_of(quarter * QUARTER, QUARTER), QUARTER)

    def own(quarter, slot, target):
        return remote(
            w.at[rows_of(quarter)],
            wb.at[y, rows_of(quarter)],
            w_send.at[slot],
            w_recv.at[y, quarter],
            target,
        )

    def relay(slab, quarter, slot, target):
        piece = wb.at[slab, rows_of(quarter)]
        return remote(piece, piece, w_send.at[slot], w_recv.at[slab, quarter], target)

    first = [own(qa, 0, right), own(qb, 1, left), own(qb, 2, right), own(qa, 3, left)]
    for copy in first:
        copy.start()
    relays = [
        (yl, qa, ((4, right), (6, twin))),
        (yr, qb, ((5, left), (7, twin))),
        (yl, qb, ((8, twin),)),
        (yr, qa, ((9, twin),)),
        (yo, qa, ((10, twin),)),
        (yo, qb, ((11, twin),)),
    ]
    sent = list(first)
    for slab, quarter, targets in relays:
        relay(slab, quarter, 0, right).wait_recv()
        for slot, target in targets:
            copy = relay(slab, quarter, slot, target)
            copy.start()
            sent.append(copy)
    qc = (1 - core) * 2
    for slab in (yl, yr, yo):
        for quarter in (qc, qc + 1):
            relay(slab, quarter, 0, twin).wait_recv()
    load_w.wait()
    load_gain.wait()
    for slot, at in enumerate((yr, yo, yl)):
        remote(gains, gbuf.at[at], gain_send.at[slot], gain_recv.at[at], dev(base + at, dp)).wait_recv()

    def to_home(src, dst, slot, recv, unit):
        away = remote(src, dst.at[y], out_send.at[slot, unit], recv.at[y], dev(base + unit, dp))
        here = pltpu.make_async_copy(src, dst.at[y], out_send.at[slot, unit])
        return away, here

    def start_home(*args):
        away, here = to_home(*args)
        unit = args[-1]

        @pl.when(unit != y)
        def _():
            away.start()

        @pl.when(unit == y)
        def _():
            here.start()

    def finish_home(*args):
        away, here = to_home(*args)
        unit = args[-1]

        @pl.when(unit != y)
        def _():
            away.wait_send()

        @pl.when(unit == y)
        def _():
            here.wait()

    def arrived(dst, recv):
        for at in (yr, yo, yl):
            remote(dst.at[at], dst.at[at], out_send.at[0, 0], recv.at[at], dev(base + at, dp)).wait_recv()

    hop_x = remote(xs.at[UNITS], xs.at[0], hop_send.at[0], hop_recv.at[0], dev(other_half, dp))
    hop_g = remote(gs.at[0], gs.at[UNITS], hop_send.at[1], hop_recv.at[1], dev(other_half, dp))

    @pl.when(half == 0)
    def _():
        pltpu.make_async_copy(video.at[y], xs.at[0], load_sem.at[2]).wait()

    @pl.when(half == 1)
    def _():
        pltpu.make_async_copy(cot.at[y], gs.at[UNITS], load_sem.at[2]).wait()
        hop_x.wait_recv()

    count = 1.0 / (PIX * (C // GROUPS))

    def forward(unit, _):
        gain = gbuf[unit].reshape(1, 1, C)
        x = xs[unit].astype(F32).reshape(PIX // COLS, COLS, C)
        mean = group_sum(jnp.sum(x, axis=0)) * count
        centred = x - mean.reshape(1, 1, C)
        var = group_sum(jnp.sum(centred * centred, axis=0)) * count
        rstd = lax.rsqrt(var + 1e-06)
        xhat = centred * rstd.reshape(1, 1, C)
        normed = xhat * gain
        sig = jax.nn.sigmoid(normed)
        act = normed * sig
        acts[unit] = act.reshape(PIX, C).astype(BF16)
        fill_shifts(act, shifts, False)
        xhat_s[unit] = xhat
        slope_s[unit] = (sig + act * (1.0 - sig)) * gain
        rstd_s[unit] = rstd
        part0 = dot(shifts[:PLANE], wb[unit, :SLAB])
        part1 = dot(shifts[: 2 * PLANE], wb[unit, SLAB : 2 * SLAB])
        part2 = dot(shifts[...], wb[unit, 2 * SLAB :])
        x = x.reshape(PIX, C)
        early = part0 + part1[:PLANE]
        branch = (early, early, part0 + part1[PLANE:])
        for frame in range(FRAMES):
            at = slice(frame * PLANE, (frame + 1) * PLANE)
            xs[unit + 1, at] = (x[at] + branch[frame] + part2[at]).astype(BF16)
        start_home(xs.at[unit + 1], seg_out, 0, seg_recv, unit)
        start_home(acts.at[unit], actb, 1, act_recv, unit)
        return 0

    lax.fori_loop(0, UNITS, forward, 0)

    @pl.when(half == 0)
    def _():
        hop_x.start()
        hop_g.wait_recv()

    def backward(step, _):
        unit = UNITS - 1 - step
        start_home(gs.at[unit + 1], grdb, 2, grd_recv, unit)
        grad = gs[unit + 1].astype(F32)
        fill_shifts(grad.reshape(PIX // COLS, COLS, C), shifts, True)
        parts = []
        for frame_off in range(3):
            taps = [
                wb[unit, frame_off * SLAB + tap * C : frame_off * SLAB + (tap + 1) * C]
                for tap in range(TAPS)
            ]
            parts.append(
                lax.dot_general(
                    shifts[...],
                    jnp.concatenate(taps, axis=1),
                    (((1,), (1,)), ((), ())),
                    preferred_element_type=F32,
                )
            )
        p0, p1, p2 = ([part[f * PLANE : (f + 1) * PLANE] for f in range(3)] for part in parts)
        gact = jnp.concatenate(
            [p0[0] + p0[1] + p0[2] + p1[0] + p1[1] + p2[0], p1[2] + p2[1], p2[2]], axis=0
        )
        xhat = xhat_s[unit]
        inner = gact.reshape(PIX // COLS, COLS, C) * slope_s[unit]
        mean_a = group_sum(jnp.sum(inner, axis=0)) * count
        mean_b = group_sum(jnp.sum(inner * xhat, axis=0)) * count
        slant = (inner - mean_a.reshape(1, 1, C) - xhat * mean_b.reshape(1, 1, C)) * rstd_s[unit].reshape(
            1, 1, C
        )
        gs[unit] = (grad + slant.reshape(PIX, C)).astype(BF16)
        start_home(gs.at[unit], grad_out, 3, ing_recv, unit)
        return 0

    lax.fori_loop(0, UNITS, backward, 0)

    @pl.when(half == 1)
    def _():
        hop_g.start()

    for slot in (1, 2):
        src, dst, recv = ((acts.at[y], actb, act_recv), (gs.at[y + 1], grdb, grd_recv))[slot - 1]
        finish_home(src, dst, slot, recv, y)
    arrived(actb, act_recv)
    arrived(grdb, grd_recv)

    def wgrad(clip, _):
        act = actb[clip].astype(F32)
        turned = [act[f * PLANE : (f + 1) * PLANE].T.astype(BF16) for f in range(FRAMES)]
        lhs = jnp.concatenate(
            [
                jnp.concatenate([turned[max(f - 2 + frame_off, 0)] for f in range(FRAMES)], axis=1)
                for frame_off in range(3)
            ],
            axis=0,
        )
        fill_shifts(grdb[clip].astype(F32).reshape(PIX // COLS, COLS, C), shifts, True)
        for tap in range(TAPS):
            block = dot(lhs, shifts[:, tap * C : (tap + 1) * C])
            for frame_off in range(3):
                at = (frame_off * TAPS + tap) * C
                part = block[frame_off * C : (frame_off + 1) * C]
                total[at : at + C] = total[at : at + C] + part
        return 0

    total[...] = jnp.zeros_like(total)
    lax.fori_loop(0, UNITS, wgrad, 0)

    chunk = WROWS // (4 * depth)
    for at_z in range(depth):
        for at_x in range(2):
            for at_core in range(2):
                start = (at_z * 4 + at_x * 2 + at_core) * chunk
                buf1[at_core, at_x, at_z] = total[start : start + chunk].astype(BF16)
    copy = remote(buf1.at[1 - core], got1, rs_send.at[0], rs_recv.at[0], dev(pipe, other_core))
    copy.start()
    copy.wait()
    buf2[...] = (buf1[core].astype(F32) + got1[...].astype(F32)).astype(BF16)
    copy = remote(buf2.at[1 - x_lo], got2, rs_send.at[1], rs_recv.at[1], dev(pipe, other_x))
    copy.start()
    copy.wait()
    buf3[...] = (buf2[x_lo].astype(F32) + got2[...].astype(F32)).astype(BF16)

    def z_copy(step):
        target = lax.rem(z + step, depth)
        return remote(
            buf3.at[target], got3.at[step - 1], z_send.at[step - 1], z_recv.at[step - 1], dev(pipe, z_peer(step))
        )

    for step in range(1, depth):
        z_copy(step).start()
    result = buf3[z].astype(F32)
    for step in range(1, depth):
        z_copy(step).wait_recv()
        result = result + got3[step - 1].astype(F32)
    wg_out[...] = result * scale

    for step in range(1, depth):
        z_copy(step).wait_send()
    for copy in sent:
        copy.wait_send()
    for slot, at in enumerate((yr, yo, yl)):
        gain_copy(at, slot).wait_send()
    for unit in range(UNITS):
        finish_home(xs.at[unit + 1], seg_out, 0, seg_recv, unit)
        finish_home(gs.at[unit], grad_out, 3, ing_recv, unit)

        @pl.when(unit != y)
        def _():
            to_home(acts.at[unit], actb, 1, act_recv, unit)[0].wait_send()
            to_home(gs.at[unit + 1], grdb, 2, grd_recv, unit)[0].wait_send()

    @pl.when(half == 0)
    def _():
        hop_x.wait_send()

    @pl.when(half == 1)
    def _():
        hop_g.wait_send()

    arrived(seg_out, seg_recv)
    arrived(grad_out, ing_recv)


def body(video, cotangent, weights, gains):
    micro = video.shape[0]
    devices = lax.axis_size("dp")
    depth = devices // 4
    chunk = WROWS // devices
    scale = 1.0 / math.sqrt(micro * devices * PIX)
    clip = (PIX, C)
    any_spec = pl.BlockSpec(memory_space=pl.ANY)
    dma = pltpu.SemaphoreType.DMA
    outputs, grads_out, share = pl.pallas_call(
        functools.partial(kernel, depth, scale),
        out_shape=(
            jax.ShapeDtypeStruct((micro, *clip), BF16),
            jax.ShapeDtypeStruct((micro, *clip), BF16),
            jax.ShapeDtypeStruct((chunk, C), F32),
        ),
        in_specs=[any_spec] * 4,
        out_specs=(any_spec, any_spec, pl.BlockSpec(memory_space=pltpu.VMEM)),
        scratch_shapes=[
            pltpu.VMEM((UNITS, WROWS, C), BF16),
            pltpu.VMEM((UNITS, 1, C), F32),
            pltpu.VMEM((UNITS + 1, *clip), BF16),
            pltpu.VMEM((UNITS + 1, *clip), BF16),
            pltpu.VMEM((UNITS, *clip), BF16),
            pltpu.VMEM((UNITS, PIX // COLS, COLS, C), F32),
            pltpu.VMEM((UNITS, PIX // COLS, COLS, C), F32),
            pltpu.VMEM((UNITS, 1, C), F32),
            pltpu.VMEM((PIX, SLAB), BF16),
            pltpu.VMEM((UNITS, *clip), BF16),
            pltpu.VMEM((UNITS, *clip), BF16),
            pltpu.VMEM((WROWS, C), F32),
            pltpu.VMEM((2, 2, depth, chunk, C), BF16),
            pltpu.VMEM((2, depth, chunk, C), BF16),
            pltpu.VMEM((2, depth, chunk, C), BF16),
            pltpu.VMEM((depth, chunk, C), BF16),
            pltpu.VMEM((depth, chunk, C), BF16),
            pltpu.VMEM((max(depth - 1, 1), chunk, C), BF16),
            dma((3,)),
            dma((12,)),
            dma((UNITS, 4)),
            dma((3,)),
            dma((UNITS,)),
            dma((2,)),
            dma((2,)),
            dma((4, UNITS)),
            dma((UNITS,)),
            dma((UNITS,)),
            dma((UNITS,)),
            dma((UNITS,)),
            dma((2,)),
            dma((2,)),
            dma((max(depth - 1, 1),)),
            dma((max(depth - 1, 1),)),
        ],
        compiler_params=pltpu.CompilerParams(collective_id=0, has_side_effects=True),
    )(
        video.reshape(micro, *clip),
        cotangent.reshape(micro, *clip),
        weights.reshape(WROWS, C),
        gains,
    )
    full = (1, micro, 1, FRAMES, ROWS, COLS, C)
    return (outputs.reshape(full), grads_out.reshape(full), share.reshape(1, -1))


def solution(mesh):
    in_specs = (
        P(None, "dp", None, None, None, None),
        P(None, "dp", None, None, None, None),
        P("pipe", None, None),
        P("pipe", None),
    )
    out_specs = (
        P("pipe", None, "dp", None, None, None, None),
        P("pipe", None, "dp", None, None, None, None),
        P("pipe", "dp"),
    )
    return jax.shard_map(body, mesh=mesh, in_specs=in_specs, out_specs=out_specs, check_vma=False)
```

```python
import functools
import math

import jax
import jax.numpy as jnp
from jax import lax
from jax.experimental import pallas as pl
from jax.experimental.pallas import tpu as pltpu
from jax.sharding import PartitionSpec as P

GROUPS = 32
UNITS = 4
FRAMES, ROWS, COLS, C = 3, 16, 8, 128
PLANE = ROWS * COLS
PIX = FRAMES * PLANE
TAPS = 9
SLAB = TAPS * C
WROWS = 3 * SLAB
EIGHTH = WROWS // 8
MESH = pl.DeviceIdType.MESH
F32, BF16 = jnp.float32, jnp.bfloat16


def group_sum(part):
    lane = lax.broadcasted_iota(jnp.int32, part.shape, 1)
    pair = part + jnp.where(lane % 2 == 0, pltpu.roll(part, C - 1, 1), pltpu.roll(part, 1, 1))
    quad = pair + jnp.where(lane % 4 < 2, pltpu.roll(pair, C - 2, 1), pltpu.roll(pair, 2, 1))
    return jnp.sum(quad, axis=0, keepdims=True)


def fill_shifts(field, dest, flip):
    col = lax.broadcasted_iota(jnp.int32, field.shape, 1)
    for col_off in range(3):
        step = (1 - col_off) if flip else (col_off - 1)
        if step == 0:
            moved = field
        elif step == 1:
            moved = jnp.where(col < COLS - 1, pltpu.roll(field, COLS - 1, 1), 0.0)
        else:
            moved = jnp.where(col > 0, pltpu.roll(field, 1, 1), 0.0)
        planes = moved.reshape(FRAMES, ROWS, COLS, C)
        blank = jnp.zeros((FRAMES, 1, COLS, C), F32)
        for row_off in range(3):
            step = (1 - row_off) if flip else (row_off - 1)
            if step == 0:
                rows = planes
            elif step == 1:
                rows = jnp.concatenate([planes[:, 1:], blank], axis=1)
            else:
                rows = jnp.concatenate([blank, planes[:, : ROWS - 1]], axis=1)
            at = (row_off * 3 + col_off) * C
            dest[:, at : at + C] = rows.reshape(PIX, C).astype(BF16)


def dot(lhs, rhs):
    return jnp.dot(lhs, rhs, preferred_element_type=F32)


def kernel(
    depth,
    scale,
    video,
    cot,
    w,
    gains,
    seg_out,
    grad_out,
    wg_out,
    wb,
    gbuf,
    xs,
    gs,
    acts,
    xhat_s,
    slope_s,
    rstd_s,
    shifts,
    actb,
    grdb,
    total,
    buf1,
    got1,
    buf2,
    got2,
    buf3,
    got3,
    load_sem,
    w_send,
    w_recv,
    gain_send,
    gain_recv,
    hop_send,
    hop_recv,
    out_send,
    seg_recv,
    act_recv,
    grd_recv,
    ing_recv,
    rs_send,
    rs_recv,
    z_send,
    z_recv,
):
    pipe = lax.axis_index("pipe")
    dp = lax.axis_index("dp")
    half = lax.div(pipe, UNITS)
    y = lax.rem(pipe, UNITS)
    core = lax.rem(dp, 2)
    x_lo = lax.rem(lax.div(dp, 2), 2)
    z = lax.div(dp, 4)
    base = half * UNITS
    yr = lax.rem(y + 1, UNITS)
    yo = lax.rem(y + 2, UNITS)
    yl = lax.rem(y + 3, UNITS)
    other_core = dp + 1 - 2 * core
    other_x = dp + 2 - 4 * x_lo
    other_half = pipe + UNITS - 2 * base
    other_z = dp + 4 - 8 * lax.rem(z, 2)
    owner = dp + half * (2 - 4 * x_lo)

    def dev(pipe_at, dp_at):
        return (pipe_at, dp_at)

    def z_peer(step):
        return lax.rem(z + step, depth) * 4 + lax.rem(dp, 4)

    def remote(src, dst, send, recv, target):
        return pltpu.make_async_remote_copy(
            src_ref=src, dst_ref=dst, send_sem=send, recv_sem=recv, device_id=target, device_id_type=MESH
        )

    load_w = pltpu.make_async_copy(w, wb.at[y], load_sem.at[0])
    load_w.start()
    load_gain = pltpu.make_async_copy(gains, gbuf.at[y], load_sem.at[1])
    load_gain.start()

    load_x = pltpu.make_async_copy(video.at[y], xs.at[0], load_sem.at[2])
    cot_copy = remote(cot.at[y], gs.at[UNITS], hop_send.at[2], hop_recv.at[2], dev(pipe, other_x))

    @pl.when(half == 0)
    def _():
        load_x.start()

    barrier = pltpu.get_barrier_semaphore()
    peers = [dev(base + at, dp) for at in (yr, yo, yl)]
    peers += [dev(base + at, other_x) for at in (y, yr, yo, yl)]
    peers += [dev(other_half, other_x), dev(pipe, other_core)]
    peers += [dev(pipe, z_peer(step)) for step in range(1, depth)]
    for peer in peers:
        pl.semaphore_signal(barrier, inc=1, device_id=peer, device_id_type=MESH)
    pl.semaphore_wait(barrier, len(peers))

    def gain_copy(at, slot):
        return remote(gains, gbuf.at[y], gain_send.at[slot], gain_recv.at[y], dev(base + at, dp))

    for slot, at in enumerate((yr, yo, yl)):
        gain_copy(at, slot).start()

    @pl.when(half == 1)
    def _():
        cot_copy.start()

    parity = lax.rem(x_lo + z, 2)
    qa, qb = (parity * 2 + at for at in range(2))
    pa, pb = ((1 - parity) * 2 + at for at in range(2))
    right, left, twin = dev(base + yr, dp), dev(base + yl, dp), dev(pipe, other_core)
    near_x, near_z = dev(pipe, other_x), dev(pipe, other_z)

    def rows_of(quarter, which):
        return pl.ds(pl.multiple_of((quarter * 2 + which) * EIGHTH, EIGHTH), EIGHTH)

    def own(quarter, slot, target):
        return remote(
            w.at[rows_of(quarter, core)],
            wb.at[y, rows_of(quarter, core)],
            w_send.at[slot],
            w_recv.at[y, quarter * 2 + core],
            target,
        )

    def relay(slab, quarter, slot, target, which=core):
        piece = wb.at[slab, rows_of(quarter, which)]
        return remote(piece, piece, w_send.at[slot], w_recv.at[slab, quarter * 2 + which], target)

    sent = [own(qa, 0, right), own(qb, 1, left), own(qb, 2, right), own(qa, 3, left)]
    for copy in sent:
        copy.start()
    relays = [
        (yl, qa, (right, twin, near_x)),
        (yr, qb, (left, twin, near_z)),
        (yl, qb, (twin, near_z)),
        (yr, qa, (twin, near_x)),
        (yl, pa, (twin,)),
        (yr, pb, (twin,)),
        (yo, qa, (twin, near_x)),
        (yo, qb, (twin, near_z)),
        (yr, pa, (twin,)),
        (yl, pb, (twin,)),
        (yo, pa, (twin,)),
        (yo, pb, (twin,)),
    ]
    for slab, quarter, targets in relays:
        relay(slab, quarter, 0, right).wait_recv()
        for target in targets:
            copy = relay(slab, quarter, len(sent), target)
            copy.start()
            sent.append(copy)
    for slab in (yl, yr, yo):
        for quarter in range(4):
            relay(slab, quarter, 0, twin, 1 - core).wait_recv()
    load_w.wait()
    load_gain.wait()
    for slot, at in enumerate((yr, yo, yl)):
        remote(gains, gbuf.at[at], gain_send.at[slot], gain_recv.at[at], dev(base + at, dp)).wait_recv()

    def home(src, dst, slot, recv, unit, holder=dp):
        local = (unit == y) & (holder == dp)

        def away():
            return remote(src, dst.at[y], out_send.at[slot, unit], recv.at[y], dev(base + unit, holder))

        def here():
            return pltpu.make_async_copy(src, dst.at[y], out_send.at[slot, unit])

        return local, away, here

    def start_home(*args):
        local, away, here = home(*args)

        @pl.when(jnp.logical_not(local))
        def _():
            away().start()

        @pl.when(local)
        def _():
            here().start()

    def finish_home(*args):
        local, away, here = home(*args)

        @pl.when(jnp.logical_not(local))
        def _():
            away().wait_send()

        @pl.when(local)
        def _():
            here().wait()

    def arrived(dst, recv, places):
        for at in places:
            remote(dst.at[at], dst.at[at], out_send.at[0, 0], recv.at[at], near_x).wait_recv()

    hop_x = remote(xs.at[UNITS], xs.at[0], hop_send.at[0], hop_recv.at[0], dev(other_half, other_x))
    hop_g = remote(gs.at[0], gs.at[UNITS], hop_send.at[1], hop_recv.at[1], dev(other_half, other_x))

    @pl.when(half == 0)
    def _():
        load_x.wait()

    @pl.when(half == 1)
    def _():
        cot_copy.wait_recv()
        hop_x.wait_recv()

    count = 1.0 / (PIX * (C // GROUPS))

    def forward(unit, _):
        gain = gbuf[unit].reshape(1, 1, C)
        x = xs[unit].astype(F32).reshape(PIX // COLS, COLS, C)
        mean = group_sum(jnp.sum(x, axis=0)) * count
        centred = x - mean.reshape(1, 1, C)
        var = group_sum(jnp.sum(centred * centred, axis=0)) * count
        rstd = lax.rsqrt(var + 1e-06)
        xhat = centred * rstd.reshape(1, 1, C)
        normed = xhat * gain
        sig = jax.nn.sigmoid(normed)
        act = normed * sig
        acts[unit] = act.reshape(PIX, C).astype(BF16)
        fill_shifts(act, shifts, False)
        xhat_s[unit] = xhat
        slope_s[unit] = (sig + act * (1.0 - sig)) * gain
        rstd_s[unit] = rstd
        part0 = dot(shifts[:PLANE], wb[unit, :SLAB])
        part1 = dot(shifts[: 2 * PLANE], wb[unit, SLAB : 2 * SLAB])
        part2 = dot(shifts[...], wb[unit, 2 * SLAB :])
        x = x.reshape(PIX, C)
        early = part0 + part1[:PLANE]
        branch = (early, early, part0 + part1[PLANE:])
        for frame in range(FRAMES):
            at = slice(frame * PLANE, (frame + 1) * PLANE)
            xs[unit + 1, at] = (x[at] + branch[frame] + part2[at]).astype(BF16)
        start_home(xs.at[unit + 1], seg_out, 0, seg_recv, unit, owner)
        start_home(acts.at[unit], actb, 1, act_recv, unit)
        return 0

    lax.fori_loop(0, UNITS, forward, 0)

    @pl.when(half == 0)
    def _():
        hop_x.start()
        hop_g.wait_recv()

    def backward(step, _):
        unit = UNITS - 1 - step
        start_home(gs.at[unit + 1], grdb, 2, grd_recv, unit)
        grad = gs[unit + 1].astype(F32)
        fill_shifts(grad.reshape(PIX // COLS, COLS, C), shifts, True)
        parts = []
        for frame_off in range(3):
            taps = [
                wb[unit, frame_off * SLAB + tap * C : frame_off * SLAB + (tap + 1) * C]
                for tap in range(TAPS)
            ]
            parts.append(
                lax.dot_general(
                    shifts[...],
                    jnp.concatenate(taps, axis=1),
                    (((1,), (1,)), ((), ())),
                    preferred_element_type=F32,
                )
            )
        p0, p1, p2 = ([part[f * PLANE : (f + 1) * PLANE] for f in range(3)] for part in parts)
        gact = jnp.concatenate(
            [p0[0] + p0[1] + p0[2] + p1[0] + p1[1] + p2[0], p1[2] + p2[1], p2[2]], axis=0
        )
        xhat = xhat_s[unit]
        inner = gact.reshape(PIX // COLS, COLS, C) * slope_s[unit]
        mean_a = group_sum(jnp.sum(inner, axis=0)) * count
        mean_b = group_sum(jnp.sum(inner * xhat, axis=0)) * count
        slant = (inner - mean_a.reshape(1, 1, C) - xhat * mean_b.reshape(1, 1, C)) * rstd_s[unit].reshape(
            1, 1, C
        )
        gs[unit] = (grad + slant.reshape(PIX, C)).astype(BF16)
        start_home(gs.at[unit], grad_out, 3, ing_recv, unit, owner)
        return 0

    lax.fori_loop(0, UNITS, backward, 0)

    @pl.when(half == 1)
    def _():
        hop_g.start()

    home(acts.at[y], actb, 1, act_recv, y)[2]().wait()
    home(gs.at[y + 1], grdb, 2, grd_recv, y)[2]().wait()
    arrived(actb, act_recv, (yr, yo, yl))
    arrived(grdb, grd_recv, (yr, yo, yl))

    def wgrad(clip, _):
        act = actb[clip].astype(F32)
        turned = [act[f * PLANE : (f + 1) * PLANE].T.astype(BF16) for f in range(FRAMES)]
        lhs = jnp.concatenate(
            [
                jnp.concatenate([turned[max(f - 2 + frame_off, 0)] for f in range(FRAMES)], axis=1)
                for frame_off in range(3)
            ],
            axis=0,
        )
        fill_shifts(grdb[clip].astype(F32).reshape(PIX // COLS, COLS, C), shifts, True)
        for tap in range(TAPS):
            block = dot(lhs, shifts[:, tap * C : (tap + 1) * C])
            for frame_off in range(3):
                at = (frame_off * TAPS + tap) * C
                part = block[frame_off * C : (frame_off + 1) * C]
                total[at : at + C] = total[at : at + C] + part
        return 0

    total[...] = jnp.zeros_like(total)
    lax.fori_loop(0, UNITS, wgrad, 0)

    chunk = WROWS // (4 * depth)
    for at_z in range(depth):
        for at_x in range(2):
            for at_core in range(2):
                start = (at_z * 4 + at_x * 2 + at_core) * chunk
                buf1[at_core, at_x, at_z] = total[start : start + chunk].astype(BF16)
    copy = remote(buf1.at[1 - core], got1, rs_send.at[0], rs_recv.at[0], dev(pipe, other_core))
    copy.start()
    copy.wait()
    buf2[...] = (buf1[core].astype(F32) + got1[...].astype(F32)).astype(BF16)
    copy = remote(buf2.at[1 - x_lo], got2, rs_send.at[1], rs_recv.at[1], dev(pipe, other_x))
    copy.start()
    copy.wait()
    buf3[...] = (buf2[x_lo].astype(F32) + got2[...].astype(F32)).astype(BF16)

    def z_copy(step):
        target = lax.rem(z + step, depth)
        return remote(
            buf3.at[target], got3.at[step - 1], z_send.at[step - 1], z_recv.at[step - 1], dev(pipe, z_peer(step))
        )

    for step in range(1, depth):
        z_copy(step).start()
    result = buf3[z].astype(F32)
    for step in range(1, depth):
        z_copy(step).wait_recv()
        result = result + got3[step - 1].astype(F32)
    wg_out[...] = result * scale

    for step in range(1, depth):
        z_copy(step).wait_send()
    for copy in sent:
        copy.wait_send()
    for slot, at in enumerate((yr, yo, yl)):
        gain_copy(at, slot).wait_send()
    for unit in range(UNITS):
        finish_home(xs.at[unit + 1], seg_out, 0, seg_recv, unit, owner)
        finish_home(gs.at[unit], grad_out, 3, ing_recv, unit, owner)

        @pl.when(unit != y)
        def _():
            home(acts.at[unit], actb, 1, act_recv, unit)[1]().wait_send()
            home(gs.at[unit + 1], grdb, 2, grd_recv, unit)[1]().wait_send()

    @pl.when(half == 0)
    def _():
        hop_x.wait_send()

    @pl.when(half == 1)
    def _():
        cot_copy.wait_send()
        hop_g.wait_send()
        arrived(seg_out, seg_recv, (y,))
        arrived(grad_out, ing_recv, (y,))

    arrived(seg_out, seg_recv, (yr, yo, yl))
    arrived(grad_out, ing_recv, (yr, yo, yl))


def write_results(seg, grad, share, seg_out, grad_out, share_out):
    seg_out[...] = seg[...]
    grad_out[...] = grad[...]
    for row in range(share.shape[0]):
        share_out[:, row * C : (row + 1) * C] = share[row : row + 1]


def body(video, cotangent, weights, gains):
    micro = video.shape[0]
    devices = lax.axis_size("dp")
    depth = devices // 4
    chunk = WROWS // devices
    scale = 1.0 / math.sqrt(micro * devices * PIX)
    clip = (PIX, C)
    any_spec = pl.BlockSpec(memory_space=pl.ANY)
    dma = pltpu.SemaphoreType.DMA
    outputs, grads_out, share = pl.pallas_call(
        functools.partial(kernel, depth, scale),
        out_shape=(
            jax.ShapeDtypeStruct((micro, *clip), BF16),
            jax.ShapeDtypeStruct((micro, *clip), BF16),
            jax.ShapeDtypeStruct((chunk, C), F32),
        ),
        in_specs=[any_spec] * 4,
        out_specs=(any_spec, any_spec, pl.BlockSpec(memory_space=pltpu.VMEM)),
        scratch_shapes=[
            pltpu.VMEM((UNITS, WROWS, C), BF16),
            pltpu.VMEM((UNITS, 1, C), F32),
            pltpu.VMEM((UNITS + 1, *clip), BF16),
            pltpu.VMEM((UNITS + 1, *clip), BF16),
            pltpu.VMEM((UNITS, *clip), BF16),
            pltpu.VMEM((UNITS, PIX // COLS, COLS, C), F32),
            pltpu.VMEM((UNITS, PIX // COLS, COLS, C), F32),
            pltpu.VMEM((UNITS, 1, C), F32),
            pltpu.VMEM((PIX, SLAB), BF16),
            pltpu.VMEM((UNITS, *clip), BF16),
            pltpu.VMEM((UNITS, *clip), BF16),
            pltpu.VMEM((WROWS, C), F32),
            pltpu.VMEM((2, 2, depth, chunk, C), BF16),
            pltpu.VMEM((2, depth, chunk, C), BF16),
            pltpu.VMEM((2, depth, chunk, C), BF16),
            pltpu.VMEM((depth, chunk, C), BF16),
            pltpu.VMEM((depth, chunk, C), BF16),
            pltpu.VMEM((max(depth - 1, 1), chunk, C), BF16),
            dma((3,)),
            dma((24,)),
            dma((UNITS, 8)),
            dma((3,)),
            dma((UNITS,)),
            dma((3,)),
            dma((3,)),
            dma((4, UNITS)),
            dma((UNITS,)),
            dma((UNITS,)),
            dma((UNITS,)),
            dma((UNITS,)),
            dma((2,)),
            dma((2,)),
            dma((max(depth - 1, 1),)),
            dma((max(depth - 1, 1),)),
        ],
        compiler_params=pltpu.CompilerParams(collective_id=0, has_side_effects=True),
    )(
        video.reshape(micro, *clip),
        cotangent.reshape(micro, *clip),
        weights.reshape(WROWS, C),
        gains,
    )
    whole = pl.BlockSpec(memory_space=pltpu.VMEM)
    outputs, grads_out, share = pl.pallas_call(
        write_results,
        out_shape=(
            jax.ShapeDtypeStruct((micro, *clip), BF16),
            jax.ShapeDtypeStruct((micro, *clip), BF16),
            jax.ShapeDtypeStruct((1, chunk * C), F32),
        ),
        in_specs=[whole] * 3,
        out_specs=(whole,) * 3,
    )(outputs, grads_out, share)
    full = (1, micro, 1, FRAMES, ROWS, COLS, C)
    return (outputs.reshape(full), grads_out.reshape(full), share)


def solution(mesh):
    in_specs = (
        P(None, "dp", None, None, None, None),
        P(None, "dp", None, None, None, None),
        P("pipe", None, None),
        P("pipe", None),
    )
    out_specs = (
        P("pipe", None, "dp", None, None, None, None),
        P("pipe", None, "dp", None, None, None, None),
        P("pipe", "dp"),
    )
    return jax.shard_map(body, mesh=mesh, in_specs=in_specs, out_specs=out_specs, check_vma=False)
```

```python
import functools
import math

import jax
import jax.numpy as jnp
from jax import lax
from jax.experimental import pallas as pl
from jax.experimental.pallas import tpu as pltpu
from jax.sharding import PartitionSpec as P

GROUPS = 32
UNITS = 4
FRAMES, ROWS, COLS, C = 3, 16, 8, 128
PLANE = ROWS * COLS
PIX = FRAMES * PLANE
TAPS = 9
SLAB = TAPS * C
WROWS = 3 * SLAB
EIGHTH = WROWS // 8
MESH = pl.DeviceIdType.MESH
F32, BF16 = jnp.float32, jnp.bfloat16


def group_sum(part):
    lane = lax.broadcasted_iota(jnp.int32, part.shape, 1)
    pair = part + jnp.where(lane % 2 == 0, pltpu.roll(part, C - 1, 1), pltpu.roll(part, 1, 1))
    quad = pair + jnp.where(lane % 4 < 2, pltpu.roll(pair, C - 2, 1), pltpu.roll(pair, 2, 1))
    return jnp.sum(quad, axis=0, keepdims=True)


def fill_shifts(field, dest, clip, flip):
    col = lax.broadcasted_iota(jnp.int32, field.shape, 1)
    for col_off in range(3):
        step = (1 - col_off) if flip else (col_off - 1)
        if step == 0:
            moved = field
        elif step == 1:
            moved = jnp.where(col < COLS - 1, pltpu.roll(field, COLS - 1, 1), 0.0)
        else:
            moved = jnp.where(col > 0, pltpu.roll(field, 1, 1), 0.0)
        planes = moved.reshape(FRAMES, ROWS, COLS, C)
        blank = jnp.zeros((FRAMES, 1, COLS, C), F32)
        for row_off in range(3):
            step = (1 - row_off) if flip else (row_off - 1)
            if step == 0:
                rows = planes
            elif step == 1:
                rows = jnp.concatenate([planes[:, 1:], blank], axis=1)
            else:
                rows = jnp.concatenate([blank, planes[:, : ROWS - 1]], axis=1)
            dest[row_off * 3 + col_off, clip] = rows.reshape(PIX, C).astype(BF16)


def beside(parts):
    return jnp.concatenate(parts, axis=1)


def dot(lhs, rhs):
    return jnp.dot(lhs, rhs, preferred_element_type=F32)


def kernel(
    depth,
    scale,
    video,
    cot,
    w,
    gains,
    seg_out,
    grad_out,
    wg_out,
    wb,
    gbuf,
    xs,
    gs,
    acts,
    xhat_s,
    slope_s,
    rstd_s,
    shifts,
    actb,
    grdb,
    turned,
    total,
    buf1,
    got1,
    buf2,
    got2,
    buf3,
    got3,
    load_sem,
    w_send,
    w_recv,
    gain_send,
    gain_recv,
    hop_send,
    hop_recv,
    out_send,
    seg_recv,
    act_recv,
    grd_recv,
    ing_recv,
    rs_send,
    rs_recv,
):
    pipe = lax.axis_index("pipe")
    dp = lax.axis_index("dp")
    half = lax.div(pipe, UNITS)
    y = lax.rem(pipe, UNITS)
    core = lax.rem(dp, 2)
    x_lo = lax.rem(lax.div(dp, 2), 2)
    z = lax.div(dp, 4)
    base = half * UNITS
    yr = lax.rem(y + 1, UNITS)
    yo = lax.rem(y + 2, UNITS)
    yl = lax.rem(y + 3, UNITS)
    other_core = dp + 1 - 2 * core
    other_x = dp + 2 - 4 * x_lo
    other_half = pipe + UNITS - 2 * base
    other_z = dp + 4 - 8 * lax.rem(z, 2)
    owner = dp + half * (2 - 4 * x_lo)

    def dev(pipe_at, dp_at):
        return (pipe_at, dp_at)

    def z_peer(step):
        return lax.rem(z + step, depth) * 4 + lax.rem(dp, 4)

    def remote(src, dst, send, recv, target):
        return pltpu.make_async_remote_copy(
            src_ref=src, dst_ref=dst, send_sem=send, recv_sem=recv, device_id=target, device_id_type=MESH
        )

    load_w = pltpu.make_async_copy(w, wb.at[y], load_sem.at[0])
    load_w.start()
    load_gain = pltpu.make_async_copy(gains, gbuf.at[y], load_sem.at[1])
    load_gain.start()

    load_x = pltpu.make_async_copy(video.at[y], xs.at[0], load_sem.at[2])
    cot_copy = remote(cot.at[y], gs.at[UNITS], hop_send.at[2], hop_recv.at[2], dev(pipe, other_x))

    @pl.when(half == 0)
    def _():
        load_x.start()

    barrier = pltpu.get_barrier_semaphore()
    peers = [dev(base + at, dp) for at in (yr, yo, yl)]
    peers += [dev(base + at, other_x) for at in (y, yr, yo, yl)]
    peers += [dev(other_half, other_x), dev(pipe, other_core)]
    peers += [dev(pipe, z_peer(step)) for step in range(1, depth)]
    for peer in peers:
        pl.semaphore_signal(barrier, inc=1, device_id=peer, device_id_type=MESH)
    pl.semaphore_wait(barrier, len(peers))

    def gain_copy(at, slot):
        return remote(gains, gbuf.at[y], gain_send.at[slot], gain_recv.at[y], dev(base + at, dp))

    for slot, at in enumerate((yr, yo, yl)):
        gain_copy(at, slot).start()

    @pl.when(half == 1)
    def _():
        cot_copy.start()

    parity = lax.rem(x_lo + z, 2)
    qa, qb = (parity * 2 + at for at in range(2))
    pa, pb = ((1 - parity) * 2 + at for at in range(2))
    right, left, twin = dev(base + yr, dp), dev(base + yl, dp), dev(pipe, other_core)
    near_x, near_z = dev(pipe, other_x), dev(pipe, other_z)

    def rows_of(quarter, which):
        return pl.ds(pl.multiple_of((quarter * 2 + which) * EIGHTH, EIGHTH), EIGHTH)

    def own(quarter, slot, target):
        return remote(
            w.at[rows_of(quarter, core)],
            wb.at[y, rows_of(quarter, core)],
            w_send.at[slot],
            w_recv.at[y, quarter * 2 + core],
            target,
        )

    def relay(slab, quarter, slot, target, which=core):
        piece = wb.at[slab, rows_of(quarter, which)]
        return remote(piece, piece, w_send.at[slot], w_recv.at[slab, quarter * 2 + which], target)

    sent = [own(qa, 0, right), own(qb, 1, left), own(qb, 2, right), own(qa, 3, left)]
    for copy in sent:
        copy.start()
    relays = [
        (yl, qa, (right, twin, near_x)),
        (yr, qb, (left, twin, near_z)),
        (yl, qb, (twin, near_z)),
        (yr, qa, (twin, near_x)),
        (yl, pa, (twin,)),
        (yr, pb, (twin,)),
        (yo, qa, (twin, near_x)),
        (yo, qb, (twin, near_z)),
        (yr, pa, (twin,)),
        (yl, pb, (twin,)),
        (yo, pa, (twin,)),
        (yo, pb, (twin,)),
    ]
    for slab, quarter, targets in relays:
        relay(slab, quarter, 0, right).wait_recv()
        for target in targets:
            copy = relay(slab, quarter, len(sent), target)
            copy.start()
            sent.append(copy)
    for slab in (yl, yr, yo):
        for quarter in range(4):
            relay(slab, quarter, 0, twin, 1 - core).wait_recv()
    load_w.wait()
    load_gain.wait()
    for slot, at in enumerate((yr, yo, yl)):
        remote(gains, gbuf.at[at], gain_send.at[slot], gain_recv.at[at], dev(base + at, dp)).wait_recv()

    def home(src, dst, slot, recv, unit, holder=dp):
        local = (unit == y) & (holder == dp)

        def away():
            return remote(src, dst.at[y], out_send.at[slot, unit], recv.at[y], dev(base + unit, holder))

        def here():
            return pltpu.make_async_copy(src, dst.at[y], out_send.at[slot, unit])

        return local, away, here

    def start_home(*args):
        local, away, here = home(*args)

        @pl.when(jnp.logical_not(local))
        def _():
            away().start()

        @pl.when(local)
        def _():
            here().start()

    def finish_home(*args):
        local, away, here = home(*args)

        @pl.when(jnp.logical_not(local))
        def _():
            away().wait_send()

        @pl.when(local)
        def _():
            here().wait()

    def arrived(dst, recv, places):
        for at in places:
            remote(dst.at[at], dst.at[at], out_send.at[0, 0], recv.at[at], near_x).wait_recv()

    hop_x = remote(xs.at[UNITS], xs.at[0], hop_send.at[0], hop_recv.at[0], dev(other_half, other_x))
    hop_g = remote(gs.at[0], gs.at[UNITS], hop_send.at[1], hop_recv.at[1], dev(other_half, other_x))

    @pl.when(half == 0)
    def _():
        load_x.wait()

    @pl.when(half == 1)
    def _():
        cot_copy.wait_recv()
        hop_x.wait_recv()

    count = 1.0 / (PIX * (C // GROUPS))

    def forward(unit, _):
        gain = gbuf[unit].reshape(1, 1, C)
        x = xs[unit].astype(F32).reshape(PIX // COLS, COLS, C)
        mean = group_sum(jnp.sum(x, axis=0)) * count
        centred = x - mean.reshape(1, 1, C)
        var = group_sum(jnp.sum(centred * centred, axis=0)) * count
        rstd = lax.rsqrt(var + 1e-06)
        xhat = centred * rstd.reshape(1, 1, C)
        normed = xhat * gain
        sig = jax.nn.sigmoid(normed)
        act = normed * sig
        acts[unit] = act.reshape(PIX, C).astype(BF16)
        fill_shifts(act, shifts, 0, False)
        xhat_s[unit] = xhat
        slope_s[unit] = (sig + act * (1.0 - sig)) * gain
        rstd_s[unit] = rstd
        lhs = beside([shifts[tap, 0] for tap in range(TAPS)])
        part0 = dot(lhs[:PLANE], wb[unit, :SLAB])
        part1 = dot(lhs[: 2 * PLANE], wb[unit, SLAB : 2 * SLAB])
        part2 = dot(lhs, wb[unit, 2 * SLAB :])
        x = x.reshape(PIX, C)
        early = part0 + part1[:PLANE]
        branch = (early, early, part0 + part1[PLANE:])
        for frame in range(FRAMES):
            at = slice(frame * PLANE, (frame + 1) * PLANE)
            xs[unit + 1, at] = (x[at] + branch[frame] + part2[at]).astype(BF16)
        start_home(acts.at[unit], actb, 1, act_recv, unit)
        return 0

    lax.fori_loop(0, UNITS, forward, 0)

    def send_outputs():
        for unit in range(UNITS):
            start_home(xs.at[unit + 1], seg_out, 0, seg_recv, unit, owner)

    def turn_acts():
        home(acts.at[y], actb, 1, act_recv, y)[2]().wait()
        arrived(actb, act_recv, (yr, yo, yl))

        def turn(clip, _):
            act = actb[clip].astype(F32)
            frames = [act[f * PLANE : (f + 1) * PLANE].T.astype(BF16) for f in range(FRAMES)]
            for frame_off in range(3):
                turned[clip, frame_off] = beside([frames[max(f - 2 + frame_off, 0)] for f in range(FRAMES)])
            return 0

        lax.fori_loop(0, UNITS, turn, 0)

    @pl.when(half == 0)
    def _():
        hop_x.start()
        send_outputs()
        turn_acts()
        hop_g.wait_recv()

    def backward(step, _):
        unit = UNITS - 1 - step
        start_home(gs.at[unit + 1], grdb, 2, grd_recv, unit)
        grad = gs[unit + 1].astype(F32)
        fill_shifts(grad.reshape(PIX // COLS, COLS, C), shifts, 0, True)
        lhs = beside([shifts[tap, 0] for tap in range(TAPS)])
        parts = []
        for frame_off in range(3):
            taps = [
                wb[unit, frame_off * SLAB + tap * C : frame_off * SLAB + (tap + 1) * C]
                for tap in range(TAPS)
            ]
            parts.append(
                lax.dot_general(
                    lhs,
                    beside(taps),
                    (((1,), (1,)), ((), ())),
                    preferred_element_type=F32,
                )
            )
        p0, p1, p2 = ([part[f * PLANE : (f + 1) * PLANE] for f in range(3)] for part in parts)
        gact = jnp.concatenate(
            [p0[0] + p0[1] + p0[2] + p1[0] + p1[1] + p2[0], p1[2] + p2[1], p2[2]], axis=0
        )
        xhat = xhat_s[unit]
        inner = gact.reshape(PIX // COLS, COLS, C) * slope_s[unit]
        mean_a = group_sum(jnp.sum(inner, axis=0)) * count
        mean_b = group_sum(jnp.sum(inner * xhat, axis=0)) * count
        slant = (inner - mean_a.reshape(1, 1, C) - xhat * mean_b.reshape(1, 1, C)) * rstd_s[unit].reshape(
            1, 1, C
        )
        gs[unit] = (grad + slant.reshape(PIX, C)).astype(BF16)
        return 0

    lax.fori_loop(0, UNITS, backward, 0)

    @pl.when(half == 1)
    def _():
        hop_g.start()
        turn_acts()

    home(gs.at[y + 1], grdb, 2, grd_recv, y)[2]().wait()
    arrived(grdb, grd_recv, (yr, yo, yl))

    @pl.when(half == 1)
    def _():
        send_outputs()

    for unit in range(UNITS):
        start_home(gs.at[unit], grad_out, 3, ing_recv, unit, owner)

    def spread(clip, _):
        fill_shifts(grdb[clip].astype(F32).reshape(PIX // COLS, COLS, C), shifts, clip, True)
        return 0

    lax.fori_loop(0, UNITS, spread, 0)
    lhs = beside([turned[clip].reshape(3 * C, PIX) for clip in range(UNITS)])
    for first in range(0, TAPS, 2):
        taps = range(first, min(first + 2, TAPS))
        block = dot(lhs, beside([shifts[tap].reshape(UNITS * PIX, C) for tap in taps]))
        for tap in taps:
            for frame_off in range(3):
                at = (frame_off * TAPS + tap) * C
                total[at : at + C] = block[frame_off * C : (frame_off + 1) * C, (tap - first) * C :][:, :C]

    chunk = WROWS // (4 * depth)
    for at_z in range(depth):
        for at_x in range(2):
            for at_core in range(2):
                start = (at_z * 4 + at_x * 2 + at_core) * chunk
                buf1[at_z, at_core, at_x] = total[start : start + chunk].astype(BF16)
    steps = sorted(range(depth), key=lambda step: -min(step, depth - step))
    places = [lax.rem(z + step, depth) for step in steps]

    def core_copy(at):
        return remote(buf1.at[at, 1 - core], got1.at[at], rs_send.at[0, at], rs_recv.at[0, at], twin)

    def x_copy(at):
        return remote(buf2.at[at, 1 - x_lo], got2.at[at], rs_send.at[1, at], rs_recv.at[1, at], near_x)

    def z_copy(at):
        target = dev(pipe, at * 4 + lax.rem(dp, 4))
        return remote(buf3.at[at], got3.at[z], rs_send.at[2, at], rs_recv.at[2, z], target)

    for at in places:
        core_copy(at).start()
    for at in places:
        core_copy(at).wait_recv()
        buf2[at] = (buf1[at, core].astype(F32) + got1[at].astype(F32)).astype(BF16)
        x_copy(at).start()
    for step, at in zip(steps, places):
        x_copy(at).wait_recv()
        buf3[at] = (buf2[at, x_lo].astype(F32) + got2[at].astype(F32)).astype(BF16)
        if step:
            z_copy(at).start()
    result = buf3[z].astype(F32)
    for step in reversed(steps):
        if step:
            at = lax.rem(z + step, depth)
            remote(got3.at[at], got3.at[at], rs_send.at[2, at], rs_recv.at[2, at], twin).wait_recv()
            result = result + got3[at].astype(F32)
    wg_out[...] = result * scale

    for step, at in zip(steps, places):
        core_copy(at).wait_send()
        x_copy(at).wait_send()
        if step:
            z_copy(at).wait_send()
    for copy in sent:
        copy.wait_send()
    for slot, at in enumerate((yr, yo, yl)):
        gain_copy(at, slot).wait_send()
    for unit in range(UNITS):
        finish_home(xs.at[unit + 1], seg_out, 0, seg_recv, unit, owner)
        finish_home(gs.at[unit], grad_out, 3, ing_recv, unit, owner)

        @pl.when(unit != y)
        def _():
            home(acts.at[unit], actb, 1, act_recv, unit)[1]().wait_send()
            home(gs.at[unit + 1], grdb, 2, grd_recv, unit)[1]().wait_send()

    @pl.when(half == 0)
    def _():
        hop_x.wait_send()

    @pl.when(half == 1)
    def _():
        cot_copy.wait_send()
        hop_g.wait_send()
        arrived(seg_out, seg_recv, (y,))
        arrived(grad_out, ing_recv, (y,))

    arrived(seg_out, seg_recv, (yr, yo, yl))
    arrived(grad_out, ing_recv, (yr, yo, yl))


def write_results(seg, grad, share, seg_out, grad_out, share_out, flat, sem):
    copies = [
        pltpu.make_async_copy(seg, seg_out, sem.at[0]),
        pltpu.make_async_copy(grad, grad_out, sem.at[1]),
        pltpu.make_async_copy(flat, share_out, sem.at[2]),
    ]
    copies[0].start()
    copies[1].start()
    for row in range(share.shape[0]):
        flat[:, row * C : (row + 1) * C] = share[row : row + 1]
    copies[2].start()
    for copy in copies:
        copy.wait()


def body(video, cotangent, weights, gains):
    micro = video.shape[0]
    devices = lax.axis_size("dp")
    depth = devices // 4
    chunk = WROWS // devices
    scale = 1.0 / math.sqrt(micro * devices * PIX)
    clip = (PIX, C)
    any_spec = pl.BlockSpec(memory_space=pl.ANY)
    dma = pltpu.SemaphoreType.DMA
    outputs, grads_out, share = pl.pallas_call(
        functools.partial(kernel, depth, scale),
        out_shape=(
            jax.ShapeDtypeStruct((micro, *clip), BF16),
            jax.ShapeDtypeStruct((micro, *clip), BF16),
            jax.ShapeDtypeStruct((chunk, C), F32),
        ),
        in_specs=[pl.BlockSpec(memory_space=pltpu.HBM)] * 4,
        out_specs=(any_spec, any_spec, pl.BlockSpec(memory_space=pltpu.VMEM)),
        scratch_shapes=[
            pltpu.VMEM((UNITS, WROWS, C), BF16),
            pltpu.VMEM((UNITS, 1, C), F32),
            pltpu.VMEM((UNITS + 1, *clip), BF16),
            pltpu.VMEM((UNITS + 1, *clip), BF16),
            pltpu.VMEM((UNITS, *clip), BF16),
            pltpu.VMEM((UNITS, PIX // COLS, COLS, C), F32),
            pltpu.VMEM((UNITS, PIX // COLS, COLS, C), F32),
            pltpu.VMEM((UNITS, 1, C), F32),
            pltpu.VMEM((TAPS, UNITS, *clip), BF16),
            pltpu.VMEM((UNITS, *clip), BF16),
            pltpu.VMEM((UNITS, *clip), BF16),
            pltpu.VMEM((UNITS, 3, C, PIX), BF16),
            pltpu.VMEM((WROWS, C), F32),
            pltpu.VMEM((depth, 2, 2, chunk, C), BF16),
            pltpu.VMEM((depth, 2, chunk, C), BF16),
            pltpu.VMEM((depth, 2, chunk, C), BF16),
            pltpu.VMEM((depth, chunk, C), BF16),
            pltpu.VMEM((depth, chunk, C), BF16),
            pltpu.VMEM((depth, chunk, C), BF16),
            dma((3,)),
            dma((24,)),
            dma((UNITS, 8)),
            dma((3,)),
            dma((UNITS,)),
            dma((3,)),
            dma((3,)),
            dma((4, UNITS)),
            dma((UNITS,)),
            dma((UNITS,)),
            dma((UNITS,)),
            dma((UNITS,)),
            dma((3, depth)),
            dma((3, depth)),
        ],
        compiler_params=pltpu.CompilerParams(collective_id=0, has_side_effects=True, vmem_limit_bytes=32 << 20),
    )(
        *(
            pltpu.with_memory_space_constraint(array, pltpu.HBM)
            for array in (
                video.reshape(micro, *clip),
                cotangent.reshape(micro, *clip),
                weights.reshape(WROWS, C),
                gains,
            )
        )
    )
    whole = pl.BlockSpec(memory_space=pltpu.VMEM)
    outputs, grads_out, share = pl.pallas_call(
        write_results,
        out_shape=(
            jax.ShapeDtypeStruct((micro, *clip), BF16),
            jax.ShapeDtypeStruct((micro, *clip), BF16),
            jax.ShapeDtypeStruct((1, chunk * C), F32),
        ),
        in_specs=[any_spec, any_spec, whole],
        out_specs=(pl.BlockSpec(memory_space=pltpu.HBM),) * 3,
        scratch_shapes=[pltpu.VMEM((1, chunk * C), F32), dma((3,))],
        compiler_params=pltpu.CompilerParams(vmem_limit_bytes=4 << 20),
    )(outputs, grads_out, share)
    full = (1, micro, 1, FRAMES, ROWS, COLS, C)
    return (outputs.reshape(full), grads_out.reshape(full), share)


def solution(mesh):
    in_specs = (
        P(None, "dp", None, None, None, None),
        P(None, "dp", None, None, None, None),
        P("pipe", None, None),
        P("pipe", None),
    )
    out_specs = (
        P("pipe", None, "dp", None, None, None, None),
        P("pipe", None, "dp", None, None, None, None),
        P("pipe", "dp"),
    )
    return jax.shard_map(body, mesh=mesh, in_specs=in_specs, out_specs=out_specs, check_vma=False)
```

```python
import functools
import math

import jax
import jax.numpy as jnp
from jax import lax
from jax.experimental import pallas as pl
from jax.experimental.pallas import tpu as pltpu
from jax.sharding import PartitionSpec as P

GROUPS = 32
UNITS = 4
FRAMES, ROWS, COLS, C = 3, 16, 8, 128
PLANE = ROWS * COLS
PIX = FRAMES * PLANE
TAPS = 9
SLAB = TAPS * C
WROWS = 3 * SLAB
HALVES = 2
PIECE = WROWS // (8 * HALVES)
MESH = pl.DeviceIdType.MESH
F32, BF16 = jnp.float32, jnp.bfloat16


def group_sum(part):
    lane = lax.broadcasted_iota(jnp.int32, part.shape, 1)
    pair = part + jnp.where(lane % 2 == 0, pltpu.roll(part, C - 1, 1), pltpu.roll(part, 1, 1))
    quad = pair + jnp.where(lane % 4 < 2, pltpu.roll(pair, C - 2, 1), pltpu.roll(pair, 2, 1))
    return jnp.sum(quad, axis=0, keepdims=True)


def fill_shifts(field, dest, clip, flip):
    col = lax.broadcasted_iota(jnp.int32, field.shape, 1)
    for col_off in range(3):
        step = (1 - col_off) if flip else (col_off - 1)
        if step == 0:
            moved = field
        elif step == 1:
            moved = jnp.where(col < COLS - 1, pltpu.roll(field, COLS - 1, 1), 0.0)
        else:
            moved = jnp.where(col > 0, pltpu.roll(field, 1, 1), 0.0)
        planes = moved.reshape(FRAMES, ROWS, COLS, C)
        blank = jnp.zeros((FRAMES, 1, COLS, C), F32)
        for row_off in range(3):
            step = (1 - row_off) if flip else (row_off - 1)
            if step == 0:
                rows = planes
            elif step == 1:
                rows = jnp.concatenate([planes[:, 1:], blank], axis=1)
            else:
                rows = jnp.concatenate([blank, planes[:, : ROWS - 1]], axis=1)
            dest[row_off * 3 + col_off, clip] = rows.reshape(PIX, C).astype(BF16)


def beside(parts):
    return jnp.concatenate(parts, axis=1)


def dot(lhs, rhs):
    return jnp.dot(lhs, rhs, preferred_element_type=F32)


def kernel(
    depth,
    scale,
    video,
    cot,
    w,
    gains,
    seg_out,
    grad_out,
    wg_out,
    wb,
    gbuf,
    xs,
    gs,
    xs2,
    gs2,
    acts,
    xhat_s,
    slope_s,
    rstd_s,
    shifts,
    actb,
    grdb,
    turned,
    total,
    buf1,
    got1,
    buf2,
    got2,
    buf3,
    got3,
    load_sem,
    w_send,
    w_recv,
    gain_send,
    gain_recv,
    hop_send,
    hop_recv,
    out_send,
    seg_recv,
    act_recv,
    grd_recv,
    ing_recv,
    swap_send,
    swap_recv,
    rs_send,
    rs_recv,
):
    pipe = lax.axis_index("pipe")
    dp = lax.axis_index("dp")
    half = lax.div(pipe, UNITS)
    y = lax.rem(pipe, UNITS)
    core = lax.rem(dp, 2)
    x_lo = lax.rem(lax.div(dp, 2), 2)
    z = lax.div(dp, 4)
    base = half * UNITS
    yr = lax.rem(y + 1, UNITS)
    yo = lax.rem(y + 2, UNITS)
    yl = lax.rem(y + 3, UNITS)
    other_core = dp + 1 - 2 * core
    other_x = dp + 2 - 4 * x_lo
    other_half = pipe + UNITS - 2 * base
    other_z = dp + 4 - 8 * lax.rem(z, 2)

    def dev(pipe_at, dp_at):
        return (pipe_at, dp_at)

    def z_peer(step):
        return lax.rem(z + step, depth) * 4 + lax.rem(dp, 4)

    def remote(src, dst, send, recv, target):
        return pltpu.make_async_remote_copy(
            src_ref=src, dst_ref=dst, send_sem=send, recv_sem=recv, device_id=target, device_id_type=MESH
        )

    load_w = pltpu.make_async_copy(w, wb.at[y], load_sem.at[0])
    load_w.start()
    load_gain = pltpu.make_async_copy(gains, gbuf.at[y], load_sem.at[1])
    load_gain.start()

    load_x = pltpu.make_async_copy(video.at[y], xs.at[0], load_sem.at[2])
    cot_copy = remote(cot.at[y], gs.at[UNITS], hop_send.at[2], hop_recv.at[2], dev(pipe, other_x))

    @pl.when(half == 0)
    def _():
        load_x.start()

    barrier = pltpu.get_barrier_semaphore()
    peers = [dev(base + at, dp) for at in (yr, yo, yl)]
    peers += [dev(pipe, other_x), dev(other_half, other_x), dev(pipe, other_core)]
    peers += [dev(pipe, z_peer(step)) for step in range(1, depth)]
    for peer in peers:
        pl.semaphore_signal(barrier, inc=1, device_id=peer, device_id_type=MESH)
    pl.semaphore_wait(barrier, len(peers))

    def gain_copy(at, slot):
        return remote(gains, gbuf.at[y], gain_send.at[slot], gain_recv.at[y], dev(base + at, dp))

    for slot, at in enumerate((yr, yo, yl)):
        gain_copy(at, slot).start()

    @pl.when(half == 1)
    def _():
        cot_copy.start()

    parity = lax.rem(x_lo + z, 2)
    qa, qb = (parity * 2 + at for at in range(2))
    pa, pb = ((1 - parity) * 2 + at for at in range(2))
    right, left, twin = dev(base + yr, dp), dev(base + yl, dp), dev(pipe, other_core)
    near_x, near_z = dev(pipe, other_x), dev(pipe, other_z)

    def place_of(quarter, part, which):
        return (quarter * 2 + which) * HALVES + part

    def rows_of(place):
        return pl.ds(pl.multiple_of(place * PIECE, PIECE), PIECE)

    def own(quarter, part, slot, target):
        place = place_of(quarter, part, core)
        rows = rows_of(place)
        return remote(w.at[rows], wb.at[y, rows], w_send.at[slot], w_recv.at[y, place], target)

    def relay(slab, quarter, part, slot, target, which=core):
        place = place_of(quarter, part, which)
        piece = wb.at[slab, rows_of(place)]
        return remote(piece, piece, w_send.at[slot], w_recv.at[slab, place], target)

    sent = []
    for quarters in ((qa, qb), (qb, qa)):
        for part in range(HALVES):
            for quarter, target in zip(quarters, (right, left)):
                copy = own(quarter, part, len(sent), target)
                copy.start()
                sent.append(copy)
    rounds = [
        [(yl, qa, (right, near_x, twin)), (yr, qb, (left, near_z, twin))],
        [(yl, qb, (near_z, twin)), (yr, qa, (near_x, twin))],
        [(yl, pa, (twin,)), (yr, pb, (twin,))],
        [(yo, qa, (near_x, twin)), (yo, qb, (near_z, twin))],
        [(yr, pa, (twin,)), (yl, pb, (twin,))],
        [(yo, pa, (twin,)), (yo, pb, (twin,))],
    ]
    for group in rounds:
        for part in range(HALVES):
            for slab, quarter, targets in group:
                relay(slab, quarter, part, 0, right).wait_recv()
                for target in targets:
                    copy = relay(slab, quarter, part, len(sent), target)
                    copy.start()
                    sent.append(copy)
    for slab in (yl, yr, yo):
        for quarter in range(4):
            for part in range(HALVES):
                relay(slab, quarter, part, 0, twin, 1 - core).wait_recv()
    load_w.wait()
    load_gain.wait()
    for slot, at in enumerate((yr, yo, yl)):
        remote(gains, gbuf.at[at], gain_send.at[slot], gain_recv.at[at], dev(base + at, dp)).wait_recv()

    def home(src, dst, slot, recv, unit):
        local = unit == y

        def away():
            return remote(src, dst.at[y], out_send.at[slot, unit], recv.at[y], dev(base + unit, dp))

        def here():
            return pltpu.make_async_copy(src, dst.at[y], out_send.at[slot, unit])

        return local, away, here

    def start_home(*args):
        local, away, here = home(*args)

        @pl.when(jnp.logical_not(local))
        def _():
            away().start()

        @pl.when(local)
        def _():
            here().start()

    def finish_home(*args):
        local, away, here = home(*args)

        @pl.when(jnp.logical_not(local))
        def _():
            away().wait_send()

        @pl.when(local)
        def _():
            here().wait()

    def arrived(dst, recv, places):
        for at in places:
            remote(dst.at[at], dst.at[at], out_send.at[0, 0], recv.at[at], near_x).wait_recv()

    def swap(src, dst, slot, unit):
        return remote(src.at[unit + 1 - slot], dst.at[unit], swap_send.at[slot, unit], swap_recv.at[slot, unit], near_x)

    hop_x = remote(xs.at[UNITS], xs.at[0], hop_send.at[0], hop_recv.at[0], dev(other_half, other_x))
    hop_g = remote(gs.at[0], gs.at[UNITS], hop_send.at[1], hop_recv.at[1], dev(other_half, other_x))

    @pl.when(half == 0)
    def _():
        load_x.wait()

    @pl.when(half == 1)
    def _():
        cot_copy.wait_recv()
        hop_x.wait_recv()

    count = 1.0 / (PIX * (C // GROUPS))

    def forward(unit, _):
        gain = gbuf[unit].reshape(1, 1, C)
        x = xs[unit].astype(F32).reshape(PIX // COLS, COLS, C)
        mean = group_sum(jnp.sum(x, axis=0)) * count
        centred = x - mean.reshape(1, 1, C)
        var = group_sum(jnp.sum(centred * centred, axis=0)) * count
        rstd = lax.rsqrt(var + 1e-06)
        xhat = centred * rstd.reshape(1, 1, C)
        normed = xhat * gain
        sig = jax.nn.sigmoid(normed)
        act = normed * sig
        acts[unit] = act.reshape(PIX, C).astype(BF16)
        fill_shifts(act, shifts, 0, False)
        xhat_s[unit] = xhat
        slope_s[unit] = (sig + act * (1.0 - sig)) * gain
        rstd_s[unit] = rstd
        lhs = beside([shifts[tap, 0] for tap in range(TAPS)])
        part0 = dot(lhs[:PLANE], wb[unit, :SLAB])
        part1 = dot(lhs[: 2 * PLANE], wb[unit, SLAB : 2 * SLAB])
        part2 = dot(lhs, wb[unit, 2 * SLAB :])
        x = x.reshape(PIX, C)
        early = part0 + part1[:PLANE]
        branch = (early, early, part0 + part1[PLANE:])
        for frame in range(FRAMES):
            at = slice(frame * PLANE, (frame + 1) * PLANE)
            xs[unit + 1, at] = (x[at] + branch[frame] + part2[at]).astype(BF16)
        start_home(acts.at[unit], actb, 1, act_recv, unit)

        @pl.when(half == 1)
        def _():
            swap(xs, xs2, 0, unit).start()

        return 0

    lax.fori_loop(0, UNITS, forward, 0)

    def send_outputs(kept, slot, swapped, dst, recv):
        for unit in range(UNITS):

            @pl.when(half == 0)
            def _():
                start_home(kept.at[unit + 1 - slot // 3], dst, slot, recv, unit)

            @pl.when(half == 1)
            def _():
                swap(kept, swapped, slot // 3, unit).wait_recv()
                start_home(swapped.at[unit], dst, slot, recv, unit)

    def turn_acts():
        home(acts.at[y], actb, 1, act_recv, y)[2]().wait()
        arrived(actb, act_recv, (yr, yo, yl))

        def turn(clip, _):
            act = actb[clip].astype(F32)
            frames = [act[f * PLANE : (f + 1) * PLANE].T.astype(BF16) for f in range(FRAMES)]
            for frame_off in range(3):
                turned[clip, frame_off] = beside([frames[max(f - 2 + frame_off, 0)] for f in range(FRAMES)])
            return 0

        lax.fori_loop(0, UNITS, turn, 0)

    @pl.when(half == 0)
    def _():
        hop_x.start()
        turn_acts()

    @pl.when(half == 0)
    def _():
        send_outputs(xs, 0, xs2, seg_out, seg_recv)
        hop_g.wait_recv()

    def backward(step, _):
        unit = UNITS - 1 - step
        start_home(gs.at[unit + 1], grdb, 2, grd_recv, unit)
        grad = gs[unit + 1].astype(F32)
        fill_shifts(grad.reshape(PIX // COLS, COLS, C), shifts, 0, True)
        lhs = beside([shifts[tap, 0] for tap in range(TAPS)])
        parts = []
        for frame_off in range(3):
            taps = [
                wb[unit, frame_off * SLAB + tap * C : frame_off * SLAB + (tap + 1) * C]
                for tap in range(TAPS)
            ]
            parts.append(
                lax.dot_general(
                    lhs,
                    beside(taps),
                    (((1,), (1,)), ((), ())),
                    preferred_element_type=F32,
                )
            )
        p0, p1, p2 = ([part[f * PLANE : (f + 1) * PLANE] for f in range(3)] for part in parts)
        gact = jnp.concatenate(
            [p0[0] + p0[1] + p0[2] + p1[0] + p1[1] + p2[0], p1[2] + p2[1], p2[2]], axis=0
        )
        xhat = xhat_s[unit]
        inner = gact.reshape(PIX // COLS, COLS, C) * slope_s[unit]
        mean_a = group_sum(jnp.sum(inner, axis=0)) * count
        mean_b = group_sum(jnp.sum(inner * xhat, axis=0)) * count
        slant = (inner - mean_a.reshape(1, 1, C) - xhat * mean_b.reshape(1, 1, C)) * rstd_s[unit].reshape(
            1, 1, C
        )
        gs[unit] = (grad + slant.reshape(PIX, C)).astype(BF16)

        @pl.when(half == 1)
        def _():
            swap(gs, gs2, 1, unit).start()

        return 0

    lax.fori_loop(0, UNITS, backward, 0)

    @pl.when(half == 1)
    def _():
        hop_g.start()
        turn_acts()

    home(gs.at[y + 1], grdb, 2, grd_recv, y)[2]().wait()

    def spread(step, _):
        clip = lax.rem(y + step + (step // 2) * (5 - 2 * step), UNITS)

        @pl.when(step > 0)
        def _():
            arrived(grdb, grd_recv, (clip,))

        fill_shifts(grdb[clip].astype(F32).reshape(PIX // COLS, COLS, C), shifts, clip, True)
        return 0

    lax.fori_loop(0, UNITS, spread, 0)

    @pl.when(half == 1)
    def _():
        send_outputs(xs, 0, xs2, seg_out, seg_recv)

    lhs = beside([turned[clip].reshape(3 * C, PIX) for clip in range(UNITS)])
    for first in range(0, TAPS, 2):
        taps = range(first, min(first + 2, TAPS))
        block = dot(lhs, beside([shifts[tap].reshape(UNITS * PIX, C) for tap in taps]))
        for tap in taps:
            for frame_off in range(3):
                at = (frame_off * TAPS + tap) * C
                total[at : at + C] = block[frame_off * C : (frame_off + 1) * C, (tap - first) * C :][:, :C]

    chunk = WROWS // (4 * depth)
    for at_z in range(depth):
        for at_x in range(2):
            for at_core in range(2):
                start = (at_z * 4 + at_x * 2 + at_core) * chunk
                buf1[at_z, at_core, at_x] = total[start : start + chunk].astype(BF16)
    steps = sorted(range(depth), key=lambda step: -min(step, depth - step))
    places = [lax.rem(z + step, depth) for step in steps]

    def core_copy(at):
        return remote(buf1.at[at, 1 - core], got1.at[at], rs_send.at[0, at], rs_recv.at[0, at], twin)

    def x_copy(at):
        return remote(buf2.at[at, 1 - x_lo], got2.at[at], rs_send.at[1, at], rs_recv.at[1, at], near_x)

    def z_copy(at):
        target = dev(pipe, at * 4 + lax.rem(dp, 4))
        return remote(buf3.at[at], got3.at[z], rs_send.at[2, at], rs_recv.at[2, z], target)

    for at in places:
        core_copy(at).start()
    for at in places:
        core_copy(at).wait_recv()
        buf2[at] = (buf1[at, core].astype(F32) + got1[at].astype(F32)).astype(BF16)
        x_copy(at).start()
    send_outputs(gs, 3, gs2, grad_out, ing_recv)
    for step, at in zip(steps, places):
        x_copy(at).wait_recv()
        buf3[at] = (buf2[at, x_lo].astype(F32) + got2[at].astype(F32)).astype(BF16)
        if step:
            z_copy(at).start()
    result = buf3[z].astype(F32)
    for step in reversed(steps):
        if step:
            at = lax.rem(z + step, depth)
            remote(got3.at[at], got3.at[at], rs_send.at[2, at], rs_recv.at[2, at], twin).wait_recv()
            result = result + got3[at].astype(F32)
    wg_out[...] = result * scale

    for step, at in zip(steps, places):
        core_copy(at).wait_send()
        x_copy(at).wait_send()
        if step:
            z_copy(at).wait_send()
    for copy in sent:
        copy.wait_send()
    for slot, at in enumerate((yr, yo, yl)):
        gain_copy(at, slot).wait_send()
    for unit in range(UNITS):
        finish_home(xs2.at[unit], seg_out, 0, seg_recv, unit)
        finish_home(gs2.at[unit], grad_out, 3, ing_recv, unit)

        @pl.when(unit != y)
        def _():
            home(acts.at[unit], actb, 1, act_recv, unit)[1]().wait_send()
            home(gs.at[unit + 1], grdb, 2, grd_recv, unit)[1]().wait_send()

    @pl.when(half == 0)
    def _():
        hop_x.wait_send()

    @pl.when(half == 1)
    def _():
        cot_copy.wait_send()
        hop_g.wait_send()
        for unit in range(UNITS):
            swap(xs, xs2, 0, unit).wait_send()
            swap(gs, gs2, 1, unit).wait_send()

    arrived(seg_out, seg_recv, (yr, yo, yl))
    arrived(grad_out, ing_recv, (yr, yo, yl))


def write_results(seg, grad, share, seg_out, grad_out, share_out, flat, sem):
    copies = [
        pltpu.make_async_copy(seg, seg_out, sem.at[0]),
        pltpu.make_async_copy(grad, grad_out, sem.at[1]),
        pltpu.make_async_copy(flat, share_out, sem.at[2]),
    ]
    copies[0].start()
    copies[1].start()
    for row in range(share.shape[0]):
        flat[:, row * C : (row + 1) * C] = share[row : row + 1]
    copies[2].start()
    for copy in copies:
        copy.wait()


def body(video, cotangent, weights, gains):
    micro = video.shape[0]
    devices = lax.axis_size("dp")
    depth = devices // 4
    chunk = WROWS // devices
    scale = 1.0 / math.sqrt(micro * devices * PIX)
    clip = (PIX, C)
    any_spec = pl.BlockSpec(memory_space=pl.ANY)
    dma = pltpu.SemaphoreType.DMA
    outputs, grads_out, share = pl.pallas_call(
        functools.partial(kernel, depth, scale),
        out_shape=(
            jax.ShapeDtypeStruct((micro, *clip), BF16),
            jax.ShapeDtypeStruct((micro, *clip), BF16),
            jax.ShapeDtypeStruct((chunk, C), F32),
        ),
        in_specs=[pl.BlockSpec(memory_space=pltpu.HBM)] * 4,
        out_specs=(any_spec, any_spec, pl.BlockSpec(memory_space=pltpu.VMEM)),
        scratch_shapes=[
            pltpu.VMEM((UNITS, WROWS, C), BF16),
            pltpu.VMEM((UNITS, 1, C), F32),
            pltpu.VMEM((UNITS + 1, *clip), BF16),
            pltpu.VMEM((UNITS + 1, *clip), BF16),
            pltpu.VMEM((UNITS, *clip), BF16),
            pltpu.VMEM((UNITS, *clip), BF16),
            pltpu.VMEM((UNITS, *clip), BF16),
            pltpu.VMEM((UNITS, PIX // COLS, COLS, C), F32),
            pltpu.VMEM((UNITS, PIX // COLS, COLS, C), F32),
            pltpu.VMEM((UNITS, 1, C), F32),
            pltpu.VMEM((TAPS, UNITS, *clip), BF16),
            pltpu.VMEM((UNITS, *clip), BF16),
            pltpu.VMEM((UNITS, *clip), BF16),
            pltpu.VMEM((UNITS, 3, C, PIX), BF16),
            pltpu.VMEM((WROWS, C), F32),
            pltpu.VMEM((depth, 2, 2, chunk, C), BF16),
            pltpu.VMEM((depth, 2, chunk, C), BF16),
            pltpu.VMEM((depth, 2, chunk, C), BF16),
            pltpu.VMEM((depth, chunk, C), BF16),
            pltpu.VMEM((depth, chunk, C), BF16),
            pltpu.VMEM((depth, chunk, C), BF16),
            dma((3,)),
            dma((24 * HALVES,)),
            dma((UNITS, 8 * HALVES)),
            dma((3,)),
            dma((UNITS,)),
            dma((3,)),
            dma((3,)),
            dma((4, UNITS)),
            dma((UNITS,)),
            dma((UNITS,)),
            dma((UNITS,)),
            dma((UNITS,)),
            dma((2, UNITS)),
            dma((2, UNITS)),
            dma((3, depth)),
            dma((3, depth)),
        ],
        compiler_params=pltpu.CompilerParams(collective_id=0, has_side_effects=True, vmem_limit_bytes=32 << 20),
    )(
        *(
            pltpu.with_memory_space_constraint(array, pltpu.HBM)
            for array in (
                video.reshape(micro, *clip),
                cotangent.reshape(micro, *clip),
                weights.reshape(WROWS, C),
                gains,
            )
        )
    )
    whole = pl.BlockSpec(memory_space=pltpu.VMEM)
    outputs, grads_out, share = pl.pallas_call(
        write_results,
        out_shape=(
            jax.ShapeDtypeStruct((micro, *clip), BF16),
            jax.ShapeDtypeStruct((micro, *clip), BF16),
            jax.ShapeDtypeStruct((1, chunk * C), F32),
        ),
        in_specs=[any_spec, any_spec, whole],
        out_specs=(pl.BlockSpec(memory_space=pltpu.HBM),) * 3,
        scratch_shapes=[pltpu.VMEM((1, chunk * C), F32), dma((3,))],
        compiler_params=pltpu.CompilerParams(vmem_limit_bytes=4 << 20),
    )(outputs, grads_out, share)
    full = (1, micro, 1, FRAMES, ROWS, COLS, C)
    return (outputs.reshape(full), grads_out.reshape(full), share)


def solution(mesh):
    in_specs = (
        P(None, "dp", None, None, None, None),
        P(None, "dp", None, None, None, None),
        P("pipe", None, None),
        P("pipe", None),
    )
    out_specs = (
        P("pipe", None, "dp", None, None, None, None),
        P("pipe", None, "dp", None, None, None, None),
        P("pipe", "dp"),
    )
    return jax.shard_map(body, mesh=mesh, in_specs=in_specs, out_specs=out_specs, check_vma=False)
```

```python
import functools
import math

import jax
import jax.numpy as jnp
from jax import lax
from jax.experimental import pallas as pl
from jax.experimental.pallas import tpu as pltpu
from jax.sharding import PartitionSpec as P

GROUPS = 32
UNITS = 4
FRAMES, ROWS, COLS, C = 3, 16, 8, 128
PLANE = ROWS * COLS
PIX = FRAMES * PLANE
TAPS = 9
SLAB = TAPS * C
WROWS = 3 * SLAB
HALVES = 2
PIECE = WROWS // (8 * HALVES)
MESH = pl.DeviceIdType.MESH
F32, BF16 = jnp.float32, jnp.bfloat16


def group_sum(part):
    lane = lax.broadcasted_iota(jnp.int32, part.shape, 1)
    pair = part + jnp.where(lane % 2 == 0, pltpu.roll(part, C - 1, 1), pltpu.roll(part, 1, 1))
    quad = pair + jnp.where(lane % 4 < 2, pltpu.roll(pair, C - 2, 1), pltpu.roll(pair, 2, 1))
    return jnp.sum(quad, axis=0, keepdims=True)


def fill_shifts(field, dest, clip, flip):
    col = lax.broadcasted_iota(jnp.int32, field.shape, 1)
    for col_off in range(3):
        step = (1 - col_off) if flip else (col_off - 1)
        if step == 0:
            moved = field
        elif step == 1:
            moved = jnp.where(col < COLS - 1, pltpu.roll(field, COLS - 1, 1), 0.0)
        else:
            moved = jnp.where(col > 0, pltpu.roll(field, 1, 1), 0.0)
        dest[col_off, clip, :, 1 : ROWS + 1] = moved.reshape(FRAMES, ROWS, COLS, C).astype(BF16)


def shifted(kept, tap, flip, clips=1):
    row_off, col_off = divmod(tap, 3)
    first = 2 - row_off if flip else row_off
    return kept[col_off, :clips, :, first : first + ROWS].reshape(clips * PIX, C)


def beside(parts):
    return jnp.concatenate(parts, axis=1)


def dot(lhs, rhs):
    return jnp.dot(lhs, rhs, preferred_element_type=F32)


def kernel(
    depth,
    scale,
    video,
    cot,
    w,
    gains,
    seg_out,
    grad_out,
    wg_out,
    wb,
    gbuf,
    xs,
    gs,
    xs2,
    gs2,
    acts,
    xhat_s,
    slope_s,
    rstd_s,
    shifts,
    actb,
    grdb,
    turned,
    total,
    buf1,
    got1,
    buf2,
    got2,
    buf3,
    got3,
    load_sem,
    w_send,
    w_recv,
    gain_send,
    gain_recv,
    hop_send,
    hop_recv,
    out_send,
    seg_recv,
    act_recv,
    grd_recv,
    ing_recv,
    swap_send,
    swap_recv,
    rs_send,
    rs_recv,
):
    pipe = lax.axis_index("pipe")
    dp = lax.axis_index("dp")
    half = lax.div(pipe, UNITS)
    y = lax.rem(pipe, UNITS)
    core = lax.rem(dp, 2)
    x_lo = lax.rem(lax.div(dp, 2), 2)
    z = lax.div(dp, 4)
    base = half * UNITS
    yr = lax.rem(y + 1, UNITS)
    yo = lax.rem(y + 2, UNITS)
    yl = lax.rem(y + 3, UNITS)
    other_core = dp + 1 - 2 * core
    other_x = dp + 2 - 4 * x_lo
    other_half = pipe + UNITS - 2 * base
    other_z = dp + 4 - 8 * lax.rem(z, 2)

    def dev(pipe_at, dp_at):
        return (pipe_at, dp_at)

    def z_peer(step):
        return lax.rem(z + step, depth) * 4 + lax.rem(dp, 4)

    def remote(src, dst, send, recv, target):
        return pltpu.make_async_remote_copy(
            src_ref=src, dst_ref=dst, send_sem=send, recv_sem=recv, device_id=target, device_id_type=MESH
        )

    load_w = pltpu.make_async_copy(w, wb.at[y], load_sem.at[0])
    load_w.start()
    load_gain = pltpu.make_async_copy(gains, gbuf.at[y], load_sem.at[1])
    load_gain.start()

    load_x = pltpu.make_async_copy(video.at[y], xs.at[0], load_sem.at[2])
    cot_copy = remote(cot.at[y], gs.at[UNITS], hop_send.at[2], hop_recv.at[2], dev(pipe, other_x))

    @pl.when(half == 0)
    def _():
        load_x.start()

    for row in (0, ROWS + 1):
        shifts[:, :, :, row] = jnp.zeros((3, UNITS, FRAMES, COLS, C), BF16)

    barrier = pltpu.get_barrier_semaphore()
    peers = [dev(base + at, dp) for at in (yr, yo, yl)]
    peers += [dev(pipe, other_x), dev(other_half, other_x), dev(pipe, other_core)]
    peers += [dev(pipe, z_peer(step)) for step in range(1, depth)]
    for peer in peers:
        pl.semaphore_signal(barrier, inc=1, device_id=peer, device_id_type=MESH)
    pl.semaphore_wait(barrier, len(peers))

    def gain_copy(at, slot):
        return remote(gains, gbuf.at[y], gain_send.at[slot], gain_recv.at[y], dev(base + at, dp))

    for slot, at in enumerate((yr, yo, yl)):
        gain_copy(at, slot).start()

    @pl.when(half == 1)
    def _():
        cot_copy.start()

    parity = lax.rem(x_lo + z, 2)
    qa, qb = (parity * 2 + at for at in range(2))
    pa, pb = ((1 - parity) * 2 + at for at in range(2))
    right, left, twin = dev(base + yr, dp), dev(base + yl, dp), dev(pipe, other_core)
    near_x, near_z = dev(pipe, other_x), dev(pipe, other_z)

    def place_of(quarter, part, which):
        return (quarter * 2 + which) * HALVES + part

    def rows_of(place):
        return pl.ds(pl.multiple_of(place * PIECE, PIECE), PIECE)

    def own(quarter, part, slot, target):
        place = place_of(quarter, part, core)
        rows = rows_of(place)
        return remote(w.at[rows], wb.at[y, rows], w_send.at[slot], w_recv.at[y, place], target)

    def relay(slab, quarter, part, slot, target, which=core):
        place = place_of(quarter, part, which)
        piece = wb.at[slab, rows_of(place)]
        return remote(piece, piece, w_send.at[slot], w_recv.at[slab, place], target)

    sent = []
    for quarters in ((qa, qb), (qb, qa)):
        for part in range(HALVES):
            for quarter, target in zip(quarters, (right, left)):
                copy = own(quarter, part, len(sent), target)
                copy.start()
                sent.append(copy)
    rounds = [
        [(yl, qa, (right, near_x, twin)), (yr, qb, (left, near_z, twin))],
        [(yl, qb, (near_z, twin)), (yr, qa, (near_x, twin))],
        [(yl, pa, (twin,)), (yr, pb, (twin,))],
        [(yo, qa, (near_x, twin)), (yo, qb, (near_z, twin))],
        [(yr, pa, (twin,)), (yl, pb, (twin,))],
        [(yo, pa, (twin,)), (yo, pb, (twin,))],
    ]
    for group in rounds:
        for part in range(HALVES):
            for slab, quarter, targets in group:
                relay(slab, quarter, part, 0, right).wait_recv()
                for target in targets:
                    copy = relay(slab, quarter, part, len(sent), target)
                    copy.start()
                    sent.append(copy)
    for slab in (yl, yr, yo):
        for quarter in range(4):
            for part in range(HALVES):
                relay(slab, quarter, part, 0, twin, 1 - core).wait_recv()
    load_w.wait()
    load_gain.wait()
    for slot, at in enumerate((yr, yo, yl)):
        remote(gains, gbuf.at[at], gain_send.at[slot], gain_recv.at[at], dev(base + at, dp)).wait_recv()

    def home(src, dst, slot, recv, unit):
        local = unit == y

        def away():
            return remote(src, dst.at[y], out_send.at[slot, unit], recv.at[y], dev(base + unit, dp))

        def here():
            return pltpu.make_async_copy(src, dst.at[y], out_send.at[slot, unit])

        return local, away, here

    def start_home(*args):
        local, away, here = home(*args)

        @pl.when(jnp.logical_not(local))
        def _():
            away().start()

        @pl.when(local)
        def _():
            here().start()

    def finish_home(*args):
        local, away, here = home(*args)

        @pl.when(jnp.logical_not(local))
        def _():
            away().wait_send()

        @pl.when(local)
        def _():
            here().wait()

    def arrived(dst, recv, places):
        for at in places:
            remote(dst.at[at], dst.at[at], out_send.at[0, 0], recv.at[at], near_x).wait_recv()

    def swap(src, dst, slot, unit):
        return remote(src.at[unit + 1 - slot], dst.at[unit], swap_send.at[slot, unit], swap_recv.at[slot, unit], near_x)

    hop_x = remote(xs.at[UNITS], xs.at[0], hop_send.at[0], hop_recv.at[0], dev(other_half, other_x))
    hop_g = remote(gs.at[0], gs.at[UNITS], hop_send.at[1], hop_recv.at[1], dev(other_half, other_x))

    @pl.when(half == 0)
    def _():
        load_x.wait()

    @pl.when(half == 1)
    def _():
        cot_copy.wait_recv()
        hop_x.wait_recv()

    count = 1.0 / (PIX * (C // GROUPS))

    def forward(unit, _):
        gain = gbuf[unit].reshape(1, 1, C)
        x = xs[unit].astype(F32).reshape(PIX // COLS, COLS, C)
        mean = group_sum(jnp.sum(x, axis=0)) * count
        centred = x - mean.reshape(1, 1, C)
        var = group_sum(jnp.sum(centred * centred, axis=0)) * count
        rstd = lax.rsqrt(var + 1e-06)
        xhat = centred * rstd.reshape(1, 1, C)
        normed = xhat * gain
        sig = jax.nn.sigmoid(normed)
        act = normed * sig
        acts[unit] = act.reshape(PIX, C).astype(BF16)
        fill_shifts(act, shifts, 0, False)
        xhat_s[unit] = xhat
        slope_s[unit] = (sig + act * (1.0 - sig)) * gain
        rstd_s[unit] = rstd
        lhs = beside([shifted(shifts, tap, False) for tap in range(TAPS)])
        pair = dot(lhs[: 2 * PLANE], beside([wb[unit, SLAB : 2 * SLAB], wb[unit, 2 * SLAB :]]))
        part0 = dot(lhs[:PLANE], wb[unit, :SLAB])
        part1 = pair[:, :C]
        part2 = jnp.concatenate([pair[:, C:], dot(lhs[2 * PLANE :], wb[unit, 2 * SLAB :])], axis=0)
        x = x.reshape(PIX, C)
        early = part0 + part1[:PLANE]
        branch = (early, early, part0 + part1[PLANE:])
        for frame in range(FRAMES):
            at = slice(frame * PLANE, (frame + 1) * PLANE)
            xs[unit + 1, at] = (x[at] + branch[frame] + part2[at]).astype(BF16)
        start_home(acts.at[unit], actb, 1, act_recv, unit)

        @pl.when(half == 1)
        def _():
            swap(xs, xs2, 0, unit).start()

        return 0

    lax.fori_loop(0, UNITS, forward, 0)

    def send_outputs(kept, slot, swapped, dst, recv):
        for unit in range(UNITS):

            @pl.when(half == 0)
            def _():
                start_home(kept.at[unit + 1 - slot // 3], dst, slot, recv, unit)

            @pl.when(half == 1)
            def _():
                swap(kept, swapped, slot // 3, unit).wait_recv()
                start_home(swapped.at[unit], dst, slot, recv, unit)

    def turn_acts():
        home(acts.at[y], actb, 1, act_recv, y)[2]().wait()
        arrived(actb, act_recv, (yr, yo, yl))

        def turn(clip, _):
            act = actb[clip].astype(F32)
            frames = [act[f * PLANE : (f + 1) * PLANE].T.astype(BF16) for f in range(FRAMES)]
            for frame_off in range(3):
                turned[clip, frame_off] = beside([frames[max(f - 2 + frame_off, 0)] for f in range(FRAMES)])
            return 0

        lax.fori_loop(0, UNITS, turn, 0)

    @pl.when(half == 0)
    def _():
        hop_x.start()
        turn_acts()

    @pl.when(half == 0)
    def _():
        send_outputs(xs, 0, xs2, seg_out, seg_recv)
        hop_g.wait_recv()

    def backward(step, _):
        unit = UNITS - 1 - step
        start_home(gs.at[unit + 1], grdb, 2, grd_recv, unit)
        grad = gs[unit + 1].astype(F32)
        fill_shifts(grad.reshape(PIX // COLS, COLS, C), shifts, 0, True)
        lhs = beside([shifted(shifts, tap, True) for tap in range(TAPS)])
        flat = jnp.concatenate(
            [
                beside([wb[unit, k * SLAB + tap * C : k * SLAB + (tap + 1) * C] for tap in range(TAPS)])
                for k in range(3)
            ],
            axis=0,
        )
        wide = lax.dot_general(lhs, flat, (((1,), (1,)), ((), ())), preferred_element_type=F32)
        parts = [wide[:, k * C : (k + 1) * C] for k in range(3)]
        p0, p1, p2 = ([part[f * PLANE : (f + 1) * PLANE] for f in range(3)] for part in parts)
        gact = jnp.concatenate(
            [p0[0] + p0[1] + p0[2] + p1[0] + p1[1] + p2[0], p1[2] + p2[1], p2[2]], axis=0
        )
        xhat = xhat_s[unit]
        inner = gact.reshape(PIX // COLS, COLS, C) * slope_s[unit]
        mean_a = group_sum(jnp.sum(inner, axis=0)) * count
        mean_b = group_sum(jnp.sum(inner * xhat, axis=0)) * count
        slant = (inner - mean_a.reshape(1, 1, C) - xhat * mean_b.reshape(1, 1, C)) * rstd_s[unit].reshape(
            1, 1, C
        )
        gs[unit] = (grad + slant.reshape(PIX, C)).astype(BF16)

        @pl.when(half == 1)
        def _():
            swap(gs, gs2, 1, unit).start()

        return 0

    lax.fori_loop(0, UNITS, backward, 0)

    @pl.when(half == 1)
    def _():
        hop_g.start()
        turn_acts()

    home(gs.at[y + 1], grdb, 2, grd_recv, y)[2]().wait()

    def spread(step, _):
        clip = lax.rem(y + step + (step // 2) * (5 - 2 * step), UNITS)

        @pl.when(step > 0)
        def _():
            arrived(grdb, grd_recv, (clip,))

        fill_shifts(grdb[clip].astype(F32).reshape(PIX // COLS, COLS, C), shifts, clip, True)
        return 0

    lax.fori_loop(0, UNITS, spread, 0)

    @pl.when(half == 1)
    def _():
        send_outputs(xs, 0, xs2, seg_out, seg_recv)

    lhs = beside([turned[clip].reshape(3 * C, PIX) for clip in range(UNITS)])
    for first in range(0, TAPS, 2):
        taps = range(first, min(first + 2, TAPS))
        block = dot(lhs, beside([shifted(shifts, tap, True, UNITS) for tap in taps]))
        for tap in taps:
            for frame_off in range(3):
                at = (frame_off * TAPS + tap) * C
                total[at : at + C] = block[frame_off * C : (frame_off + 1) * C, (tap - first) * C :][:, :C]

    chunk = WROWS // (4 * depth)
    for at_z in range(depth):
        for at_x in range(2):
            for at_core in range(2):
                start = (at_z * 4 + at_x * 2 + at_core) * chunk
                buf1[at_z, at_core, at_x] = total[start : start + chunk].astype(BF16)
    steps = sorted(range(depth), key=lambda step: -min(step, depth - step))
    places = [lax.rem(z + step, depth) for step in steps]

    def core_copy(at):
        return remote(buf1.at[at, 1 - core], got1.at[at], rs_send.at[0, at], rs_recv.at[0, at], twin)

    def x_copy(at):
        return remote(buf2.at[at, 1 - x_lo], got2.at[at], rs_send.at[1, at], rs_recv.at[1, at], near_x)

    def z_copy(at):
        target = dev(pipe, at * 4 + lax.rem(dp, 4))
        return remote(buf3.at[at], got3.at[z], rs_send.at[2, at], rs_recv.at[2, z], target)

    for at in places:
        core_copy(at).start()
    for at in places:
        core_copy(at).wait_recv()
        buf2[at] = (buf1[at, core].astype(F32) + got1[at].astype(F32)).astype(BF16)
        x_copy(at).start()
    send_outputs(gs, 3, gs2, grad_out, ing_recv)
    for step, at in zip(steps, places):
        x_copy(at).wait_recv()
        buf3[at] = (buf2[at, x_lo].astype(F32) + got2[at].astype(F32)).astype(BF16)
        if step:
            z_copy(at).start()
    result = buf3[z].astype(F32)
    for step in reversed(steps):
        if step:
            at = lax.rem(z + step, depth)
            remote(got3.at[at], got3.at[at], rs_send.at[2, at], rs_recv.at[2, at], twin).wait_recv()
            result = result + got3[at].astype(F32)
    wg_out[...] = result * scale

    for step, at in zip(steps, places):
        core_copy(at).wait_send()
        x_copy(at).wait_send()
        if step:
            z_copy(at).wait_send()
    for copy in sent:
        copy.wait_send()
    for slot, at in enumerate((yr, yo, yl)):
        gain_copy(at, slot).wait_send()
    for unit in range(UNITS):
        finish_home(xs2.at[unit], seg_out, 0, seg_recv, unit)
        finish_home(gs2.at[unit], grad_out, 3, ing_recv, unit)

        @pl.when(unit != y)
        def _():
            home(acts.at[unit], actb, 1, act_recv, unit)[1]().wait_send()
            home(gs.at[unit + 1], grdb, 2, grd_recv, unit)[1]().wait_send()

    @pl.when(half == 0)
    def _():
        hop_x.wait_send()

    @pl.when(half == 1)
    def _():
        cot_copy.wait_send()
        hop_g.wait_send()
        for unit in range(UNITS):
            swap(xs, xs2, 0, unit).wait_send()
            swap(gs, gs2, 1, unit).wait_send()

    arrived(seg_out, seg_recv, (yr, yo, yl))
    arrived(grad_out, ing_recv, (yr, yo, yl))


def write_results(seg, grad, share, seg_out, grad_out, share_out, flat, sem):
    copies = [
        pltpu.make_async_copy(seg, seg_out, sem.at[0]),
        pltpu.make_async_copy(grad, grad_out, sem.at[1]),
        pltpu.make_async_copy(flat, share_out, sem.at[2]),
    ]
    copies[0].start()
    copies[1].start()
    for row in range(share.shape[0]):
        flat[:, row * C : (row + 1) * C] = share[row : row + 1]
    copies[2].start()
    for copy in copies:
        copy.wait()


def body(video, cotangent, weights, gains):
    micro = video.shape[0]
    devices = lax.axis_size("dp")
    depth = devices // 4
    chunk = WROWS // devices
    scale = 1.0 / math.sqrt(micro * devices * PIX)
    clip = (PIX, C)
    any_spec = pl.BlockSpec(memory_space=pl.ANY)
    dma = pltpu.SemaphoreType.DMA
    outputs, grads_out, share = pl.pallas_call(
        functools.partial(kernel, depth, scale),
        out_shape=(
            jax.ShapeDtypeStruct((micro, *clip), BF16),
            jax.ShapeDtypeStruct((micro, *clip), BF16),
            jax.ShapeDtypeStruct((chunk, C), F32),
        ),
        in_specs=[pl.BlockSpec(memory_space=pltpu.HBM)] * 4,
        out_specs=(any_spec, any_spec, pl.BlockSpec(memory_space=pltpu.VMEM)),
        scratch_shapes=[
            pltpu.VMEM((UNITS, WROWS, C), BF16),
            pltpu.VMEM((UNITS, 1, C), F32),
            pltpu.VMEM((UNITS + 1, *clip), BF16),
            pltpu.VMEM((UNITS + 1, *clip), BF16),
            pltpu.VMEM((UNITS, *clip), BF16),
            pltpu.VMEM((UNITS, *clip), BF16),
            pltpu.VMEM((UNITS, *clip), BF16),
            pltpu.VMEM((UNITS, PIX // COLS, COLS, C), F32),
            pltpu.VMEM((UNITS, PIX // COLS, COLS, C), F32),
            pltpu.VMEM((UNITS, 1, C), F32),
            pltpu.VMEM((3, UNITS, FRAMES, ROWS + 2, COLS, C), BF16),
            pltpu.VMEM((UNITS, *clip), BF16),
            pltpu.VMEM((UNITS, *clip), BF16),
            pltpu.VMEM((UNITS, 3, C, PIX), BF16),
            pltpu.VMEM((WROWS, C), F32),
            pltpu.VMEM((depth, 2, 2, chunk, C), BF16),
            pltpu.VMEM((depth, 2, chunk, C), BF16),
            pltpu.VMEM((depth, 2, chunk, C), BF16),
            pltpu.VMEM((depth, chunk, C), BF16),
            pltpu.VMEM((depth, chunk, C), BF16),
            pltpu.VMEM((depth, chunk, C), BF16),
            dma((3,)),
            dma((24 * HALVES,)),
            dma((UNITS, 8 * HALVES)),
            dma((3,)),
            dma((UNITS,)),
            dma((3,)),
            dma((3,)),
            dma((4, UNITS)),
            dma((UNITS,)),
            dma((UNITS,)),
            dma((UNITS,)),
            dma((UNITS,)),
            dma((2, UNITS)),
            dma((2, UNITS)),
            dma((3, depth)),
            dma((3, depth)),
        ],
        compiler_params=pltpu.CompilerParams(collective_id=0, has_side_effects=True, vmem_limit_bytes=32 << 20),
    )(
        *(
            pltpu.with_memory_space_constraint(array, pltpu.HBM)
            for array in (
                video.reshape(micro, *clip),
                cotangent.reshape(micro, *clip),
                weights.reshape(WROWS, C),
                gains,
            )
        )
    )
    whole = pl.BlockSpec(memory_space=pltpu.VMEM)
    outputs, grads_out, share = pl.pallas_call(
        write_results,
        out_shape=(
            jax.ShapeDtypeStruct((micro, *clip), BF16),
            jax.ShapeDtypeStruct((micro, *clip), BF16),
            jax.ShapeDtypeStruct((1, chunk * C), F32),
        ),
        in_specs=[any_spec, any_spec, whole],
        out_specs=(pl.BlockSpec(memory_space=pltpu.HBM),) * 3,
        scratch_shapes=[pltpu.VMEM((1, chunk * C), F32), dma((3,))],
        compiler_params=pltpu.CompilerParams(vmem_limit_bytes=4 << 20),
    )(outputs, grads_out, share)
    full = (1, micro, 1, FRAMES, ROWS, COLS, C)
    return (outputs.reshape(full), grads_out.reshape(full), share)


def solution(mesh):
    in_specs = (
        P(None, "dp", None, None, None, None),
        P(None, "dp", None, None, None, None),
        P("pipe", None, None),
        P("pipe", None),
    )
    out_specs = (
        P("pipe", None, "dp", None, None, None, None),
        P("pipe", None, "dp", None, None, None, None),
        P("pipe", "dp"),
    )
    return jax.shard_map(body, mesh=mesh, in_specs=in_specs, out_specs=out_specs, check_vma=False)
```

```python
import functools
import math

import jax
import jax.numpy as jnp
from jax import lax
from jax.experimental import pallas as pl
from jax.experimental.pallas import tpu as pltpu
from jax.sharding import PartitionSpec as P

GROUPS = 32
UNITS = 4
FRAMES, ROWS, COLS, C = 3, 16, 8, 128
PLANE = ROWS * COLS
PIX = FRAMES * PLANE
TAPS = 9
SLAB = TAPS * C
WROWS = 3 * SLAB
HALVES = 2
PIECE = WROWS // (8 * HALVES)
MESH = pl.DeviceIdType.MESH
F32, BF16 = jnp.float32, jnp.bfloat16


def group_sum(part):
    lane = lax.broadcasted_iota(jnp.int32, part.shape, 1)
    pair = part + jnp.where(lane % 2 == 0, pltpu.roll(part, C - 1, 1), pltpu.roll(part, 1, 1))
    quad = pair + jnp.where(lane % 4 < 2, pltpu.roll(pair, C - 2, 1), pltpu.roll(pair, 2, 1))
    return jnp.sum(quad, axis=0, keepdims=True)


def fill_shifts(field, dest, clip, flip):
    col = lax.broadcasted_iota(jnp.int32, field.shape, 1)
    for col_off in range(3):
        step = (1 - col_off) if flip else (col_off - 1)
        if step == 0:
            moved = field
        elif step == 1:
            moved = jnp.where(col < COLS - 1, pltpu.roll(field, COLS - 1, 1), 0.0)
        else:
            moved = jnp.where(col > 0, pltpu.roll(field, 1, 1), 0.0)
        dest[col_off, clip, :, 1 : ROWS + 1] = moved.reshape(FRAMES, ROWS, COLS, C).astype(BF16)


def shifted(kept, tap, flip, clips=1):
    row_off, col_off = divmod(tap, 3)
    first = 2 - row_off if flip else row_off
    return kept[col_off, :clips, :, first : first + ROWS].reshape(clips * PIX, C)


def beside(parts):
    return jnp.concatenate(parts, axis=1)


def dot(lhs, rhs):
    return jnp.dot(lhs, rhs, preferred_element_type=F32)


def kernel(
    depth,
    scale,
    video,
    cot,
    w,
    gains,
    seg_out,
    grad_out,
    wg_out,
    wb,
    gbuf,
    xs,
    gs,
    xs2,
    gs2,
    acts,
    xhat_s,
    slope_s,
    rstd_s,
    early_s,
    shifts,
    actb,
    grdb,
    turned,
    total,
    buf1,
    got1,
    buf2,
    got2,
    buf3,
    got3,
    load_sem,
    w_send,
    w_recv,
    gain_send,
    gain_recv,
    hop_send,
    hop_recv,
    out_send,
    seg_recv,
    act_recv,
    grd_recv,
    ing_recv,
    known,
    swap_send,
    swap_recv,
    rs_send,
    rs_recv,
):
    pipe = lax.axis_index("pipe")
    dp = lax.axis_index("dp")
    half = lax.div(pipe, UNITS)
    y = lax.rem(pipe, UNITS)
    core = lax.rem(dp, 2)
    x_lo = lax.rem(lax.div(dp, 2), 2)
    z = lax.div(dp, 4)
    base = half * UNITS
    yr = lax.rem(y + 1, UNITS)
    yo = lax.rem(y + 2, UNITS)
    yl = lax.rem(y + 3, UNITS)
    other_core = dp + 1 - 2 * core
    other_x = dp + 2 - 4 * x_lo
    other_half = pipe + UNITS - 2 * base
    other_z = dp + 4 - 8 * lax.rem(z, 2)

    def dev(pipe_at, dp_at):
        return (pipe_at, dp_at)

    def z_peer(step):
        return lax.rem(z + step, depth) * 4 + lax.rem(dp, 4)

    def remote(src, dst, send, recv, target):
        return pltpu.make_async_remote_copy(
            src_ref=src, dst_ref=dst, send_sem=send, recv_sem=recv, device_id=target, device_id_type=MESH
        )

    load_w = pltpu.make_async_copy(w, wb.at[y], load_sem.at[0])
    load_w.start()
    load_gain = pltpu.make_async_copy(gains, gbuf.at[y], load_sem.at[1])
    load_gain.start()

    load_x = pltpu.make_async_copy(video.at[y], xs.at[0], load_sem.at[2])
    cot_copy = remote(cot.at[y], gs.at[UNITS], hop_send.at[2], hop_recv.at[2], dev(pipe, other_x))

    @pl.when(half == 0)
    def _():
        load_x.start()

    for row in (0, ROWS + 1):
        shifts[:, :, :, row] = jnp.zeros((3, UNITS, FRAMES, COLS, C), BF16)

    barrier = pltpu.get_barrier_semaphore()
    peers = [dev(base + at, dp) for at in (yr, yo, yl)]
    peers += [dev(pipe, other_x), dev(other_half, other_x), dev(pipe, other_core)]
    peers += [dev(pipe, z_peer(step)) for step in (1, depth - 1)]
    for peer in peers:
        pl.semaphore_signal(barrier, inc=1, device_id=peer, device_id_type=MESH)
    pl.semaphore_wait(barrier, len(peers))

    right, left, twin = dev(base + yr, dp), dev(base + yl, dp), dev(pipe, other_core)
    near_x, near_z = dev(pipe, other_x), dev(pipe, other_z)

    def home(src, dst, slot, recv, unit):
        local = unit == y

        def away():
            return remote(src, dst.at[y], out_send.at[slot, unit], recv.at[y], dev(base + unit, dp))

        def here():
            return pltpu.make_async_copy(src, dst.at[y], out_send.at[slot, unit])

        return local, away, here

    def start_home(*args):
        local, away, here = home(*args)

        @pl.when(jnp.logical_not(local))
        def _():
            away().start()

        @pl.when(local)
        def _():
            here().start()

    def finish_home(*args):
        local, away, here = home(*args)

        @pl.when(jnp.logical_not(local))
        def _():
            away().wait_send()

        @pl.when(local)
        def _():
            here().wait()

    def arrived(dst, recv, places):
        for at in places:
            remote(dst.at[at], dst.at[at], out_send.at[0, 0], recv.at[at], near_x).wait_recv()

    def swap(src, dst, slot, unit):
        return remote(src.at[unit + 1 - slot], dst.at[unit], swap_send.at[slot, unit], swap_recv.at[slot, unit], near_x)

    count = 1.0 / (PIX * (C // GROUPS))

    def normalise(unit):
        gain = gbuf[unit].reshape(1, 1, C)
        x = xs[unit].astype(F32).reshape(PIX // COLS, COLS, C)
        mean = group_sum(jnp.sum(x, axis=0)) * count
        centred = x - mean.reshape(1, 1, C)
        var = group_sum(jnp.sum(centred * centred, axis=0)) * count
        rstd = lax.rsqrt(var + 1e-06)
        xhat = centred * rstd.reshape(1, 1, C)
        normed = xhat * gain
        sig = jax.nn.sigmoid(normed)
        act = normed * sig
        acts[unit] = act.reshape(PIX, C).astype(BF16)
        fill_shifts(act, shifts, 0, False)
        xhat_s[unit] = xhat
        slope_s[unit] = (sig + act * (1.0 - sig)) * gain
        rstd_s[unit] = rstd

    def convolve(unit, fresh=True):
        if fresh:
            start_home(acts.at[unit], actb, 1, act_recv, unit)
        lhs = beside([shifted(shifts, tap, False) for tap in range(TAPS)])
        pair = dot(lhs[: 2 * PLANE], beside([wb[unit, SLAB : 2 * SLAB], wb[unit, 2 * SLAB :]]))
        part0 = dot(lhs[:PLANE], wb[unit, :SLAB])
        part1 = pair[:, :C]
        part2 = jnp.concatenate([pair[:, C:], dot(lhs[2 * PLANE :], wb[unit, 2 * SLAB :])], axis=0)
        x = xs[unit].astype(F32)
        early = part0 + part1[:PLANE]
        branch = (early, early, part0 + part1[PLANE:])
        for frame in range(FRAMES):
            at = slice(frame * PLANE, (frame + 1) * PLANE)
            xs[unit + 1, at] = (x[at] + branch[frame] + part2[at]).astype(BF16)

        @pl.when(half == 1)
        def _():
            swap(xs, xs2, 0, unit).start()

    def spread_back(unit):
        grad = gs[unit + 1].astype(F32)
        fill_shifts(grad.reshape(PIX // COLS, COLS, C), shifts, 0, True)
        lhs = beside([shifted(shifts, tap, True) for tap in range(TAPS)])
        flat = jnp.concatenate(
            [
                beside([wb[unit, k * SLAB + tap * C : k * SLAB + (tap + 1) * C] for tap in range(TAPS)])
                for k in range(3)
            ],
            axis=0,
        )
        wide = lax.dot_general(lhs, flat, (((1,), (1,)), ((), ())), preferred_element_type=F32)
        parts = [wide[:, k * C : (k + 1) * C] for k in range(3)]
        p0, p1, p2 = ([part[f * PLANE : (f + 1) * PLANE] for f in range(3)] for part in parts)
        return jnp.concatenate(
            [p0[0] + p0[1] + p0[2] + p1[0] + p1[1] + p2[0], p1[2] + p2[1], p2[2]], axis=0
        )

    def through_norm(unit, gact):
        xhat = xhat_s[unit]
        inner = gact.reshape(PIX // COLS, COLS, C) * slope_s[unit]
        mean_a = group_sum(jnp.sum(inner, axis=0)) * count
        mean_b = group_sum(jnp.sum(inner * xhat, axis=0)) * count
        slant = (inner - mean_a.reshape(1, 1, C) - xhat * mean_b.reshape(1, 1, C)) * rstd_s[unit].reshape(
            1, 1, C
        )
        gs[unit] = (gs[unit + 1].astype(F32) + slant.reshape(PIX, C)).astype(BF16)

        @pl.when(half == 1)
        def _():
            swap(gs, gs2, 1, unit).start()

    def pass_on(step):
        pl.semaphore_signal(known.at[step], inc=1, device_id=dev(pipe, z_peer(1)), device_id_type=MESH)
        pl.semaphore_wait(known.at[step], 1)

    def gain_copy(at, slot):
        return remote(gains, gbuf.at[y], gain_send.at[slot], gain_recv.at[y], dev(base + at, dp))

    for slot, at in enumerate((yr, yo, yl)):
        gain_copy(at, slot).start()

    @pl.when(half == 1)
    def _():
        cot_copy.start()

    parity = lax.rem(x_lo + z, 2)
    qa, qb = (parity * 2 + at for at in range(2))
    pa, pb = ((1 - parity) * 2 + at for at in range(2))

    def place_of(quarter, part, which):
        return (quarter * 2 + which) * HALVES + part

    def rows_of(place):
        return pl.ds(pl.multiple_of(place * PIECE, PIECE), PIECE)

    def own(quarter, part, slot, target):
        place = place_of(quarter, part, core)
        rows = rows_of(place)
        return remote(w.at[rows], wb.at[y, rows], w_send.at[slot], w_recv.at[y, place], target)

    def relay(slab, quarter, part, slot, target, which=core):
        place = place_of(quarter, part, which)
        piece = wb.at[slab, rows_of(place)]
        return remote(piece, piece, w_send.at[slot], w_recv.at[slab, place], target)

    sent = []
    for quarters in ((qa, qb), (qb, qa)):
        for part in range(HALVES):
            for quarter, target in zip(quarters, (right, left)):
                copy = own(quarter, part, len(sent), target)
                copy.start()
                sent.append(copy)
    load_gain.wait()
    for slot, at in enumerate((yr, yo, yl)):
        remote(gains, gbuf.at[at], gain_send.at[slot], gain_recv.at[at], dev(base + at, dp)).wait_recv()

    @pl.when(half == 0)
    def _():
        load_x.wait()
        normalise(0)

    rounds = [
        [(yl, qa, (right, near_x, twin)), (yr, qb, (left, near_z, twin))],
        [(yl, qb, (near_z, twin)), (yr, qa, (near_x, twin))],
        [(yl, pa, (twin,)), (yr, pb, (twin,))],
        [(yo, qa, (near_x, twin)), (yo, qb, (near_z, twin))],
        [(yr, pa, (twin,)), (yl, pb, (twin,))],
        [(yo, pa, (twin,)), (yo, pb, (twin,))],
    ]
    for group in rounds:
        for part in range(HALVES):
            for slab, quarter, targets in group:
                relay(slab, quarter, part, 0, right).wait_recv()
                for target in targets:
                    copy = relay(slab, quarter, part, len(sent), target)
                    copy.start()
                    sent.append(copy)
    for slab in (yl, yr, yo):
        for quarter in range(4):
            for part in range(HALVES):
                relay(slab, quarter, part, 0, twin, 1 - core).wait_recv()
    load_w.wait()

    hop_x = remote(xs.at[UNITS], xs.at[0], hop_send.at[0], hop_recv.at[0], dev(other_half, other_x))
    hop_g = remote(gs.at[0], gs.at[UNITS], hop_send.at[1], hop_recv.at[1], dev(other_half, other_x))

    @pl.when(half == 1)
    def _():
        cot_copy.wait_recv()
        early_s[...] = spread_back(UNITS - 1)
        for step in range(depth - 3):
            pass_on(step)
        hop_x.wait_recv()

    def forward(unit, _):
        normalise(unit)
        convolve(unit)
        return 0

    @pl.when(half == 0)
    def _():
        convolve(0)

    lax.fori_loop(1 - half, UNITS - half, forward, 0)

    @pl.when(half == 1)
    def _():
        normalise(UNITS - 1)
        start_home(acts.at[UNITS - 1], actb, 1, act_recv, UNITS - 1)


    def send_outputs(kept, slot, swapped, dst, recv):
        for unit in range(UNITS):

            @pl.when(half == 0)
            def _():
                start_home(kept.at[unit + 1 - slot // 3], dst, slot, recv, unit)

            @pl.when(half == 1)
            def _():
                swap(kept, swapped, slot // 3, unit).wait_recv()
                start_home(swapped.at[unit], dst, slot, recv, unit)

    def turn_acts():
        home(acts.at[y], actb, 1, act_recv, y)[2]().wait()
        arrived(actb, act_recv, (yr, yo, yl))

        def turn(clip, _):
            act = actb[clip].astype(F32)
            frames = [act[f * PLANE : (f + 1) * PLANE].T.astype(BF16) for f in range(FRAMES)]
            for frame_off in range(3):
                turned[clip, frame_off] = beside([frames[max(f - 2 + frame_off, 0)] for f in range(FRAMES)])
            return 0

        lax.fori_loop(0, UNITS, turn, 0)

    @pl.when(half == 0)
    def _():
        hop_x.start()
        turn_acts()

    @pl.when(half == 0)
    def _():
        send_outputs(xs, 0, xs2, seg_out, seg_recv)
        for step in range(depth - 3):
            pass_on(step)
        hop_g.wait_recv()

    def backward(step, _):
        unit = UNITS - 1 - step
        start_home(gs.at[unit + 1], grdb, 2, grd_recv, unit)
        through_norm(unit, spread_back(unit))
        return 0

    @pl.when(half == 1)
    def _():
        start_home(gs.at[UNITS], grdb, 2, grd_recv, UNITS - 1)
        through_norm(UNITS - 1, early_s[...])

    lax.fori_loop(half, UNITS, backward, 0)

    @pl.when(half == 1)
    def _():
        hop_g.start()
        fill_shifts(acts[UNITS - 1].astype(F32).reshape(PIX // COLS, COLS, C), shifts, 0, False)
        convolve(UNITS - 1, False)
        turn_acts()

    home(gs.at[y + 1], grdb, 2, grd_recv, y)[2]().wait()

    def spread(step, _):
        clip = lax.rem(y + step + (step // 2) * (5 - 2 * step), UNITS)

        @pl.when(step > 0)
        def _():
            arrived(grdb, grd_recv, (clip,))

        fill_shifts(grdb[clip].astype(F32).reshape(PIX // COLS, COLS, C), shifts, clip, True)
        return 0

    lax.fori_loop(0, UNITS, spread, 0)

    @pl.when(half == 1)
    def _():
        send_outputs(xs, 0, xs2, seg_out, seg_recv)

    lhs = beside([turned[clip].reshape(3 * C, PIX) for clip in range(UNITS)])
    for first in range(0, TAPS, 2):
        taps = range(first, min(first + 2, TAPS))
        block = dot(lhs, beside([shifted(shifts, tap, True, UNITS) for tap in taps]))
        for tap in taps:
            for frame_off in range(3):
                at = (frame_off * TAPS + tap) * C
                total[at : at + C] = block[frame_off * C : (frame_off + 1) * C, (tap - first) * C :][:, :C]

    chunk = WROWS // (4 * depth)
    for at_z in range(depth):
        for at_x in range(2):
            for at_core in range(2):
                start = (at_z * 4 + at_x * 2 + at_core) * chunk
                buf1[at_z, at_core, at_x] = total[start : start + chunk].astype(BF16)
    steps = sorted(range(depth), key=lambda step: -min(step, depth - step))
    places = [lax.rem(z + step, depth) for step in steps]

    def core_copy(at):
        return remote(buf1.at[at, 1 - core], got1.at[at], rs_send.at[0, at], rs_recv.at[0, at], twin)

    def x_copy(at):
        return remote(buf2.at[at, 1 - x_lo], got2.at[at], rs_send.at[1, at], rs_recv.at[1, at], near_x)

    def z_copy(at):
        target = dev(pipe, at * 4 + lax.rem(dp, 4))
        return remote(buf3.at[at], got3.at[z], rs_send.at[2, at], rs_recv.at[2, z], target)

    for at in places:
        core_copy(at).start()
    for at in places:
        core_copy(at).wait_recv()
        buf2[at] = (buf1[at, core].astype(F32) + got1[at].astype(F32)).astype(BF16)
        x_copy(at).start()
    send_outputs(gs, 3, gs2, grad_out, ing_recv)
    for step, at in zip(steps, places):
        x_copy(at).wait_recv()
        buf3[at] = (buf2[at, x_lo].astype(F32) + got2[at].astype(F32)).astype(BF16)
        if step:
            z_copy(at).start()
    result = buf3[z].astype(F32)
    for step in reversed(steps):
        if step:
            at = lax.rem(z + step, depth)
            remote(got3.at[at], got3.at[at], rs_send.at[2, at], rs_recv.at[2, at], twin).wait_recv()
            result = result + got3[at].astype(F32)
    wg_out[...] = result * scale

    for step, at in zip(steps, places):
        core_copy(at).wait_send()
        x_copy(at).wait_send()
        if step:
            z_copy(at).wait_send()
    for copy in sent:
        copy.wait_send()
    for slot, at in enumerate((yr, yo, yl)):
        gain_copy(at, slot).wait_send()
    for unit in range(UNITS):
        finish_home(xs2.at[unit], seg_out, 0, seg_recv, unit)
        finish_home(gs2.at[unit], grad_out, 3, ing_recv, unit)

        @pl.when(unit != y)
        def _():
            home(acts.at[unit], actb, 1, act_recv, unit)[1]().wait_send()
            home(gs.at[unit + 1], grdb, 2, grd_recv, unit)[1]().wait_send()

    @pl.when(half == 0)
    def _():
        hop_x.wait_send()

    @pl.when(half == 1)
    def _():
        cot_copy.wait_send()
        hop_g.wait_send()
        for unit in range(UNITS):
            swap(xs, xs2, 0, unit).wait_send()
            swap(gs, gs2, 1, unit).wait_send()

    arrived(seg_out, seg_recv, (yr, yo, yl))
    arrived(grad_out, ing_recv, (yr, yo, yl))


def write_results(seg, grad, share, seg_out, grad_out, share_out, flat, sem):
    copies = [
        pltpu.make_async_copy(seg, seg_out, sem.at[0]),
        pltpu.make_async_copy(grad, grad_out, sem.at[1]),
        pltpu.make_async_copy(flat, share_out, sem.at[2]),
    ]
    copies[0].start()
    copies[1].start()
    for row in range(share.shape[0]):
        flat[:, row * C : (row + 1) * C] = share[row : row + 1]
    copies[2].start()
    for copy in copies:
        copy.wait()


def body(video, cotangent, weights, gains):
    micro = video.shape[0]
    devices = lax.axis_size("dp")
    depth = devices // 4
    chunk = WROWS // devices
    scale = 1.0 / math.sqrt(micro * devices * PIX)
    clip = (PIX, C)
    any_spec = pl.BlockSpec(memory_space=pl.ANY)
    dma = pltpu.SemaphoreType.DMA
    outputs, grads_out, share = pl.pallas_call(
        functools.partial(kernel, depth, scale),
        out_shape=(
            jax.ShapeDtypeStruct((micro, *clip), BF16),
            jax.ShapeDtypeStruct((micro, *clip), BF16),
            jax.ShapeDtypeStruct((chunk, C), F32),
        ),
        in_specs=[pl.BlockSpec(memory_space=pltpu.HBM)] * 4,
        out_specs=(any_spec, any_spec, pl.BlockSpec(memory_space=pltpu.VMEM)),
        scratch_shapes=[
            pltpu.VMEM((UNITS, WROWS, C), BF16),
            pltpu.VMEM((UNITS, 1, C), F32),
            pltpu.VMEM((UNITS + 1, *clip), BF16),
            pltpu.VMEM((UNITS + 1, *clip), BF16),
            pltpu.VMEM((UNITS, *clip), BF16),
            pltpu.VMEM((UNITS, *clip), BF16),
            pltpu.VMEM((UNITS, *clip), BF16),
            pltpu.VMEM((UNITS, PIX // COLS, COLS, C), F32),
            pltpu.VMEM((UNITS, PIX // COLS, COLS, C), F32),
            pltpu.VMEM((UNITS, 1, C), F32),
            pltpu.VMEM(clip, F32),
            pltpu.VMEM((3, UNITS, FRAMES, ROWS + 2, COLS, C), BF16),
            pltpu.VMEM((UNITS, *clip), BF16),
            pltpu.VMEM((UNITS, *clip), BF16),
            pltpu.VMEM((UNITS, 3, C, PIX), BF16),
            pltpu.VMEM((WROWS, C), F32),
            pltpu.VMEM((depth, 2, 2, chunk, C), BF16),
            pltpu.VMEM((depth, 2, chunk, C), BF16),
            pltpu.VMEM((depth, 2, chunk, C), BF16),
            pltpu.VMEM((depth, chunk, C), BF16),
            pltpu.VMEM((depth, chunk, C), BF16),
            pltpu.VMEM((depth, chunk, C), BF16),
            dma((3,)),
            dma((24 * HALVES,)),
            dma((UNITS, 8 * HALVES)),
            dma((3,)),
            dma((UNITS,)),
            dma((3,)),
            dma((3,)),
            dma((4, UNITS)),
            dma((UNITS,)),
            dma((UNITS,)),
            dma((UNITS,)),
            dma((UNITS,)),
            pltpu.SemaphoreType.REGULAR((depth - 3,)),
            dma((2, UNITS)),
            dma((2, UNITS)),
            dma((3, depth)),
            dma((3, depth)),
        ],
        compiler_params=pltpu.CompilerParams(collective_id=0, has_side_effects=True, vmem_limit_bytes=32 << 20),
    )(
        *(
            pltpu.with_memory_space_constraint(array, pltpu.HBM)
            for array in (
                video.reshape(micro, *clip),
                cotangent.reshape(micro, *clip),
                weights.reshape(WROWS, C),
                gains,
            )
        )
    )
    whole = pl.BlockSpec(memory_space=pltpu.VMEM)
    outputs, grads_out, share = pl.pallas_call(
        write_results,
        out_shape=(
            jax.ShapeDtypeStruct((micro, *clip), BF16),
            jax.ShapeDtypeStruct((micro, *clip), BF16),
            jax.ShapeDtypeStruct((1, chunk * C), F32),
        ),
        in_specs=[any_spec, any_spec, whole],
        out_specs=(pl.BlockSpec(memory_space=pltpu.HBM),) * 3,
        scratch_shapes=[pltpu.VMEM((1, chunk * C), F32), dma((3,))],
        compiler_params=pltpu.CompilerParams(vmem_limit_bytes=4 << 20),
    )(outputs, grads_out, share)
    full = (1, micro, 1, FRAMES, ROWS, COLS, C)
    return (outputs.reshape(full), grads_out.reshape(full), share)


def solution(mesh):
    in_specs = (
        P(None, "dp", None, None, None, None),
        P(None, "dp", None, None, None, None),
        P("pipe", None, None),
        P("pipe", None),
    )
    out_specs = (
        P("pipe", None, "dp", None, None, None, None),
        P("pipe", None, "dp", None, None, None, None),
        P("pipe", "dp"),
    )
    return jax.shard_map(body, mesh=mesh, in_specs=in_specs, out_specs=out_specs, check_vma=False)
```

```python
import functools
import math

import jax
import jax.numpy as jnp
from jax import lax
from jax.experimental import pallas as pl
from jax.experimental.pallas import tpu as pltpu
from jax.sharding import PartitionSpec as P

GROUPS = 32
UNITS = 4
FRAMES, ROWS, COLS, C = 3, 16, 8, 128
PLANE = ROWS * COLS
PIX = FRAMES * PLANE
TAPS = 9
SLAB = TAPS * C
WROWS = 3 * SLAB
HALVES = 2
PIECE = WROWS // (8 * HALVES)
MESH = pl.DeviceIdType.MESH
F32, BF16 = jnp.float32, jnp.bfloat16


def group_sum(part):
    lane = lax.broadcasted_iota(jnp.int32, part.shape, 1)
    pair = part + jnp.where(lane % 2 == 0, pltpu.roll(part, C - 1, 1), pltpu.roll(part, 1, 1))
    quad = pair + jnp.where(lane % 4 < 2, pltpu.roll(pair, C - 2, 1), pltpu.roll(pair, 2, 1))
    return jnp.sum(quad, axis=0, keepdims=True)


def fill_shifts(field, dest, clip, flip):
    col = lax.broadcasted_iota(jnp.int32, field.shape, 1)
    for col_off in range(3):
        step = (1 - col_off) if flip else (col_off - 1)
        if step == 0:
            moved = field
        elif step == 1:
            moved = jnp.where(col < COLS - 1, pltpu.roll(field, COLS - 1, 1), 0.0)
        else:
            moved = jnp.where(col > 0, pltpu.roll(field, 1, 1), 0.0)
        dest[col_off, clip, :, 1 : ROWS + 1] = moved.reshape(FRAMES, ROWS, COLS, C).astype(BF16)


def shifted(kept, tap, flip, clips=1):
    row_off, col_off = divmod(tap, 3)
    first = 2 - row_off if flip else row_off
    return kept[col_off, :clips, :, first : first + ROWS].reshape(clips * PIX, C)


def beside(parts):
    return jnp.concatenate(parts, axis=1)


def dot(lhs, rhs):
    return jnp.dot(lhs, rhs, preferred_element_type=F32)


def kernel(
    depth,
    scale,
    video,
    cot,
    w,
    gains,
    seg_out,
    grad_out,
    wg_out,
    wb,
    gbuf,
    xs,
    gs,
    xs2,
    gs2,
    acts,
    xhat_s,
    slope_s,
    rstd_s,
    early_s,
    shifts,
    actb,
    grdb,
    turned,
    total,
    buf1,
    got1,
    buf2,
    got2,
    buf3,
    got3,
    load_sem,
    w_send,
    w_recv,
    gain_send,
    gain_recv,
    hop_send,
    hop_recv,
    out_send,
    seg_recv,
    act_recv,
    grd_recv,
    ing_recv,
    known,
    swap_send,
    swap_recv,
    rs_send,
    rs_recv,
):
    pipe = lax.axis_index("pipe")
    dp = lax.axis_index("dp")
    half = lax.div(pipe, UNITS)
    y = lax.rem(pipe, UNITS)
    core = lax.rem(dp, 2)
    x_lo = lax.rem(lax.div(dp, 2), 2)
    z = lax.div(dp, 4)
    base = half * UNITS
    yr = lax.rem(y + 1, UNITS)
    yo = lax.rem(y + 2, UNITS)
    yl = lax.rem(y + 3, UNITS)
    other_core = dp + 1 - 2 * core
    other_x = dp + 2 - 4 * x_lo
    other_half = pipe + UNITS - 2 * base
    other_z = dp + 4 - 8 * lax.rem(z, 2)

    def dev(pipe_at, dp_at):
        return (pipe_at, dp_at)

    def z_peer(step):
        return lax.rem(z + step, depth) * 4 + lax.rem(dp, 4)

    def remote(src, dst, send, recv, target):
        return pltpu.make_async_remote_copy(
            src_ref=src, dst_ref=dst, send_sem=send, recv_sem=recv, device_id=target, device_id_type=MESH
        )

    load_w = pltpu.make_async_copy(w, wb.at[y], load_sem.at[0])
    load_w.start()
    load_gain = pltpu.make_async_copy(gains, gbuf.at[y], load_sem.at[1])
    load_gain.start()

    load_x = pltpu.make_async_copy(video.at[y], xs.at[0], load_sem.at[2])
    cot_copy = remote(cot.at[y], gs.at[UNITS], hop_send.at[2], hop_recv.at[2], dev(pipe, other_x))

    @pl.when(half == 0)
    def _():
        load_x.start()

    for row in (0, ROWS + 1):
        shifts[:, :, :, row] = jnp.zeros((3, UNITS, FRAMES, COLS, C), BF16)

    barrier = pltpu.get_barrier_semaphore()
    peers = [dev(base + at, dp) for at in (yr, yo, yl)]
    peers += [dev(pipe, other_x), dev(other_half, other_x), dev(pipe, other_core)]
    peers += [dev(pipe, z_peer(step)) for step in (1, depth - 1)]
    for peer in peers:
        pl.semaphore_signal(barrier, inc=1, device_id=peer, device_id_type=MESH)
    pl.semaphore_wait(barrier, len(peers))

    right, left, twin = dev(base + yr, dp), dev(base + yl, dp), dev(pipe, other_core)
    near_x, near_z = dev(pipe, other_x), dev(pipe, other_z)

    def home(src, dst, slot, recv, unit):
        local = unit == y

        def away():
            return remote(src, dst.at[y], out_send.at[slot, unit], recv.at[y], dev(base + unit, dp))

        def here():
            return pltpu.make_async_copy(src, dst.at[y], out_send.at[slot, unit])

        return local, away, here

    def start_home(*args):
        local, away, here = home(*args)

        @pl.when(jnp.logical_not(local))
        def _():
            away().start()

        @pl.when(local)
        def _():
            here().start()

    def finish_home(*args):
        local, away, here = home(*args)

        @pl.when(jnp.logical_not(local))
        def _():
            away().wait_send()

        @pl.when(local)
        def _():
            here().wait()

    def arrived(dst, recv, places):
        for at in places:
            remote(dst.at[at], dst.at[at], out_send.at[0, 0], recv.at[at], near_x).wait_recv()

    def swap(src, dst, slot, unit):
        return remote(src.at[unit + 1 - slot], dst.at[unit], swap_send.at[slot, unit], swap_recv.at[slot, unit], near_x)

    count = 1.0 / (PIX * (C // GROUPS))

    def normalise(unit):
        gain = gbuf[unit].reshape(1, 1, C)
        x = xs[unit].astype(F32).reshape(PIX // COLS, COLS, C)
        mean = group_sum(jnp.sum(x, axis=0)) * count
        centred = x - mean.reshape(1, 1, C)
        var = group_sum(jnp.sum(centred * centred, axis=0)) * count
        rstd = lax.rsqrt(var + 1e-06)
        xhat = centred * rstd.reshape(1, 1, C)
        normed = xhat * gain
        sig = jax.nn.sigmoid(normed)
        act = normed * sig
        acts[unit] = act.reshape(PIX, C).astype(BF16)
        fill_shifts(act, shifts, 0, False)
        xhat_s[unit] = xhat
        slope_s[unit] = (sig + act * (1.0 - sig)) * gain
        rstd_s[unit] = rstd

    def convolve(unit, fresh=True):
        if fresh:
            start_home(acts.at[unit], actb, 1, act_recv, unit)
        lhs = beside([shifted(shifts, tap, False) for tap in range(TAPS)])
        pair = dot(lhs[: 2 * PLANE], beside([wb[unit, SLAB : 2 * SLAB], wb[unit, 2 * SLAB :]]))
        part0 = dot(lhs[:PLANE], wb[unit, :SLAB])
        part1 = pair[:, :C]
        part2 = jnp.concatenate([pair[:, C:], dot(lhs[2 * PLANE :], wb[unit, 2 * SLAB :])], axis=0)
        x = xs[unit].astype(F32)
        early = part0 + part1[:PLANE]
        branch = (early, early, part0 + part1[PLANE:])
        for frame in range(FRAMES):
            at = slice(frame * PLANE, (frame + 1) * PLANE)
            xs[unit + 1, at] = (x[at] + branch[frame] + part2[at]).astype(BF16)

        @pl.when(half == 1)
        def _():
            swap(xs, xs2, 0, unit).start()

    def spread_back(unit):
        grad = gs[unit + 1].astype(F32)
        fill_shifts(grad.reshape(PIX // COLS, COLS, C), shifts, 0, True)
        lhs = beside([shifted(shifts, tap, True) for tap in range(TAPS)])
        flat = jnp.concatenate(
            [
                beside([wb[unit, k * SLAB + tap * C : k * SLAB + (tap + 1) * C] for tap in range(TAPS)])
                for k in range(3)
            ],
            axis=0,
        )
        wide = lax.dot_general(lhs, flat, (((1,), (1,)), ((), ())), preferred_element_type=F32)
        parts = [wide[:, k * C : (k + 1) * C] for k in range(3)]
        p0, p1, p2 = ([part[f * PLANE : (f + 1) * PLANE] for f in range(3)] for part in parts)
        return jnp.concatenate(
            [p0[0] + p0[1] + p0[2] + p1[0] + p1[1] + p2[0], p1[2] + p2[1], p2[2]], axis=0
        )

    def through_norm(unit, gact):
        xhat = xhat_s[unit]
        inner = gact.reshape(PIX // COLS, COLS, C) * slope_s[unit]
        mean_a = group_sum(jnp.sum(inner, axis=0)) * count
        mean_b = group_sum(jnp.sum(inner * xhat, axis=0)) * count
        slant = (inner - mean_a.reshape(1, 1, C) - xhat * mean_b.reshape(1, 1, C)) * rstd_s[unit].reshape(
            1, 1, C
        )
        gs[unit] = (gs[unit + 1].astype(F32) + slant.reshape(PIX, C)).astype(BF16)

        @pl.when(half == 1)
        def _():
            swap(gs, gs2, 1, unit).start()

    def pass_on(step):
        pl.semaphore_signal(known.at[step], inc=1, device_id=dev(pipe, z_peer(1)), device_id_type=MESH)
        pl.semaphore_wait(known.at[step], 1)

    def gain_copy(at, slot):
        return remote(gains, gbuf.at[y], gain_send.at[slot], gain_recv.at[y], dev(base + at, dp))

    for slot, at in enumerate((yr, yo, yl)):
        gain_copy(at, slot).start()

    @pl.when(half == 1)
    def _():
        cot_copy.start()

    parity = lax.rem(x_lo + z, 2)
    qa, qb = (parity * 2 + at for at in range(2))
    pa, pb = ((1 - parity) * 2 + at for at in range(2))

    def place_of(quarter, part, which):
        return (quarter * 2 + which) * HALVES + part

    def rows_of(place):
        return pl.ds(pl.multiple_of(place * PIECE, PIECE), PIECE)

    def own(quarter, part, slot, target):
        place = place_of(quarter, part, core)
        rows = rows_of(place)
        return remote(w.at[rows], wb.at[y, rows], w_send.at[slot], w_recv.at[y, place], target)

    def relay(slab, quarter, part, slot, target, which=core):
        place = place_of(quarter, part, which)
        piece = wb.at[slab, rows_of(place)]
        return remote(piece, piece, w_send.at[slot], w_recv.at[slab, place], target)

    sent = []
    for quarters in ((qa, qb), (qb, qa)):
        for part in range(HALVES):
            for quarter, target in zip(quarters, (right, left)):
                copy = own(quarter, part, len(sent), target)
                copy.start()
                sent.append(copy)
    load_gain.wait()
    for slot, at in enumerate((yr, yo, yl)):
        remote(gains, gbuf.at[at], gain_send.at[slot], gain_recv.at[at], dev(base + at, dp)).wait_recv()

    @pl.when(half == 0)
    def _():
        load_x.wait()
        normalise(0)

    rounds = [
        [(yl, qa, (right, near_x, twin)), (yr, qb, (left, near_z, twin))],
        [(yl, qb, (near_z, twin)), (yr, qa, (near_x, twin))],
        [(yl, pa, (twin,)), (yr, pb, (twin,))],
        [(yo, qa, (near_x, twin)), (yo, qb, (near_z, twin))],
        [(yr, pa, (twin,)), (yl, pb, (twin,))],
        [(yo, pa, (twin,)), (yo, pb, (twin,))],
    ]
    for group in rounds:
        for part in range(HALVES):
            for slab, quarter, targets in group:
                relay(slab, quarter, part, 0, right).wait_recv()
                for target in targets:
                    copy = relay(slab, quarter, part, len(sent), target)
                    copy.start()
                    sent.append(copy)
    for slab in (yl, yr, yo):
        for quarter in range(4):
            for part in range(HALVES):
                relay(slab, quarter, part, 0, twin, 1 - core).wait_recv()
    load_w.wait()

    hop_x = remote(xs.at[UNITS], xs.at[0], hop_send.at[0], hop_recv.at[0], dev(other_half, other_x))
    hop_g = remote(gs.at[0], gs.at[UNITS], hop_send.at[1], hop_recv.at[1], dev(other_half, other_x))

    @pl.when(half == 1)
    def _():
        cot_copy.wait_recv()
        early_s[...] = spread_back(UNITS - 1)
        for step in range(depth - 3):
            pass_on(step)
        hop_x.wait_recv()

    def forward(unit, _):
        normalise(unit)
        convolve(unit)
        return 0

    @pl.when(half == 0)
    def _():
        convolve(0)

    lax.fori_loop(1 - half, UNITS - half, forward, 0)

    @pl.when(half == 1)
    def _():
        normalise(UNITS - 1)
        start_home(acts.at[UNITS - 1], actb, 1, act_recv, UNITS - 1)


    def send_outputs(kept, slot, swapped, dst, recv):
        for unit in range(UNITS):

            @pl.when(half == 0)
            def _():
                start_home(kept.at[unit + 1 - slot // 3], dst, slot, recv, unit)

            @pl.when(half == 1)
            def _():
                swap(kept, swapped, slot // 3, unit).wait_recv()
                start_home(swapped.at[unit], dst, slot, recv, unit)

    def turn_acts():
        home(acts.at[y], actb, 1, act_recv, y)[2]().wait()
        arrived(actb, act_recv, (yr, yo, yl))

        def turn(clip, _):
            act = actb[clip].astype(F32)
            frames = [act[f * PLANE : (f + 1) * PLANE].T.astype(BF16) for f in range(FRAMES)]
            for frame_off in range(3):
                turned[clip, frame_off] = beside([frames[max(f - 2 + frame_off, 0)] for f in range(FRAMES)])
            return 0

        lax.fori_loop(0, UNITS, turn, 0)

    @pl.when(half == 0)
    def _():
        hop_x.start()
        turn_acts()

    @pl.when(half == 0)
    def _():
        send_outputs(xs, 0, xs2, seg_out, seg_recv)
        for step in range(depth - 3):
            pass_on(step)
        hop_g.wait_recv()

    def backward(step, _):
        unit = UNITS - 1 - step
        start_home(gs.at[unit + 1], grdb, 2, grd_recv, unit)
        through_norm(unit, spread_back(unit))
        return 0

    @pl.when(half == 1)
    def _():
        start_home(gs.at[UNITS], grdb, 2, grd_recv, UNITS - 1)
        through_norm(UNITS - 1, early_s[...])

    lax.fori_loop(half, UNITS, backward, 0)

    @pl.when(half == 1)
    def _():
        hop_g.start()
        fill_shifts(acts[UNITS - 1].astype(F32).reshape(PIX // COLS, COLS, C), shifts, 0, False)
        convolve(UNITS - 1, False)
        turn_acts()

    home(gs.at[y + 1], grdb, 2, grd_recv, y)[2]().wait()

    def spread(step, _):
        clip = lax.rem(y + step + (step // 2) * (5 - 2 * step), UNITS)

        @pl.when(step > 0)
        def _():
            arrived(grdb, grd_recv, (clip,))

        fill_shifts(grdb[clip].astype(F32).reshape(PIX // COLS, COLS, C), shifts, clip, True)
        return 0

    lax.fori_loop(0, UNITS, spread, 0)

    lhs = beside([turned[clip].reshape(3 * C, PIX) for clip in range(UNITS)])
    for first in range(0, TAPS, 2):
        taps = range(first, min(first + 2, TAPS))
        block = dot(lhs, beside([shifted(shifts, tap, True, UNITS) for tap in taps]))
        for tap in taps:
            for frame_off in range(3):
                at = (frame_off * TAPS + tap) * C
                total[at : at + C] = block[frame_off * C : (frame_off + 1) * C, (tap - first) * C :][:, :C]

    chunk = WROWS // (4 * depth)

    def core_copy(at):
        return remote(buf1.at[at, 1 - core], got1.at[at], rs_send.at[0, at], rs_recv.at[0, at], twin)

    for at_z in range(depth):
        for at_x in range(2):
            for at_core in range(2):
                start = (at_z * 4 + at_x * 2 + at_core) * chunk
                buf1[at_z, at_core, at_x] = total[start : start + chunk].astype(BF16)
        core_copy(at_z).start()
    steps = sorted(range(depth), key=lambda step: -min(step, depth - step))
    places = [lax.rem(z + step, depth) for step in steps]

    def x_copy(at):
        return remote(buf2.at[at, 1 - x_lo], got2.at[at], rs_send.at[1, at], rs_recv.at[1, at], near_x)

    def z_copy(at):
        target = dev(pipe, at * 4 + lax.rem(dp, 4))
        return remote(buf3.at[at], got3.at[z], rs_send.at[2, at], rs_recv.at[2, z], target)

    for at in places:
        core_copy(at).wait_recv()
        buf2[at] = (buf1[at, core].astype(F32) + got1[at].astype(F32)).astype(BF16)
        x_copy(at).start()

    @pl.when(half == 1)
    def _():
        send_outputs(xs, 0, xs2, seg_out, seg_recv)

    send_outputs(gs, 3, gs2, grad_out, ing_recv)
    for step, at in zip(steps, places):
        x_copy(at).wait_recv()
        buf3[at] = (buf2[at, x_lo].astype(F32) + got2[at].astype(F32)).astype(BF16)
        if step:
            z_copy(at).start()
    result = buf3[z].astype(F32)
    for step in reversed(steps):
        if step:
            at = lax.rem(z + step, depth)
            remote(got3.at[at], got3.at[at], rs_send.at[2, at], rs_recv.at[2, at], twin).wait_recv()
            result = result + got3[at].astype(F32)
    wg_out[...] = result * scale

    for step, at in zip(steps, places):
        core_copy(at).wait_send()
        x_copy(at).wait_send()
        if step:
            z_copy(at).wait_send()
    for copy in sent:
        copy.wait_send()
    for slot, at in enumerate((yr, yo, yl)):
        gain_copy(at, slot).wait_send()
    for unit in range(UNITS):
        finish_home(xs2.at[unit], seg_out, 0, seg_recv, unit)
        finish_home(gs2.at[unit], grad_out, 3, ing_recv, unit)

        @pl.when(unit != y)
        def _():
            home(acts.at[unit], actb, 1, act_recv, unit)[1]().wait_send()
            home(gs.at[unit + 1], grdb, 2, grd_recv, unit)[1]().wait_send()

    @pl.when(half == 0)
    def _():
        hop_x.wait_send()

    @pl.when(half == 1)
    def _():
        cot_copy.wait_send()
        hop_g.wait_send()
        for unit in range(UNITS):
            swap(xs, xs2, 0, unit).wait_send()
            swap(gs, gs2, 1, unit).wait_send()

    arrived(seg_out, seg_recv, (yr, yo, yl))
    arrived(grad_out, ing_recv, (yr, yo, yl))


def write_results(seg, grad, share, seg_out, grad_out, share_out, flat, sem):
    copies = [
        pltpu.make_async_copy(seg, seg_out, sem.at[0]),
        pltpu.make_async_copy(grad, grad_out, sem.at[1]),
        pltpu.make_async_copy(flat, share_out, sem.at[2]),
    ]
    copies[0].start()
    copies[1].start()
    for row in range(share.shape[0]):
        flat[:, row * C : (row + 1) * C] = share[row : row + 1]
    copies[2].start()
    for copy in copies:
        copy.wait()


def body(video, cotangent, weights, gains):
    micro = video.shape[0]
    devices = lax.axis_size("dp")
    depth = devices // 4
    chunk = WROWS // devices
    scale = 1.0 / math.sqrt(micro * devices * PIX)
    clip = (PIX, C)
    any_spec = pl.BlockSpec(memory_space=pl.ANY)
    dma = pltpu.SemaphoreType.DMA
    outputs, grads_out, share = pl.pallas_call(
        functools.partial(kernel, depth, scale),
        out_shape=(
            jax.ShapeDtypeStruct((micro, *clip), BF16),
            jax.ShapeDtypeStruct((micro, *clip), BF16),
            jax.ShapeDtypeStruct((chunk, C), F32),
        ),
        in_specs=[pl.BlockSpec(memory_space=pltpu.HBM)] * 4,
        out_specs=(any_spec, any_spec, pl.BlockSpec(memory_space=pltpu.VMEM)),
        scratch_shapes=[
            pltpu.VMEM((UNITS, WROWS, C), BF16),
            pltpu.VMEM((UNITS, 1, C), F32),
            pltpu.VMEM((UNITS + 1, *clip), BF16),
            pltpu.VMEM((UNITS + 1, *clip), BF16),
            pltpu.VMEM((UNITS, *clip), BF16),
            pltpu.VMEM((UNITS, *clip), BF16),
            pltpu.VMEM((UNITS, *clip), BF16),
            pltpu.VMEM((UNITS, PIX // COLS, COLS, C), F32),
            pltpu.VMEM((UNITS, PIX // COLS, COLS, C), F32),
            pltpu.VMEM((UNITS, 1, C), F32),
            pltpu.VMEM(clip, F32),
            pltpu.VMEM((3, UNITS, FRAMES, ROWS + 2, COLS, C), BF16),
            pltpu.VMEM((UNITS, *clip), BF16),
            pltpu.VMEM((UNITS, *clip), BF16),
            pltpu.VMEM((UNITS, 3, C, PIX), BF16),
            pltpu.VMEM((WROWS, C), F32),
            pltpu.VMEM((depth, 2, 2, chunk, C), BF16),
            pltpu.VMEM((depth, 2, chunk, C), BF16),
            pltpu.VMEM((depth, 2, chunk, C), BF16),
            pltpu.VMEM((depth, chunk, C), BF16),
            pltpu.VMEM((depth, chunk, C), BF16),
            pltpu.VMEM((depth, chunk, C), BF16),
            dma((3,)),
            dma((24 * HALVES,)),
            dma((UNITS, 8 * HALVES)),
            dma((3,)),
            dma((UNITS,)),
            dma((3,)),
            dma((3,)),
            dma((4, UNITS)),
            dma((UNITS,)),
            dma((UNITS,)),
            dma((UNITS,)),
            dma((UNITS,)),
            pltpu.SemaphoreType.REGULAR((depth - 3,)),
            dma((2, UNITS)),
            dma((2, UNITS)),
            dma((3, depth)),
            dma((3, depth)),
        ],
        compiler_params=pltpu.CompilerParams(collective_id=0, has_side_effects=True, vmem_limit_bytes=32 << 20),
    )(
        *(
            pltpu.with_memory_space_constraint(array, pltpu.HBM)
            for array in (
                video.reshape(micro, *clip),
                cotangent.reshape(micro, *clip),
                weights.reshape(WROWS, C),
                gains,
            )
        )
    )
    whole = pl.BlockSpec(memory_space=pltpu.VMEM)
    outputs, grads_out, share = pl.pallas_call(
        write_results,
        out_shape=(
            jax.ShapeDtypeStruct((micro, *clip), BF16),
            jax.ShapeDtypeStruct((micro, *clip), BF16),
            jax.ShapeDtypeStruct((1, chunk * C), F32),
        ),
        in_specs=[any_spec, any_spec, whole],
        out_specs=(pl.BlockSpec(memory_space=pltpu.HBM),) * 3,
        scratch_shapes=[pltpu.VMEM((1, chunk * C), F32), dma((3,))],
        compiler_params=pltpu.CompilerParams(vmem_limit_bytes=4 << 20),
    )(outputs, grads_out, share)
    full = (1, micro, 1, FRAMES, ROWS, COLS, C)
    return (outputs.reshape(full), grads_out.reshape(full), share)


def solution(mesh):
    in_specs = (
        P(None, "dp", None, None, None, None),
        P(None, "dp", None, None, None, None),
        P("pipe", None, None),
        P("pipe", None),
    )
    out_specs = (
        P("pipe", None, "dp", None, None, None, None),
        P("pipe", None, "dp", None, None, None, None),
        P("pipe", "dp"),
    )
    return jax.shard_map(body, mesh=mesh, in_specs=in_specs, out_specs=out_specs, check_vma=False)
```

```python
import functools
import math

import jax
import jax.numpy as jnp
from jax import lax
from jax.experimental import pallas as pl
from jax.experimental.pallas import tpu as pltpu
from jax.sharding import PartitionSpec as P

GROUPS = 32
UNITS = 4
FRAMES, ROWS, COLS, C = 3, 16, 8, 128
PLANE = ROWS * COLS
PIX = FRAMES * PLANE
TAPS = 9
SLAB = TAPS * C
WROWS = 3 * SLAB
HALVES = 2
PIECE = WROWS // (8 * HALVES)
MESH = pl.DeviceIdType.MESH
F32, BF16 = jnp.float32, jnp.bfloat16


def group_sum(part):
    lane = lax.broadcasted_iota(jnp.int32, part.shape, 1)
    pair = part + jnp.where(lane % 2 == 0, pltpu.roll(part, C - 1, 1), pltpu.roll(part, 1, 1))
    quad = pair + jnp.where(lane % 4 < 2, pltpu.roll(pair, C - 2, 1), pltpu.roll(pair, 2, 1))
    return jnp.sum(quad, axis=0, keepdims=True)


def fill_shifts(field, dest, clip, flip):
    col = lax.broadcasted_iota(jnp.int32, field.shape, 1)
    for col_off in range(3):
        step = (1 - col_off) if flip else (col_off - 1)
        if step == 0:
            moved = field
        elif step == 1:
            moved = jnp.where(col < COLS - 1, pltpu.roll(field, COLS - 1, 1), 0.0)
        else:
            moved = jnp.where(col > 0, pltpu.roll(field, 1, 1), 0.0)
        dest[col_off, clip, :, 1 : ROWS + 1] = moved.reshape(FRAMES, ROWS, COLS, C).astype(BF16)


def shifted(kept, tap, flip, clips=1):
    row_off, col_off = divmod(tap, 3)
    first = 2 - row_off if flip else row_off
    return kept[col_off, :clips, :, first : first + ROWS].reshape(clips * PIX, C)


def beside(parts):
    return jnp.concatenate(parts, axis=1)


def dot(lhs, rhs):
    return jnp.dot(lhs, rhs, preferred_element_type=F32)


def kernel(
    depth,
    scale,
    video,
    cot,
    w,
    gains,
    seg_out,
    grad_out,
    wg_out,
    wb,
    gbuf,
    xs,
    gs,
    xs2,
    gs2,
    acts,
    xhat_s,
    slope_s,
    rstd_s,
    early_s,
    shifts,
    actb,
    grdb,
    turned,
    total,
    buf1,
    got1,
    buf2,
    got2,
    buf3,
    got3,
    load_sem,
    w_send,
    w_recv,
    gain_send,
    gain_recv,
    hop_send,
    hop_recv,
    out_send,
    seg_recv,
    act_recv,
    grd_recv,
    ing_recv,
    known,
    swap_send,
    swap_recv,
    rs_send,
    rs_recv,
):
    pipe = lax.axis_index("pipe")
    dp = lax.axis_index("dp")
    half = lax.div(pipe, UNITS)
    y = lax.rem(pipe, UNITS)
    core = lax.rem(dp, 2)
    x_lo = lax.rem(lax.div(dp, 2), 2)
    z = lax.div(dp, 4)
    base = half * UNITS
    yr = lax.rem(y + 1, UNITS)
    yo = lax.rem(y + 2, UNITS)
    yl = lax.rem(y + 3, UNITS)
    other_core = dp + 1 - 2 * core
    other_x = dp + 2 - 4 * x_lo
    other_half = pipe + UNITS - 2 * base
    other_z = dp + 4 - 8 * lax.rem(z, 2)

    def dev(pipe_at, dp_at):
        return (pipe_at, dp_at)

    def z_peer(step):
        return lax.rem(z + step, depth) * 4 + lax.rem(dp, 4)

    def remote(src, dst, send, recv, target):
        return pltpu.make_async_remote_copy(
            src_ref=src, dst_ref=dst, send_sem=send, recv_sem=recv, device_id=target, device_id_type=MESH
        )

    load_w = pltpu.make_async_copy(w, wb.at[y], load_sem.at[0])
    load_w.start()
    load_gain = pltpu.make_async_copy(gains, gbuf.at[y], load_sem.at[1])
    load_gain.start()

    load_x = pltpu.make_async_copy(video.at[y], xs.at[0], load_sem.at[2])
    cot_copy = remote(cot.at[y], gs.at[UNITS], hop_send.at[2], hop_recv.at[2], dev(pipe, other_x))

    @pl.when(half == 0)
    def _():
        load_x.start()

    for row in (0, ROWS + 1):
        shifts[:, :, :, row] = jnp.zeros((3, UNITS, FRAMES, COLS, C), BF16)

    barrier = pltpu.get_barrier_semaphore()
    peers = [dev(base + at, dp) for at in (yr, yo, yl)]
    peers += [dev(pipe, other_x), dev(other_half, other_x), dev(pipe, other_core)]
    peers += [dev(pipe, z_peer(step)) for step in (1, depth - 1)]
    for peer in peers:
        pl.semaphore_signal(barrier, inc=1, device_id=peer, device_id_type=MESH)
    load_w.wait()
    load_gain.wait()
    pl.semaphore_wait(barrier, len(peers))

    right, left, twin = dev(base + yr, dp), dev(base + yl, dp), dev(pipe, other_core)
    near_x, near_z = dev(pipe, other_x), dev(pipe, other_z)

    def home(src, dst, slot, recv, unit):
        local = unit == y

        def away():
            return remote(src, dst.at[y], out_send.at[slot, unit], recv.at[y], dev(base + unit, dp))

        def here():
            return pltpu.make_async_copy(src, dst.at[y], out_send.at[slot, unit])

        return local, away, here

    def start_home(*args):
        local, away, here = home(*args)

        @pl.when(jnp.logical_not(local))
        def _():
            away().start()

        @pl.when(local)
        def _():
            here().start()

    def finish_home(*args):
        local, away, here = home(*args)

        @pl.when(jnp.logical_not(local))
        def _():
            away().wait_send()

        @pl.when(local)
        def _():
            here().wait()

    def arrived(dst, recv, places):
        for at in places:
            remote(dst.at[at], dst.at[at], out_send.at[0, 0], recv.at[at], near_x).wait_recv()

    def swap(src, dst, slot, unit):
        return remote(src.at[unit + 1 - slot], dst.at[unit], swap_send.at[slot, unit], swap_recv.at[slot, unit], near_x)

    count = 1.0 / (PIX * (C // GROUPS))

    def normalise(unit):
        gain = gbuf[unit].reshape(1, 1, C)
        x = xs[unit].astype(F32).reshape(PIX // COLS, COLS, C)
        mean = group_sum(jnp.sum(x, axis=0)) * count
        centred = x - mean.reshape(1, 1, C)
        var = group_sum(jnp.sum(centred * centred, axis=0)) * count
        rstd = lax.rsqrt(var + 1e-06)
        xhat = centred * rstd.reshape(1, 1, C)
        normed = xhat * gain
        sig = jax.nn.sigmoid(normed)
        act = normed * sig
        acts[unit] = act.reshape(PIX, C).astype(BF16)
        fill_shifts(act, shifts, 0, False)
        xhat_s[unit] = xhat
        slope_s[unit] = (sig + act * (1.0 - sig)) * gain
        rstd_s[unit] = rstd

    def convolve(unit, fresh=True):
        if fresh:
            start_home(acts.at[unit], actb, 1, act_recv, unit)
        lhs = beside([shifted(shifts, tap, False) for tap in range(TAPS)])
        pair = dot(lhs[: 2 * PLANE], beside([wb[unit, SLAB : 2 * SLAB], wb[unit, 2 * SLAB :]]))
        part0 = dot(lhs[:PLANE], wb[unit, :SLAB])
        part1 = pair[:, :C]
        part2 = jnp.concatenate([pair[:, C:], dot(lhs[2 * PLANE :], wb[unit, 2 * SLAB :])], axis=0)
        x = xs[unit].astype(F32)
        early = part0 + part1[:PLANE]
        branch = (early, early, part0 + part1[PLANE:])
        for frame in range(FRAMES):
            at = slice(frame * PLANE, (frame + 1) * PLANE)
            xs[unit + 1, at] = (x[at] + branch[frame] + part2[at]).astype(BF16)

        @pl.when(half == 1)
        def _():
            swap(xs, xs2, 0, unit).start()

    def spread_back(unit):
        grad = gs[unit + 1].astype(F32)
        fill_shifts(grad.reshape(PIX // COLS, COLS, C), shifts, 0, True)
        lhs = beside([shifted(shifts, tap, True) for tap in range(TAPS)])
        flat = jnp.concatenate(
            [
                beside([wb[unit, k * SLAB + tap * C : k * SLAB + (tap + 1) * C] for tap in range(TAPS)])
                for k in range(3)
            ],
            axis=0,
        )
        wide = lax.dot_general(lhs, flat, (((1,), (1,)), ((), ())), preferred_element_type=F32)
        parts = [wide[:, k * C : (k + 1) * C] for k in range(3)]
        p0, p1, p2 = ([part[f * PLANE : (f + 1) * PLANE] for f in range(3)] for part in parts)
        return jnp.concatenate(
            [p0[0] + p0[1] + p0[2] + p1[0] + p1[1] + p2[0], p1[2] + p2[1], p2[2]], axis=0
        )

    def through_norm(unit, gact):
        xhat = xhat_s[unit]
        inner = gact.reshape(PIX // COLS, COLS, C) * slope_s[unit]
        mean_a = group_sum(jnp.sum(inner, axis=0)) * count
        mean_b = group_sum(jnp.sum(inner * xhat, axis=0)) * count
        slant = (inner - mean_a.reshape(1, 1, C) - xhat * mean_b.reshape(1, 1, C)) * rstd_s[unit].reshape(
            1, 1, C
        )
        gs[unit] = (gs[unit + 1].astype(F32) + slant.reshape(PIX, C)).astype(BF16)

        @pl.when(half == 1)
        def _():
            swap(gs, gs2, 1, unit).start()

    def pass_on(step):
        pl.semaphore_signal(known.at[step], inc=1, device_id=dev(pipe, z_peer(1)), device_id_type=MESH)
        pl.semaphore_wait(known.at[step], 1)

    def gain_copy(at, slot):
        return remote(gbuf.at[y], gbuf.at[y], gain_send.at[slot], gain_recv.at[y], dev(base + at, dp))

    for slot, at in enumerate((yr, yo, yl)):
        gain_copy(at, slot).start()

    @pl.when(half == 1)
    def _():
        cot_copy.start()

    parity = lax.rem(x_lo + z, 2)
    qa, qb = (parity * 2 + at for at in range(2))
    pa, pb = ((1 - parity) * 2 + at for at in range(2))

    def place_of(quarter, part, which):
        return (quarter * 2 + which) * HALVES + part

    def rows_of(place):
        return pl.ds(pl.multiple_of(place * PIECE, PIECE), PIECE)

    def own(quarter, part, slot, target):
        place = place_of(quarter, part, core)
        rows = rows_of(place)
        return remote(wb.at[y, rows], wb.at[y, rows], w_send.at[slot], w_recv.at[y, place], target)

    def relay(slab, quarter, part, slot, target, which=core):
        place = place_of(quarter, part, which)
        piece = wb.at[slab, rows_of(place)]
        return remote(piece, piece, w_send.at[slot], w_recv.at[slab, place], target)

    sent = []
    for quarters in ((qa, qb), (qb, qa)):
        for part in range(HALVES):
            for quarter, target in zip(quarters, (right, left)):
                copy = own(quarter, part, len(sent), target)
                copy.start()
                sent.append(copy)
    for slot, at in enumerate((yr, yo, yl)):
        remote(gains, gbuf.at[at], gain_send.at[slot], gain_recv.at[at], dev(base + at, dp)).wait_recv()

    @pl.when(half == 0)
    def _():
        load_x.wait()
        normalise(0)

    rounds = [
        [(yl, qa, (right, near_x, twin)), (yr, qb, (left, near_z, twin))],
        [(yl, qb, (near_z, twin)), (yr, qa, (near_x, twin))],
        [(yl, pa, (twin,)), (yr, pb, (twin,))],
        [(yo, qa, (near_x, twin)), (yo, qb, (near_z, twin))],
        [(yr, pa, (twin,)), (yl, pb, (twin,))],
        [(yo, pa, (twin,)), (yo, pb, (twin,))],
    ]
    for group in rounds:
        for part in range(HALVES):
            for slab, quarter, targets in group:
                relay(slab, quarter, part, 0, right).wait_recv()
                for target in targets:
                    copy = relay(slab, quarter, part, len(sent), target)
                    copy.start()
                    sent.append(copy)
    for slab in (yl, yr, yo):
        for quarter in range(4):
            for part in range(HALVES):
                relay(slab, quarter, part, 0, twin, 1 - core).wait_recv()

    hop_x = remote(xs.at[UNITS], xs.at[0], hop_send.at[0], hop_recv.at[0], dev(other_half, other_x))
    hop_g = remote(gs.at[0], gs.at[UNITS], hop_send.at[1], hop_recv.at[1], dev(other_half, other_x))

    @pl.when(half == 1)
    def _():
        cot_copy.wait_recv()
        early_s[...] = spread_back(UNITS - 1)
        for step in range(depth - 3):
            pass_on(step)
        hop_x.wait_recv()

    def forward(unit, _):
        normalise(unit)
        convolve(unit)
        return 0

    @pl.when(half == 0)
    def _():
        convolve(0)

    lax.fori_loop(1 - half, UNITS - half, forward, 0)

    @pl.when(half == 1)
    def _():
        normalise(UNITS - 1)
        start_home(acts.at[UNITS - 1], actb, 1, act_recv, UNITS - 1)


    def send_outputs(kept, slot, swapped, dst, recv):
        for unit in range(UNITS):

            @pl.when(half == 0)
            def _():
                start_home(kept.at[unit + 1 - slot // 3], dst, slot, recv, unit)

            @pl.when(half == 1)
            def _():
                swap(kept, swapped, slot // 3, unit).wait_recv()
                start_home(swapped.at[unit], dst, slot, recv, unit)

    def turn_acts():
        home(acts.at[y], actb, 1, act_recv, y)[2]().wait()
        arrived(actb, act_recv, (yr, yo, yl))

        def turn(clip, _):
            act = actb[clip].astype(F32)
            frames = [act[f * PLANE : (f + 1) * PLANE].T.astype(BF16) for f in range(FRAMES)]
            for frame_off in range(3):
                turned[clip, frame_off] = beside([frames[max(f - 2 + frame_off, 0)] for f in range(FRAMES)])
            return 0

        lax.fori_loop(0, UNITS, turn, 0)

    @pl.when(half == 0)
    def _():
        hop_x.start()
        turn_acts()

    @pl.when(half == 0)
    def _():
        send_outputs(xs, 0, xs2, seg_out, seg_recv)
        for step in range(depth - 3):
            pass_on(step)
        hop_g.wait_recv()

    def backward(step, _):
        unit = UNITS - 1 - step
        start_home(gs.at[unit + 1], grdb, 2, grd_recv, unit)
        through_norm(unit, spread_back(unit))
        return 0

    @pl.when(half == 1)
    def _():
        start_home(gs.at[UNITS], grdb, 2, grd_recv, UNITS - 1)
        through_norm(UNITS - 1, early_s[...])

    lax.fori_loop(half, UNITS, backward, 0)

    @pl.when(half == 1)
    def _():
        hop_g.start()
        fill_shifts(acts[UNITS - 1].astype(F32).reshape(PIX // COLS, COLS, C), shifts, 0, False)
        convolve(UNITS - 1, False)
        turn_acts()

    home(gs.at[y + 1], grdb, 2, grd_recv, y)[2]().wait()

    def spread(step, _):
        clip = lax.rem(y + step + (step // 2) * (5 - 2 * step), UNITS)

        @pl.when(step > 0)
        def _():
            arrived(grdb, grd_recv, (clip,))

        fill_shifts(grdb[clip].astype(F32).reshape(PIX // COLS, COLS, C), shifts, clip, True)
        return 0

    lax.fori_loop(0, UNITS, spread, 0)

    lhs = beside([turned[clip].reshape(3 * C, PIX) for clip in range(UNITS)])
    for first in range(0, TAPS, 2):
        taps = range(first, min(first + 2, TAPS))
        block = dot(lhs, beside([shifted(shifts, tap, True, UNITS) for tap in taps]))
        for tap in taps:
            for frame_off in range(3):
                at = (frame_off * TAPS + tap) * C
                total[at : at + C] = block[frame_off * C : (frame_off + 1) * C, (tap - first) * C :][:, :C]

    chunk = WROWS // (4 * depth)

    def core_copy(at):
        return remote(buf1.at[at, 1 - core], got1.at[at], rs_send.at[0, at], rs_recv.at[0, at], twin)

    for at_z in range(depth):
        for at_x in range(2):
            for at_core in range(2):
                start = (at_z * 4 + at_x * 2 + at_core) * chunk
                buf1[at_z, at_core, at_x] = total[start : start + chunk].astype(BF16)
        core_copy(at_z).start()
    steps = sorted(range(depth), key=lambda step: -min(step, depth - step))
    places = [lax.rem(z + step, depth) for step in steps]

    def x_copy(at):
        return remote(buf2.at[at, 1 - x_lo], got2.at[at], rs_send.at[1, at], rs_recv.at[1, at], near_x)

    def z_copy(at):
        target = dev(pipe, at * 4 + lax.rem(dp, 4))
        return remote(buf3.at[at], got3.at[z], rs_send.at[2, at], rs_recv.at[2, z], target)

    for at in places:
        core_copy(at).wait_recv()
        buf2[at] = (buf1[at, core].astype(F32) + got1[at].astype(F32)).astype(BF16)
        x_copy(at).start()

    @pl.when(half == 1)
    def _():
        send_outputs(xs, 0, xs2, seg_out, seg_recv)

    send_outputs(gs, 3, gs2, grad_out, ing_recv)
    for step, at in zip(steps, places):
        x_copy(at).wait_recv()
        buf3[at] = (buf2[at, x_lo].astype(F32) + got2[at].astype(F32)).astype(BF16)
        if step:
            z_copy(at).start()
    result = buf3[z].astype(F32)
    for step in reversed(steps):
        if step:
            at = lax.rem(z + step, depth)
            remote(got3.at[at], got3.at[at], rs_send.at[2, at], rs_recv.at[2, at], twin).wait_recv()
            result = result + got3[at].astype(F32)
    wg_out[...] = result * scale

    for step, at in zip(steps, places):
        core_copy(at).wait_send()
        x_copy(at).wait_send()
        if step:
            z_copy(at).wait_send()
    for copy in sent:
        copy.wait_send()
    for slot, at in enumerate((yr, yo, yl)):
        gain_copy(at, slot).wait_send()
    for unit in range(UNITS):
        finish_home(xs2.at[unit], seg_out, 0, seg_recv, unit)
        finish_home(gs2.at[unit], grad_out, 3, ing_recv, unit)

        @pl.when(unit != y)
        def _():
            home(acts.at[unit], actb, 1, act_recv, unit)[1]().wait_send()
            home(gs.at[unit + 1], grdb, 2, grd_recv, unit)[1]().wait_send()

    @pl.when(half == 0)
    def _():
        hop_x.wait_send()

    @pl.when(half == 1)
    def _():
        cot_copy.wait_send()
        hop_g.wait_send()
        for unit in range(UNITS):
            swap(xs, xs2, 0, unit).wait_send()
            swap(gs, gs2, 1, unit).wait_send()

    arrived(seg_out, seg_recv, (yr, yo, yl))
    arrived(grad_out, ing_recv, (yr, yo, yl))


def write_results(seg, grad, share, seg_out, grad_out, share_out, flat, sem):
    copies = [
        pltpu.make_async_copy(seg, seg_out, sem.at[0]),
        pltpu.make_async_copy(grad, grad_out, sem.at[1]),
        pltpu.make_async_copy(flat, share_out, sem.at[2]),
    ]
    copies[0].start()
    copies[1].start()
    for row in range(share.shape[0]):
        flat[:, row * C : (row + 1) * C] = share[row : row + 1]
    copies[2].start()
    for copy in copies:
        copy.wait()


def body(video, cotangent, weights, gains):
    micro = video.shape[0]
    devices = lax.axis_size("dp")
    depth = devices // 4
    chunk = WROWS // devices
    scale = 1.0 / math.sqrt(micro * devices * PIX)
    clip = (PIX, C)
    any_spec = pl.BlockSpec(memory_space=pl.ANY)
    dma = pltpu.SemaphoreType.DMA
    outputs, grads_out, share = pl.pallas_call(
        functools.partial(kernel, depth, scale),
        out_shape=(
            jax.ShapeDtypeStruct((micro, *clip), BF16),
            jax.ShapeDtypeStruct((micro, *clip), BF16),
            jax.ShapeDtypeStruct((chunk, C), F32),
        ),
        in_specs=[pl.BlockSpec(memory_space=pltpu.HBM)] * 4,
        out_specs=(any_spec, any_spec, pl.BlockSpec(memory_space=pltpu.VMEM)),
        scratch_shapes=[
            pltpu.VMEM((UNITS, WROWS, C), BF16),
            pltpu.VMEM((UNITS, 1, C), F32),
            pltpu.VMEM((UNITS + 1, *clip), BF16),
            pltpu.VMEM((UNITS + 1, *clip), BF16),
            pltpu.VMEM((UNITS, *clip), BF16),
            pltpu.VMEM((UNITS, *clip), BF16),
            pltpu.VMEM((UNITS, *clip), BF16),
            pltpu.VMEM((UNITS, PIX // COLS, COLS, C), F32),
            pltpu.VMEM((UNITS, PIX // COLS, COLS, C), F32),
            pltpu.VMEM((UNITS, 1, C), F32),
            pltpu.VMEM(clip, F32),
            pltpu.VMEM((3, UNITS, FRAMES, ROWS + 2, COLS, C), BF16),
            pltpu.VMEM((UNITS, *clip), BF16),
            pltpu.VMEM((UNITS, *clip), BF16),
            pltpu.VMEM((UNITS, 3, C, PIX), BF16),
            pltpu.VMEM((WROWS, C), F32),
            pltpu.VMEM((depth, 2, 2, chunk, C), BF16),
            pltpu.VMEM((depth, 2, chunk, C), BF16),
            pltpu.VMEM((depth, 2, chunk, C), BF16),
            pltpu.VMEM((depth, chunk, C), BF16),
            pltpu.VMEM((depth, chunk, C), BF16),
            pltpu.VMEM((depth, chunk, C), BF16),
            dma((3,)),
            dma((24 * HALVES,)),
            dma((UNITS, 8 * HALVES)),
            dma((3,)),
            dma((UNITS,)),
            dma((3,)),
            dma((3,)),
            dma((4, UNITS)),
            dma((UNITS,)),
            dma((UNITS,)),
            dma((UNITS,)),
            dma((UNITS,)),
            pltpu.SemaphoreType.REGULAR((depth - 3,)),
            dma((2, UNITS)),
            dma((2, UNITS)),
            dma((3, depth)),
            dma((3, depth)),
        ],
        compiler_params=pltpu.CompilerParams(collective_id=0, has_side_effects=True, vmem_limit_bytes=32 << 20),
    )(
        *(
            pltpu.with_memory_space_constraint(array, pltpu.HBM)
            for array in (
                video.reshape(micro, *clip),
                cotangent.reshape(micro, *clip),
                weights.reshape(WROWS, C),
                gains,
            )
        )
    )
    whole = pl.BlockSpec(memory_space=pltpu.VMEM)
    outputs, grads_out, share = pl.pallas_call(
        write_results,
        out_shape=(
            jax.ShapeDtypeStruct((micro, *clip), BF16),
            jax.ShapeDtypeStruct((micro, *clip), BF16),
            jax.ShapeDtypeStruct((1, chunk * C), F32),
        ),
        in_specs=[any_spec, any_spec, whole],
        out_specs=(pl.BlockSpec(memory_space=pltpu.HBM),) * 3,
        scratch_shapes=[pltpu.VMEM((1, chunk * C), F32), dma((3,))],
        compiler_params=pltpu.CompilerParams(vmem_limit_bytes=4 << 20),
    )(outputs, grads_out, share)
    full = (1, micro, 1, FRAMES, ROWS, COLS, C)
    return (outputs.reshape(full), grads_out.reshape(full), share)


def solution(mesh):
    in_specs = (
        P(None, "dp", None, None, None, None),
        P(None, "dp", None, None, None, None),
        P("pipe", None, None),
        P("pipe", None),
    )
    out_specs = (
        P("pipe", None, "dp", None, None, None, None),
        P("pipe", None, "dp", None, None, None, None),
        P("pipe", "dp"),
    )
    return jax.shard_map(body, mesh=mesh, in_specs=in_specs, out_specs=out_specs, check_vma=False)
```

```python
import functools
import math

import jax
import jax.numpy as jnp
from jax import lax
from jax.experimental import pallas as pl
from jax.experimental.pallas import tpu as pltpu
from jax.sharding import PartitionSpec as P

GROUPS = 32
UNITS = 4
FRAMES, ROWS, COLS, C = 3, 16, 8, 128
PLANE = ROWS * COLS
PIX = FRAMES * PLANE
TAPS = 9
SLAB = TAPS * C
WROWS = 3 * SLAB
HALVES = 2
PIECE = WROWS // (8 * HALVES)
MESH = pl.DeviceIdType.MESH
F32, BF16 = jnp.float32, jnp.bfloat16


def group_sum(part):
    lane = lax.broadcasted_iota(jnp.int32, part.shape, 1)
    pair = part + jnp.where(lane % 2 == 0, pltpu.roll(part, C - 1, 1), pltpu.roll(part, 1, 1))
    quad = pair + jnp.where(lane % 4 < 2, pltpu.roll(pair, C - 2, 1), pltpu.roll(pair, 2, 1))
    return jnp.sum(quad, axis=0, keepdims=True)


def fill_shifts(field, dest, clip, flip):
    col = lax.broadcasted_iota(jnp.int32, field.shape, 1)
    for col_off in range(3):
        step = (1 - col_off) if flip else (col_off - 1)
        if step == 0:
            moved = field
        elif step == 1:
            moved = jnp.where(col < COLS - 1, pltpu.roll(field, COLS - 1, 1), 0.0)
        else:
            moved = jnp.where(col > 0, pltpu.roll(field, 1, 1), 0.0)
        dest[col_off, clip, :, 1 : ROWS + 1] = moved.reshape(FRAMES, ROWS, COLS, C).astype(BF16)


def shifted(kept, tap, flip, clips=1):
    row_off, col_off = divmod(tap, 3)
    first = 2 - row_off if flip else row_off
    return kept[col_off, :clips, :, first : first + ROWS].reshape(clips * PIX, C)


def beside(parts):
    return jnp.concatenate(parts, axis=1)


def dot(lhs, rhs):
    return jnp.dot(lhs, rhs, preferred_element_type=F32)


def kernel(
    depth,
    scale,
    video,
    cot,
    w,
    gains,
    seg_out,
    grad_out,
    wg_out,
    wb,
    gbuf,
    xs,
    gs,
    xs2,
    gs2,
    acts,
    xhat_s,
    slope_s,
    rstd_s,
    early_s,
    shifts,
    actb,
    grdb,
    turned,
    total,
    buf1,
    got1,
    buf2,
    got2,
    buf3,
    got3,
    load_sem,
    w_send,
    w_recv,
    gain_send,
    gain_recv,
    hop_send,
    hop_recv,
    out_send,
    seg_recv,
    act_recv,
    grd_recv,
    ing_recv,
    known,
    swap_send,
    swap_recv,
    rs_send,
    rs_recv,
):
    pipe = lax.axis_index("pipe")
    dp = lax.axis_index("dp")
    half = lax.div(pipe, UNITS)
    y = lax.rem(pipe, UNITS)
    core = lax.rem(dp, 2)
    x_lo = lax.rem(lax.div(dp, 2), 2)
    z = lax.div(dp, 4)
    base = half * UNITS
    yr = lax.rem(y + 1, UNITS)
    yo = lax.rem(y + 2, UNITS)
    yl = lax.rem(y + 3, UNITS)
    other_core = dp + 1 - 2 * core
    other_x = dp + 2 - 4 * x_lo
    other_half = pipe + UNITS - 2 * base
    other_z = dp + 4 - 8 * lax.rem(z, 2)

    def dev(pipe_at, dp_at):
        return (pipe_at, dp_at)

    def z_peer(step):
        return lax.rem(z + step, depth) * 4 + lax.rem(dp, 4)

    def remote(src, dst, send, recv, target):
        return pltpu.make_async_remote_copy(
            src_ref=src, dst_ref=dst, send_sem=send, recv_sem=recv, device_id=target, device_id_type=MESH
        )

    load_w = pltpu.make_async_copy(w, wb.at[y], load_sem.at[0])
    load_w.start()
    load_gain = pltpu.make_async_copy(gains, gbuf.at[y], load_sem.at[1])
    load_gain.start()

    load_x = pltpu.make_async_copy(video.at[y], xs.at[0], load_sem.at[2])
    cot_copy = remote(cot.at[y], gs.at[UNITS], hop_send.at[2], hop_recv.at[2], dev(pipe, other_x))

    @pl.when(half == 0)
    def _():
        load_x.start()

    for row in (0, ROWS + 1):
        shifts[:, :, :, row] = jnp.zeros((3, UNITS, FRAMES, COLS, C), BF16)

    barrier = pltpu.get_barrier_semaphore()
    peers = [dev(base + at, dp) for at in (yr, yo, yl)]
    peers += [dev(pipe, other_x), dev(other_half, other_x), dev(pipe, other_core)]
    peers += [dev(pipe, z_peer(step)) for step in (1, depth - 1)]
    for peer in peers:
        pl.semaphore_signal(barrier, inc=1, device_id=peer, device_id_type=MESH)
    load_w.wait()
    load_gain.wait()
    pl.semaphore_wait(barrier, len(peers))

    right, left, twin = dev(base + yr, dp), dev(base + yl, dp), dev(pipe, other_core)
    near_x, near_z = dev(pipe, other_x), dev(pipe, other_z)

    def home(src, dst, slot, recv, unit):
        local = unit == y

        def away():
            return remote(src, dst.at[y], out_send.at[slot, unit], recv.at[y], dev(base + unit, dp))

        def here():
            return pltpu.make_async_copy(src, dst.at[y], out_send.at[slot, unit])

        return local, away, here

    def start_home(*args):
        local, away, here = home(*args)

        @pl.when(jnp.logical_not(local))
        def _():
            away().start()

        @pl.when(local)
        def _():
            here().start()

    def finish_home(*args):
        local, away, here = home(*args)

        @pl.when(jnp.logical_not(local))
        def _():
            away().wait_send()

        @pl.when(local)
        def _():
            here().wait()

    def arrived(dst, recv, places):
        for at in places:
            remote(dst.at[at], dst.at[at], out_send.at[0, 0], recv.at[at], near_x).wait_recv()

    def swap(src, dst, slot, unit):
        return remote(src.at[unit + 1 - slot], dst.at[unit], swap_send.at[slot, unit], swap_recv.at[slot, unit], near_x)

    count = 1.0 / (PIX * (C // GROUPS))

    def normalise(unit):
        gain = gbuf[unit].reshape(1, 1, C)
        x = xs[unit].astype(F32).reshape(PIX // COLS, COLS, C)
        mean = group_sum(jnp.sum(x, axis=0)) * count
        centred = x - mean.reshape(1, 1, C)
        var = group_sum(jnp.sum(centred * centred, axis=0)) * count
        rstd = lax.rsqrt(var + 1e-06)
        xhat = centred * rstd.reshape(1, 1, C)
        normed = xhat * gain
        sig = jax.nn.sigmoid(normed)
        act = normed * sig
        acts[unit] = act.reshape(PIX, C).astype(BF16)
        fill_shifts(act, shifts, 0, False)
        xhat_s[unit] = xhat
        slope_s[unit] = (sig + act * (1.0 - sig)) * gain
        rstd_s[unit] = rstd

    def convolve(unit, fresh=True):
        if fresh:
            start_home(acts.at[unit], actb, 1, act_recv, unit)
        lhs = beside([shifted(shifts, tap, False) for tap in range(TAPS)])
        pair = dot(lhs[: 2 * PLANE], beside([wb[unit, SLAB : 2 * SLAB], wb[unit, 2 * SLAB :]]))
        part0 = dot(lhs[:PLANE], wb[unit, :SLAB])
        part1 = pair[:, :C]
        part2 = jnp.concatenate([pair[:, C:], dot(lhs[2 * PLANE :], wb[unit, 2 * SLAB :])], axis=0)
        x = xs[unit].astype(F32)
        early = part0 + part1[:PLANE]
        branch = (early, early, part0 + part1[PLANE:])
        for frame in range(FRAMES):
            at = slice(frame * PLANE, (frame + 1) * PLANE)
            xs[unit + 1, at] = (x[at] + branch[frame] + part2[at]).astype(BF16)

        @pl.when(half == 1)
        def _():
            swap(xs, xs2, 0, unit).start()

    def spread_back(unit):
        grad = gs[unit + 1].astype(F32)
        fill_shifts(grad.reshape(PIX // COLS, COLS, C), shifts, 0, True)
        lhs = beside([shifted(shifts, tap, True) for tap in range(TAPS)])
        flat = jnp.concatenate(
            [
                beside([wb[unit, k * SLAB + tap * C : k * SLAB + (tap + 1) * C] for tap in range(TAPS)])
                for k in range(3)
            ],
            axis=0,
        )
        wide = lax.dot_general(lhs, flat, (((1,), (1,)), ((), ())), preferred_element_type=F32)
        parts = [wide[:, k * C : (k + 1) * C] for k in range(3)]
        p0, p1, p2 = ([part[f * PLANE : (f + 1) * PLANE] for f in range(3)] for part in parts)
        return jnp.concatenate(
            [p0[0] + p0[1] + p0[2] + p1[0] + p1[1] + p2[0], p1[2] + p2[1], p2[2]], axis=0
        )

    def through_norm(unit, gact):
        xhat = xhat_s[unit]
        inner = gact.reshape(PIX // COLS, COLS, C) * slope_s[unit]
        mean_a = group_sum(jnp.sum(inner, axis=0)) * count
        mean_b = group_sum(jnp.sum(inner * xhat, axis=0)) * count
        slant = (inner - mean_a.reshape(1, 1, C) - xhat * mean_b.reshape(1, 1, C)) * rstd_s[unit].reshape(
            1, 1, C
        )
        gs[unit] = (gs[unit + 1].astype(F32) + slant.reshape(PIX, C)).astype(BF16)

        @pl.when(half == 1)
        def _():
            swap(gs, gs2, 1, unit).start()

    def pass_on(step):
        pl.semaphore_signal(known.at[step], inc=1, device_id=dev(pipe, z_peer(1)), device_id_type=MESH)
        pl.semaphore_wait(known.at[step], 1)

    def gain_copy(at, slot):
        return remote(gbuf.at[y], gbuf.at[y], gain_send.at[slot], gain_recv.at[y], dev(base + at, dp))

    for slot, at in enumerate((yr, yo, yl)):
        gain_copy(at, slot).start()

    @pl.when(half == 1)
    def _():
        cot_copy.start()

    parity = lax.rem(x_lo + z, 2)
    qa, qb = (parity * 2 + at for at in range(2))
    pa, pb = ((1 - parity) * 2 + at for at in range(2))

    def place_of(quarter, part, which):
        return (quarter * 2 + which) * HALVES + part

    def rows_of(place):
        return pl.ds(pl.multiple_of(place * PIECE, PIECE), PIECE)

    def own(quarter, part, slot, target):
        place = place_of(quarter, part, core)
        rows = rows_of(place)
        return remote(wb.at[y, rows], wb.at[y, rows], w_send.at[slot], w_recv.at[y, place], target)

    def relay(slab, quarter, part, slot, target, which=core):
        place = place_of(quarter, part, which)
        piece = wb.at[slab, rows_of(place)]
        return remote(piece, piece, w_send.at[slot], w_recv.at[slab, place], target)

    sent = []
    for quarters in ((qa, qb), (qb, qa)):
        for part in range(HALVES):
            for quarter, target in zip(quarters, (right, left)):
                copy = own(quarter, part, len(sent), target)
                copy.start()
                sent.append(copy)
    def gain_arrived(at):
        remote(gbuf.at[at], gbuf.at[at], gain_send.at[0], gain_recv.at[at], twin).wait_recv()


    @pl.when(half == 0)
    def _():
        load_x.wait()

        @pl.when(y != 0)
        def _():
            gain_arrived(0)

        normalise(0)

    rounds = [
        [(yl, qa, (right, near_x, twin)), (yr, qb, (left, near_z, twin))],
        [(yl, qb, (near_z, twin)), (yr, qa, (near_x, twin))],
        [(yl, pa, (twin,)), (yr, pb, (twin,))],
        [(yo, qa, (near_x, twin)), (yo, qb, (near_z, twin))],
        [(yr, pa, (twin,)), (yl, pb, (twin,))],
        [(yo, pa, (twin,)), (yo, pb, (twin,))],
    ]
    for group in rounds:
        for part in range(HALVES):
            for slab, quarter, targets in group:
                relay(slab, quarter, part, 0, right).wait_recv()
                for target in targets:
                    copy = relay(slab, quarter, part, len(sent), target)
                    copy.start()
                    sent.append(copy)
    for at in (yr, yo, yl):

        @pl.when((at != 0) | (half == 1))
        def _():
            gain_arrived(at)

    for slab in (yl, yr, yo):
        for quarter in range(4):
            for part in range(HALVES):
                relay(slab, quarter, part, 0, twin, 1 - core).wait_recv()

    hop_x = remote(xs.at[UNITS], xs.at[0], hop_send.at[0], hop_recv.at[0], dev(other_half, other_x))
    hop_g = remote(gs.at[0], gs.at[UNITS], hop_send.at[1], hop_recv.at[1], dev(other_half, other_x))

    @pl.when(half == 1)
    def _():
        cot_copy.wait_recv()
        early_s[...] = spread_back(UNITS - 1)
        for step in range(depth - 3):
            pass_on(step)
        hop_x.wait_recv()

    def forward(unit, _):
        normalise(unit)
        convolve(unit)
        return 0

    @pl.when(half == 0)
    def _():
        convolve(0)

    lax.fori_loop(1 - half, UNITS - half, forward, 0)

    @pl.when(half == 1)
    def _():
        normalise(UNITS - 1)
        start_home(acts.at[UNITS - 1], actb, 1, act_recv, UNITS - 1)


    def send_outputs(kept, slot, swapped, dst, recv):
        for unit in range(UNITS):

            @pl.when(half == 0)
            def _():
                start_home(kept.at[unit + 1 - slot // 3], dst, slot, recv, unit)

            @pl.when(half == 1)
            def _():
                swap(kept, swapped, slot // 3, unit).wait_recv()
                start_home(swapped.at[unit], dst, slot, recv, unit)

    def turn_acts():
        home(acts.at[y], actb, 1, act_recv, y)[2]().wait()
        arrived(actb, act_recv, (yr, yo, yl))

        def turn(clip, _):
            act = actb[clip].astype(F32)
            frames = [act[f * PLANE : (f + 1) * PLANE].T.astype(BF16) for f in range(FRAMES)]
            for frame_off in range(3):
                turned[clip, frame_off] = beside([frames[max(f - 2 + frame_off, 0)] for f in range(FRAMES)])
            return 0

        lax.fori_loop(0, UNITS, turn, 0)

    @pl.when(half == 0)
    def _():
        hop_x.start()
        turn_acts()

    @pl.when(half == 0)
    def _():
        send_outputs(xs, 0, xs2, seg_out, seg_recv)
        for step in range(depth - 3):
            pass_on(step)
        hop_g.wait_recv()

    def backward(step, _):
        unit = UNITS - 1 - step
        start_home(gs.at[unit + 1], grdb, 2, grd_recv, unit)
        through_norm(unit, spread_back(unit))
        return 0

    @pl.when(half == 1)
    def _():
        start_home(gs.at[UNITS], grdb, 2, grd_recv, UNITS - 1)
        through_norm(UNITS - 1, early_s[...])

    lax.fori_loop(half, UNITS, backward, 0)

    @pl.when(half == 1)
    def _():
        hop_g.start()
        fill_shifts(acts[UNITS - 1].astype(F32).reshape(PIX // COLS, COLS, C), shifts, 0, False)
        convolve(UNITS - 1, False)
        turn_acts()

    home(gs.at[y + 1], grdb, 2, grd_recv, y)[2]().wait()

    def spread(step, _):
        clip = lax.rem(y + step + (step // 2) * (5 - 2 * step), UNITS)

        @pl.when(step > 0)
        def _():
            arrived(grdb, grd_recv, (clip,))

        fill_shifts(grdb[clip].astype(F32).reshape(PIX // COLS, COLS, C), shifts, clip, True)
        return 0

    lax.fori_loop(0, UNITS, spread, 0)

    lhs = beside([turned[clip].reshape(3 * C, PIX) for clip in range(UNITS)])
    for first in range(0, TAPS, 2):
        taps = range(first, min(first + 2, TAPS))
        block = dot(lhs, beside([shifted(shifts, tap, True, UNITS) for tap in taps]))
        for tap in taps:
            for frame_off in range(3):
                at = (frame_off * TAPS + tap) * C
                total[at : at + C] = block[frame_off * C : (frame_off + 1) * C, (tap - first) * C :][:, :C]

    chunk = WROWS // (4 * depth)

    def core_copy(at):
        return remote(buf1.at[at, 1 - core], got1.at[at], rs_send.at[0, at], rs_recv.at[0, at], twin)

    for at_z in range(depth):
        for at_x in range(2):
            for at_core in range(2):
                start = (at_z * 4 + at_x * 2 + at_core) * chunk
                buf1[at_z, at_core, at_x] = total[start : start + chunk].astype(BF16)
        core_copy(at_z).start()
    steps = sorted(range(depth), key=lambda step: -min(step, depth - step))
    places = [lax.rem(z + step, depth) for step in steps]

    def x_copy(at):
        return remote(buf2.at[at, 1 - x_lo], got2.at[at], rs_send.at[1, at], rs_recv.at[1, at], near_x)

    def z_copy(at):
        target = dev(pipe, at * 4 + lax.rem(dp, 4))
        return remote(buf3.at[at], got3.at[z], rs_send.at[2, at], rs_recv.at[2, z], target)

    for at in places:
        core_copy(at).wait_recv()
        buf2[at] = (buf1[at, core].astype(F32) + got1[at].astype(F32)).astype(BF16)
        x_copy(at).start()

    @pl.when(half == 1)
    def _():
        send_outputs(xs, 0, xs2, seg_out, seg_recv)

    send_outputs(gs, 3, gs2, grad_out, ing_recv)
    for step, at in zip(steps, places):
        x_copy(at).wait_recv()
        buf3[at] = (buf2[at, x_lo].astype(F32) + got2[at].astype(F32)).astype(BF16)
        if step:
            z_copy(at).start()
    result = buf3[z].astype(F32)
    for step in reversed(steps):
        if step:
            at = lax.rem(z + step, depth)
            remote(got3.at[at], got3.at[at], rs_send.at[2, at], rs_recv.at[2, at], twin).wait_recv()
            result = result + got3[at].astype(F32)
    wg_out[...] = result * scale

    for step, at in zip(steps, places):
        core_copy(at).wait_send()
        x_copy(at).wait_send()
        if step:
            z_copy(at).wait_send()
    for copy in sent:
        copy.wait_send()
    for slot, at in enumerate((yr, yo, yl)):
        gain_copy(at, slot).wait_send()
    for unit in range(UNITS):
        finish_home(xs2.at[unit], seg_out, 0, seg_recv, unit)
        finish_home(gs2.at[unit], grad_out, 3, ing_recv, unit)

        @pl.when(unit != y)
        def _():
            home(acts.at[unit], actb, 1, act_recv, unit)[1]().wait_send()
            home(gs.at[unit + 1], grdb, 2, grd_recv, unit)[1]().wait_send()

    @pl.when(half == 0)
    def _():
        hop_x.wait_send()

    @pl.when(half == 1)
    def _():
        cot_copy.wait_send()
        hop_g.wait_send()
        for unit in range(UNITS):
            swap(xs, xs2, 0, unit).wait_send()
            swap(gs, gs2, 1, unit).wait_send()

    arrived(seg_out, seg_recv, (yr, yo, yl))
    arrived(grad_out, ing_recv, (yr, yo, yl))


def write_results(seg, grad, share, seg_out, grad_out, share_out, flat, sem):
    copies = [
        pltpu.make_async_copy(seg, seg_out, sem.at[0]),
        pltpu.make_async_copy(grad, grad_out, sem.at[1]),
        pltpu.make_async_copy(flat, share_out, sem.at[2]),
    ]
    copies[0].start()
    copies[1].start()
    for row in range(share.shape[0]):
        flat[:, row * C : (row + 1) * C] = share[row : row + 1]
    copies[2].start()
    for copy in copies:
        copy.wait()


def body(video, cotangent, weights, gains):
    micro = video.shape[0]
    devices = lax.axis_size("dp")
    depth = devices // 4
    chunk = WROWS // devices
    scale = 1.0 / math.sqrt(micro * devices * PIX)
    clip = (PIX, C)
    any_spec = pl.BlockSpec(memory_space=pl.ANY)
    dma = pltpu.SemaphoreType.DMA
    outputs, grads_out, share = pl.pallas_call(
        functools.partial(kernel, depth, scale),
        out_shape=(
            jax.ShapeDtypeStruct((micro, *clip), BF16),
            jax.ShapeDtypeStruct((micro, *clip), BF16),
            jax.ShapeDtypeStruct((chunk, C), F32),
        ),
        in_specs=[pl.BlockSpec(memory_space=pltpu.HBM)] * 4,
        out_specs=(any_spec, any_spec, pl.BlockSpec(memory_space=pltpu.VMEM)),
        scratch_shapes=[
            pltpu.VMEM((UNITS, WROWS, C), BF16),
            pltpu.VMEM((UNITS, 1, C), F32),
            pltpu.VMEM((UNITS + 1, *clip), BF16),
            pltpu.VMEM((UNITS + 1, *clip), BF16),
            pltpu.VMEM((UNITS, *clip), BF16),
            pltpu.VMEM((UNITS, *clip), BF16),
            pltpu.VMEM((UNITS, *clip), BF16),
            pltpu.VMEM((UNITS, PIX // COLS, COLS, C), F32),
            pltpu.VMEM((UNITS, PIX // COLS, COLS, C), F32),
            pltpu.VMEM((UNITS, 1, C), F32),
            pltpu.VMEM(clip, F32),
            pltpu.VMEM((3, UNITS, FRAMES, ROWS + 2, COLS, C), BF16),
            pltpu.VMEM((UNITS, *clip), BF16),
            pltpu.VMEM((UNITS, *clip), BF16),
            pltpu.VMEM((UNITS, 3, C, PIX), BF16),
            pltpu.VMEM((WROWS, C), F32),
            pltpu.VMEM((depth, 2, 2, chunk, C), BF16),
            pltpu.VMEM((depth, 2, chunk, C), BF16),
            pltpu.VMEM((depth, 2, chunk, C), BF16),
            pltpu.VMEM((depth, chunk, C), BF16),
            pltpu.VMEM((depth, chunk, C), BF16),
            pltpu.VMEM((depth, chunk, C), BF16),
            dma((3,)),
            dma((24 * HALVES,)),
            dma((UNITS, 8 * HALVES)),
            dma((3,)),
            dma((UNITS,)),
            dma((3,)),
            dma((3,)),
            dma((4, UNITS)),
            dma((UNITS,)),
            dma((UNITS,)),
            dma((UNITS,)),
            dma((UNITS,)),
            pltpu.SemaphoreType.REGULAR((depth - 3,)),
            dma((2, UNITS)),
            dma((2, UNITS)),
            dma((3, depth)),
            dma((3, depth)),
        ],
        compiler_params=pltpu.CompilerParams(collective_id=0, has_side_effects=True, vmem_limit_bytes=32 << 20),
    )(
        *(
            pltpu.with_memory_space_constraint(array, pltpu.HBM)
            for array in (
                video.reshape(micro, *clip),
                cotangent.reshape(micro, *clip),
                weights.reshape(WROWS, C),
                gains,
            )
        )
    )
    whole = pl.BlockSpec(memory_space=pltpu.VMEM)
    outputs, grads_out, share = pl.pallas_call(
        write_results,
        out_shape=(
            jax.ShapeDtypeStruct((micro, *clip), BF16),
            jax.ShapeDtypeStruct((micro, *clip), BF16),
            jax.ShapeDtypeStruct((1, chunk * C), F32),
        ),
        in_specs=[any_spec, any_spec, whole],
        out_specs=(pl.BlockSpec(memory_space=pltpu.HBM),) * 3,
        scratch_shapes=[pltpu.VMEM((1, chunk * C), F32), dma((3,))],
        compiler_params=pltpu.CompilerParams(vmem_limit_bytes=4 << 20),
    )(outputs, grads_out, share)
    full = (1, micro, 1, FRAMES, ROWS, COLS, C)
    return (outputs.reshape(full), grads_out.reshape(full), share)


def solution(mesh):
    in_specs = (
        P(None, "dp", None, None, None, None),
        P(None, "dp", None, None, None, None),
        P("pipe", None, None),
        P("pipe", None),
    )
    out_specs = (
        P("pipe", None, "dp", None, None, None, None),
        P("pipe", None, "dp", None, None, None, None),
        P("pipe", "dp"),
    )
    return jax.shard_map(body, mesh=mesh, in_specs=in_specs, out_specs=out_specs, check_vma=False)
```
